512 devices in a mesh: section: 8 (over z), slab: 64 (over x, y, core).
Axes of the slice: x: 4, y: 8, z: 8, core: 2. Of those that a mesh axis runs over, the one named last changes fastest.
Arguments:
- fields: bfloat16 [8, 4, 128, 128, 128], P('section', None, 'slab'), may hold values from -6 to 6
- lift_weight: bfloat16 [4, 32], replicated, may hold values from -3 to 3
- lift_bias: bfloat16 [32], replicated, may hold values from -3 to 3
- spectral_weight: bfloat16 [2, 2, 32, 32, 16384], P(None, None, None, 'section', 'slab'), may hold values from -0.75 to 0.75
- bypass_weight: bfloat16 [2, 32, 32], replicated, may hold values from -1 to 1
- bypass_bias: bfloat16 [2, 32], replicated, may hold values from -3 to 3
Outputs:
- features: bfloat16 [8, 32, 128, 128, 128], P('section', None, 'slab')
The draws below stay inside these ranges and needn't reach their ends.
All inputs are finite; a program needn't handle non-finite values.
Results may differ from the reference program's by a relative error of at most 0.015.
Values may be sent and summed in bfloat16 or wider, within the bound.
No kernel may reach another device: no remote copies, remote signals or barrier semaphores. Data moves between devices by JAX's collectives and lax.ppermute only.
A program may use at most 64 MiB of HBM per device.

```python
import math
import jax
import jax.numpy as jnp
from jax import lax

C = 32
K = 16
CIN = 4
NX = 128
NY = 128
LAYERS = 2
M = 8
NZ = 128


def block_levels(stream_key, shape, pieces, smallest, high):
    loudness, own = 1.0, jax.random.fold_in(stream_key, 6)
    for position, blocks in pieces:
        heights = jnp.exp(jax.random.uniform(jax.random.fold_in(own, position), (blocks,), jnp.float32, smallest / len(pieces), high / len(pieces)))
        loudness = loudness * jnp.repeat(heights, shape[position] // blocks).reshape([-1 if axis == position else 1 for axis in range(len(shape))])
    return loudness


def normal_values(rng, shape, scale, bound, shards=(), held_as=jnp.bfloat16):
    level = block_levels(rng, shape, shards, -0.22, 0.18) if shards else 1.0
    result = jax.random.normal(rng, shape, jnp.float32) * scale * level
    return jnp.minimum(jnp.maximum(result, -bound), bound).astype(held_as)


def setup_inputs(seed: int = 0) -> dict:
    arg_keys = jax.random.split(jax.random.key(seed), 7)
    fields = normal_values(arg_keys[0], (M, CIN, NZ, NX, NY), 1.0, 6.0, ((0, 8), (2, 64)))
    lift_weight = normal_values(arg_keys[1], (CIN, C), CIN ** -0.5, 3.0)
    lift_bias = normal_values(arg_keys[2], (C,), 0.5, 3.0)
    spectral_weight = normal_values(arg_keys[3], (LAYERS, 2, C, C, 4 * K * K * K), (2 * C) ** -0.5, 0.75, ((3, 8), (4, 64)))
    bypass_weight = normal_values(arg_keys[4], (LAYERS, C, C), C ** -0.5, 1.0)
    bypass_bias = normal_values(arg_keys[5], (LAYERS, C), 0.5, 3.0)
    return dict(fields=fields, lift_weight=lift_weight, lift_bias=lift_bias, spectral_weight=spectral_weight, bypass_weight=bypass_weight, bypass_bias=bypass_bias)


def signed_list(count):
    base = jnp.arange(2 * count, dtype=jnp.int32)
    return jnp.where(base < count, base, base - 2 * count)

def tables(freqs, length, first, span):
    freq = (freqs % length)[:, None]
    where = first + jnp.arange(span, dtype=jnp.int32)[None, :]
    phase = (freq * where % length).astype(jnp.float32) * (2.0 * math.pi / length)
    return (jnp.cos(phase).astype(jnp.bfloat16), jnp.sin(phase).astype(jnp.bfloat16))

def forward_pair(freqs, length):
    cosine, sine = tables(freqs, length, 0, length)
    return jnp.concatenate([cosine, -sine], axis=0).T

def product(form, left, right):
    return jnp.einsum(form, left.astype(jnp.float32), right.astype(jnp.float32), precision=lax.Precision.HIGHEST)

def one_variant(fields, lift_weight, lift_bias, spectral_weight, bypass_weight, bypass_bias):
    half = 2 * K
    modes_xy = half * half
    hidden = (product('czxy,cd->dzxy', fields, lift_weight) + lift_bias.astype(jnp.float32)[:, None, None, None]).astype(jnp.bfloat16)
    xy_list = signed_list(K)
    z_list = jnp.arange(K, dtype=jnp.int32)
    table_y = forward_pair(xy_list, NY)
    table_x = forward_pair(xy_list, NX)
    table_z = forward_pair(z_list, NZ)
    doubling = jnp.where(z_list == 0, 1.0, 2.0).astype(jnp.bfloat16)[:, None]
    cos_z, sin_z = tables(z_list, NZ, 0, NZ)
    cos_z = cos_z * doubling
    sin_z = sin_z * doubling
    cos_x, sin_x = tables(xy_list, NX, 0, NX)
    cos_y, sin_y = tables(xy_list, NY, 0, NY)
    back_y = jnp.concatenate([cos_y, -sin_y], axis=0)
    keep = (jnp.arange(modes_xy * K, dtype=jnp.int32) != 0).astype(jnp.float32).reshape(modes_xy, K)
    for layer in range(LAYERS):
        along_y = (product('czxy,yq->czxq', hidden, table_y) / math.sqrt(NY)).astype(jnp.bfloat16)
        both = product('czxq,xp->czpq', along_y, table_x)
        spec_real = both[:, :, :half, :half] - both[:, :, half:, half:]
        spec_imag = both[:, :, :half, half:] + both[:, :, half:, :half]
        spectrum = (jnp.stack([spec_real, spec_imag], 1) / math.sqrt(NX)).astype(jnp.bfloat16)
        spectrum = spectrum.reshape(C, 2, NZ, modes_xy)
        along_z = product('crzj,zq->crjq', spectrum, table_z)
        mode_real = (along_z[:, 0, :, :K] - along_z[:, 1, :, K:]) / math.sqrt(NZ) * keep
        mode_imag = (along_z[:, 1, :, :K] + along_z[:, 0, :, K:]) / math.sqrt(NZ) * keep
        weights = spectral_weight[layer].astype(jnp.float32).reshape(2, C, C, modes_xy, K)
        mixed_real = product('ijk,iojk->ojk', mode_real, weights[0]) - product('ijk,iojk->ojk', mode_imag, weights[1])
        mixed_imag = product('ijk,iojk->ojk', mode_imag, weights[0]) + product('ijk,iojk->ojk', mode_real, weights[1])
        mixed = jnp.stack([mixed_real, mixed_imag], 1).astype(jnp.bfloat16)
        plain = product('crjk,kz->crjz', mixed, cos_z)
        skewed = product('crjk,kz->crjz', mixed, sin_z)
        planes_back = (jnp.stack([plain[:, 0] - skewed[:, 1], skewed[:, 0] + plain[:, 1]], 1) * 0.25).astype(jnp.bfloat16)
        grid = planes_back.reshape(C, 2, half, half, NZ)
        plain = product('crpqz,px->czxrq', grid, cos_x)
        skewed = product('crpqz,px->czxrq', grid, sin_x)
        along_x = (jnp.concatenate([plain[:, :, :, 0] - skewed[:, :, :, 1], skewed[:, :, :, 0] + plain[:, :, :, 1]], -1) * 0.125).astype(jnp.bfloat16)
        spectral_field = product('czxq,qy->czxy', along_x, back_y) * 0.125
        bypassed = product('czxy,co->ozxy', hidden, bypass_weight[layer]) + bypass_bias[layer].astype(jnp.float32)[:, None, None, None]
        hidden = jax.nn.gelu(bypassed + spectral_field, approximate=True).astype(jnp.bfloat16)
    return hidden

def reference(fields, lift_weight, lift_bias, spectral_weight, bypass_weight, bypass_bias):

    def single(variant):
        return one_variant(variant, lift_weight, lift_bias, spectral_weight, bypass_weight, bypass_bias)
    return lax.map(single, fields)
```

```python
import math

import jax
import jax.numpy as jnp
import ml_dtypes
import numpy as np
from jax import lax
from jax.experimental import pallas as pl
from jax.experimental.pallas import tpu as pltpu
from jax.sharding import PartitionSpec as P

K = 16
HALF = 2 * K
LENGTH = 128
SLABS = 64
BF = jnp.bfloat16
F32 = jnp.float32


def wave(freqs):
    where = np.arange(LENGTH, dtype=np.int64)[None, :]
    step = (freqs % LENGTH)[:, None] * where % LENGTH
    phase = step.astype(np.float32) * np.float32(2.0 * math.pi / LENGTH)
    cosine = np.cos(phase).astype(ml_dtypes.bfloat16).astype(np.float32)
    sine = np.sin(phase).astype(ml_dtypes.bfloat16).astype(np.float32)
    return cosine, sine


def make_tables():
    base = np.arange(HALF)
    signed = np.where(base < K, base, base - HALF)
    cos, sin = wave(signed)
    cos_z, sin_z = wave(np.arange(K))
    double = np.where(np.arange(K) == 0, 1.0, 2.0)[:, None]
    table = {}
    pair = np.stack([cos, -sin], 0).reshape(2, 2, K, LENGTH)
    for name, many in (("fwd_y8", 8), ("fwd_y4", 4)):
        block = np.einsum("cd,rhpy->cyrhdp", np.eye(many), pair)
        table[name] = block.reshape(many * LENGTH, 4 * many * K)
    table["fwd_x"] = np.concatenate(
        [np.concatenate([cos, sin], 1), np.concatenate([-sin, cos], 1)], 0
    )
    fwd_z = np.stack([np.stack([cos_z, sin_z], 1), np.stack([-sin_z, cos_z], 1)], 0)
    fwd_z = fwd_z.reshape(2, K, 2, SLABS, 2)
    full = np.einsum("gf,akrsz->gaksfrz", np.eye(4), fwd_z)
    table["fwd_z"] = full.reshape(4 * HALF, SLABS * 16)
    table["fwd_z0"] = np.einsum("akrsz->zaksr", fwd_z).reshape(2 * HALF, SLABS * 2)
    cz, sz = cos_z * double * 0.25, sin_z * double * 0.25
    inv_z = np.stack([np.stack([cz, -sz], 0), np.stack([sz, cz], 0)], 0)
    inv_z = inv_z.reshape(2, 2, K, SLABS, 2)
    table["inv_z"] = np.einsum("gf,arksz->sgazfrk", np.eye(4), inv_z).reshape(SLABS * 16, 4 * HALF)
    inv_x = np.stack([np.stack([cos, -sin], 0), np.stack([sin, cos], 0)], 0)
    table["inv_x"] = np.einsum("arpx->axrp", inv_x).reshape(2 * LENGTH, 2 * HALF) * 0.125
    table["inv_y"] = (
        np.einsum("cd,rhpy->rhcpdy", np.eye(8), pair).reshape(512, 8 * LENGTH) * 0.125
    )
    one_x = (cos.sum(1) - 1j * sin.sum(1)) / math.sqrt(LENGTH)
    one_z = (cos_z.sum(1) - 1j * sin_z.sum(1)) / math.sqrt(LENGTH)
    return table, one_x, one_z


def split(value):
    return np.stack([value.real, value.imag], 0).astype(np.float32)


def dot(left, right):
    return jnp.dot(left, right, preferred_element_type=F32)


def nt_dot(left, right):
    return lax.dot_general(left, right, (((1,), (1,)), ((), ())), preferred_element_type=F32)


def spread_kernel(bypass_ref, lift_ref, bypass_bias_ref, lift_bias_ref, kb_ref, kl_ref, bias_ref):
    def picks(rows, cols):
        row = lax.broadcasted_iota(jnp.int32, (rows, cols), 0)
        col = lax.broadcasted_iota(jnp.int32, (rows, cols), 1)
        return row, col

    row, col = picks(512, 32)
    expand = jnp.where(row // 16 == col, 1.0, 0.0).astype(BF)
    row, col = picks(512, 512)
    same = (row % 16) == (col % 16)
    for layer in range(2):
        tall = lax.dot_general(
            expand, bypass_ref[layer], (((1,), (1,)), ((), ())), preferred_element_type=F32
        ).astype(BF)
        wide = nt_dot(tall, expand)
        kb_ref[layer] = jnp.where(same, wide, 0.0).astype(BF)
    row, col = picks(64, 4)
    expand4 = jnp.where(row // 16 == col, 1.0, 0.0).astype(BF)
    tall = lax.dot_general(
        expand, lift_ref[...], (((1,), (1,)), ((), ())), preferred_element_type=F32
    ).astype(BF)
    row, col = picks(512, 64)
    kl_ref[...] = jnp.where((row % 16) == (col % 16), nt_dot(tall, expand4), 0.0).astype(BF)
    ones = jnp.ones((32, LENGTH), BF)
    expand = expand.astype(F32)
    for index in range(3):
        vector = bypass_bias_ref[index : index + 1] if index < 2 else lift_bias_ref[...]
        bias_ref[index] = dot((expand * vector.astype(F32)).astype(BF), ones)


def start_kernel(fields_ref, fwd_y_ref, fwd_x_ref, out_ref, rows):
    lane = lax.broadcasted_iota(jnp.int32, (64, LENGTH), 1)
    made = []
    for z in range(2):
        wide = jnp.concatenate([fields_ref[0, c, z] for c in range(4)], axis=1)
        along = dot(wide, fwd_y_ref[...]).astype(BF)
        stacked = jnp.concatenate([along[:, :128], along[:, 128:]], axis=0)
        made.append(dot(fwd_x_ref[...], stacked) * (1.0 / LENGTH))
    first = jnp.where(lane < 64, made[0], pltpu.roll(made[1], 64, 1))
    second = jnp.where(lane < 64, pltpu.roll(made[0], 64, 1), made[1])
    for h, value in enumerate((first, second)):
        for r in range(2):
            rows[pl.ds(h * 2 + r, 32, stride=4), :] = value[r * 32 : r * 32 + 32]
    out_ref[...] = rows[...].astype(BF)


def mix(weight_ref, modes, pattern, turned, inv_z_ref, out_ref):
    low = lax.broadcasted_iota(jnp.int32, (8, LENGTH), 0) < 4
    for pair in range(16):
        for r in range(2):
            for half in range(2):
                even = jnp.broadcast_to(modes[r, half, 2 * pair : 2 * pair + 1, :], (8, LENGTH))
                odd = jnp.broadcast_to(modes[r, half, 2 * pair + 1 : 2 * pair + 2, :], (8, LENGTH))
                pattern[pair, r, half] = jnp.where(low, even, odd)
    slot = lax.broadcasted_iota(jnp.int32, (8, LENGTH), 1) // K
    mixed = {}
    for g in range(4):
        total = {}
        for side in range(2):
            section = 2 * g + side
            acc = [[jnp.zeros((8, LENGTH), F32) for _ in range(2)] for _ in range(2)]
            for quad in range(8):
                real = weight_ref[section, 0, quad * 16 : quad * 16 + 16, :].astype(F32)
                imag = weight_ref[section, 1, quad * 16 : quad * 16 + 16, :].astype(F32)
                for sub in range(2):
                    pair = quad * 2 + sub
                    for half in range(2):
                        wr = real[sub * 8 : sub * 8 + 8, half * 128 : half * 128 + 128]
                        wi = imag[sub * 8 : sub * 8 + 8, half * 128 : half * 128 + 128]
                        mr, mi = pattern[pair, 0, half], pattern[pair, 1, half]
                        acc[0][half] = acc[0][half] + wr * mr - wi * mi
                        acc[1][half] = acc[1][half] + wr * mi + wi * mr
            for r in range(2):
                for half in range(2):
                    value = acc[r][half]
                    total[side, r, half] = value + pltpu.roll(value, 4, 0)
        for r in range(2):
            for half in range(2):
                mixed[g, r, half] = jnp.where(low, total[0, r, half], total[1, r, half])
    for py in range(K):
        half, at = py // 8, py % 8
        value = None
        for g in range(4):
            for r in range(2):
                where = 2 * g + r
                moved = mixed[g, r, half]
                if where != at:
                    moved = pltpu.roll(moved, (where - at) * K % LENGTH, 1)
                value = moved if value is None else jnp.where(slot == where, moved, value)
        turned[pl.ds(py, 8, stride=K), :] = value
    out_ref[...] = nt_dot(inv_z_ref[...], turned[...].astype(BF)).astype(BF)


def unravel(turned, groups, modes):
    slot = lax.broadcasted_iota(jnp.int32, (8, LENGTH), 1) // K
    parts = [turned[pl.ds(py, 8, stride=K), :] for py in range(K)]
    for g in range(groups):
        for r in range(2):
            source = 2 * g + r
            for half in range(2):
                value = None
                for at in range(8):
                    moved = parts[half * 8 + at]
                    if at != source:
                        moved = pltpu.roll(moved, (at - source) * K % LENGTH, 1)
                    value = moved if value is None else jnp.where(slot == at, moved, value)
                modes[r, half, g * 8 : g * 8 + 8, :] = value


def dropped(place_ref, shape):
    row = lax.broadcasted_iota(jnp.int32, shape, 0)
    lane = lax.broadcasted_iota(jnp.int32, shape, 1)
    origin = jnp.logical_and(row % K == 0, lane % K == 0)
    return jnp.logical_and(origin, place_ref[0] == 0)


def first_mix_kernel(
    place_ref, one_x_ref, got_ref, weight_ref, lift_ref, one_y_ref, one_z_ref, fwd_z_ref,
    inv_z_ref, out_ref, turned, small, modes, pattern,
):
    both = dot(fwd_z_ref[...], got_ref[...])
    lane = lax.broadcasted_iota(jnp.int32, (HALF, LENGTH), 1)
    value = both[:HALF] + pltpu.roll(both[HALF:], 64, 1)
    value = jnp.where(lane < 64, value, 0.0) * (1.0 / math.sqrt(LENGTH))
    place = place_ref[0]
    xr, xi = one_x_ref[0, place // 2], one_x_ref[1, place // 2]
    yr = jnp.where(place % 2 == 0, one_y_ref[0, 0:1, :], one_y_ref[1, 0:1, :])
    yi = jnp.where(place % 2 == 0, one_y_ref[0, 1:2, :], one_y_ref[1, 1:2, :])
    pr, pi = xr * yr - xi * yi, xr * yi + xi * yr
    zr, zi = one_z_ref[0], one_z_ref[1]
    ones = jnp.concatenate([zr * pr - zi * pi, zr * pi + zi * pr], axis=0)
    value = jnp.where(lane // K == 4, ones, value)
    value = jnp.where(dropped(place_ref, value.shape), 0.0, value)
    value = jnp.concatenate([value, jnp.zeros((LENGTH - HALF, LENGTH), F32)], axis=0)
    turned[...] = value.T
    unravel(turned, 1, small)
    for r in range(2):
        for half in range(2):
            total = jnp.zeros((32, LENGTH), F32)
            for c in range(5):
                total = total + lift_ref[:, c : c + 1] * small[r, half, c : c + 1, :]
            modes[r, half] = total
    mix(weight_ref, modes, pattern, turned, inv_z_ref, out_ref)


def mix_kernel(place_ref, got_ref, weight_ref, fwd_z_ref, inv_z_ref, out_ref, turned, modes, pattern):
    value = dot(fwd_z_ref[...], got_ref[...]) * (1.0 / math.sqrt(LENGTH))
    value = jnp.where(dropped(place_ref, value.shape), 0.0, value)
    turned[...] = value.T
    unravel(turned, 4, modes)
    mix(weight_ref, modes, pattern, turned, inv_z_ref, out_ref)


def inverse(got_ref, inv_x_ref, inv_y_ref, rows, field):
    rows[...] = got_ref[...].astype(F32)
    for g in range(4):
        for z in range(2):
            parts = []
            for h in range(2):
                pieces = [
                    rows[pl.ds(h * 16 + g * 4 + r * 2 + z, 32, stride=32), :] for r in range(2)
                ]
                parts.append(jnp.concatenate(pieces, axis=0).astype(BF))
            along = dot(inv_x_ref[...], jnp.concatenate(parts, axis=1)).astype(BF)
            wide = jnp.concatenate([along[:128], along[128:]], axis=1)
            made = dot(wide, inv_y_ref[...])
            for o in range(8):
                field[g * 8 + o, z] = made[:, o * 128 : o * 128 + 128]


def activate(value):
    inner = value * (0.7978845608028654 + 0.035677408136300125 * value * value)
    half = 0.5 * value
    return half + half * jnp.tanh(inner)


def pointwise(block, hidden, kb_ref, bias, field):
    bypassed = dot(kb_ref[...], hidden)
    made = []
    for z in range(2):
        part = field[:, z, block * 16 : block * 16 + 16, :].reshape(512, LENGTH)
        value = bypassed[:, z * 128 : z * 128 + 128] + bias + part
        made.append(activate(value).astype(BF))
    return made


def middle_kernel(
    got_ref, fields_ref, kl_ref, kb_ref, bias_ref, inv_x_ref, inv_y_ref, fwd_y_ref, fwd_x_ref,
    hidden_ref, out_ref, rows, field,
):
    inverse(got_ref, inv_x_ref, inv_y_ref, rows, field)
    lift_bias = bias_ref[2]
    lift_bias = jnp.concatenate([lift_bias, lift_bias], axis=1)
    for block in range(8):
        span = slice(block * 16, block * 16 + 16)
        raw = [fields_ref[0, :, z, span, :].reshape(64, LENGTH) for z in range(2)]
        hidden = (dot(kl_ref[...], jnp.concatenate(raw, axis=1)) + lift_bias).astype(BF)
        made = pointwise(block, hidden, kb_ref.at[0], bias_ref[0], field)
        for z in range(2):
            hidden_ref[:, z, span, :] = made[z].reshape(32, 16, LENGTH)
    for g in range(4):
        for z in range(2):
            wide = jnp.concatenate([hidden_ref[g * 8 + c, z] for c in range(8)], axis=1)
            along = dot(wide, fwd_y_ref[...]).astype(BF)
            stacked = jnp.concatenate([along[:, :256], along[:, 256:]], axis=0)
            spectrum = dot(fwd_x_ref[...], stacked) * (1.0 / LENGTH)
            for h in range(2):
                for r in range(2):
                    at = h * 16 + g * 4 + r * 2 + z
                    rows[pl.ds(at, 32, stride=32), :] = spectrum[
                        r * 32 : r * 32 + 32, h * 128 : h * 128 + 128
                    ]
    out_ref[...] = rows[...].astype(BF)


def last_kernel(
    got_ref, hidden_ref, kb_ref, bias_ref, inv_x_ref, inv_y_ref, out_ref, rows, field
):
    inverse(got_ref, inv_x_ref, inv_y_ref, rows, field)
    for block in range(8):
        span = slice(block * 16, block * 16 + 16)
        raw = [hidden_ref[:, z, span, :].reshape(512, LENGTH) for z in range(2)]
        made = pointwise(block, jnp.concatenate(raw, axis=1), kb_ref.at[1], bias_ref[1], field)
        for z in range(2):
            out_ref[0, :, z, span, :] = made[z].reshape(32, 16, LENGTH)


def vmem(count):
    return [pl.BlockSpec(memory_space=pltpu.VMEM)] * count


def call(kernel, name, inputs, outputs, scratch, scalars=0):
    return pl.pallas_call(
        kernel,
        name=name,
        out_shape=outputs,
        in_specs=[pl.BlockSpec(memory_space=pltpu.SMEM)] * scalars + vmem(inputs),
        out_specs=vmem(len(outputs)),
        scratch_shapes=[pltpu.VMEM(shape, F32) for shape in scratch],
        compiler_params=pltpu.CompilerParams(vmem_limit_bytes=40 << 20),
    )


def exchange(value):
    return lax.all_to_all(value, "slab", split_axis=0, concat_axis=0, tiled=True)


def solution(mesh):
    table, one_x, one_z = make_tables()
    const = {name: value.astype(ml_dtypes.bfloat16) for name, value in table.items()}
    ones_x = split(one_x)
    ones_y = np.tile(split(one_x).reshape(2, 2, 1, K), (1, 1, 8, 1)).reshape(2, 2, LENGTH)
    ones_y = ones_y.transpose(1, 0, 2)
    ones_z = np.repeat(split(one_z)[:, :, None], LENGTH, axis=2)

    def on_device(fields, lift_weight, lift_bias, spectral_weight, bypass_weight, bypass_bias):
        place = lax.axis_index("slab").reshape(1)
        gathered = []
        for layer in range(2):
            local = spectral_weight[layer].reshape(2, LENGTH, 256)
            gathered.append(lax.all_gather(local, "section", axis=0))
        lifting = jnp.concatenate([lift_weight, lift_bias[None]], axis=0).T.astype(F32)
        (spectrum,) = call(
            start_kernel, "start", 3, [jax.ShapeDtypeStruct((128, 128), BF)], [(128, 128)]
        )(fields, const["fwd_y4"], const["fwd_x"])
        kb, kl, bias = call(
            spread_kernel,
            "spread",
            4,
            [
                jax.ShapeDtypeStruct((2, 512, 512), BF),
                jax.ShapeDtypeStruct((512, 64), BF),
                jax.ShapeDtypeStruct((3, 512, LENGTH), F32),
            ],
            [],
        )(bypass_weight, lift_weight, bypass_bias, lift_bias[None])
        packed = jax.ShapeDtypeStruct((1024, LENGTH), BF)
        square, modes, pattern = (128, 128), (2, 2, 32, 128), (16, 2, 2, 8, 128)
        (planes,) = call(
            first_mix_kernel,
            "mix0",
            7,
            [packed],
            [square, (2, 2, 8, 128), modes, pattern],
            scalars=2,
        )(
            place, ones_x, exchange(spectrum), gathered[0], lifting, ones_y, ones_z,
            const["fwd_z0"], const["inv_z"],
        )
        hidden, spectrum = call(
            middle_kernel,
            "middle",
            9,
            [jax.ShapeDtypeStruct((32, 2, 128, 128), BF), packed],
            [(1024, 128), (32, 2, 128, 128)],
        )(
            exchange(planes), fields, kl, kb, bias, const["inv_x"], const["inv_y"],
            const["fwd_y8"], const["fwd_x"],
        )
        (planes,) = call(
            mix_kernel, "mix1", 4, [packed], [square, modes, pattern], scalars=1
        )(place, exchange(spectrum), gathered[1], const["fwd_z"], const["inv_z"])
        (features,) = call(
            last_kernel,
            "last",
            6,
            [jax.ShapeDtypeStruct((1, 32, 2, 128, 128), BF)],
            [(1024, 128), (32, 2, 128, 128)],
        )(exchange(planes), hidden, kb, bias, const["inv_x"], const["inv_y"])
        return features

    placed = (
        P("section", None, "slab", None, None),
        P(),
        P(),
        P(None, None, None, "section", "slab"),
        P(),
        P(),
    )
    return jax.shard_map(
        on_device,
        mesh=mesh,
        in_specs=placed,
        out_specs=P("section", None, "slab", None, None),
        check_vma=False,
    )
```

```python
import math

import jax
import jax.numpy as jnp
import ml_dtypes
import numpy as np
from jax import lax
from jax.experimental import pallas as pl
from jax.experimental.pallas import tpu as pltpu
from jax.sharding import PartitionSpec as P

K = 16
HALF = 2 * K
LENGTH = 128
SLABS = 64
BF = jnp.bfloat16
F32 = jnp.float32


def wave(freqs):
    where = np.arange(LENGTH, dtype=np.int64)[None, :]
    step = (freqs % LENGTH)[:, None] * where % LENGTH
    phase = step.astype(np.float32) * np.float32(2.0 * math.pi / LENGTH)
    cosine = np.cos(phase).astype(ml_dtypes.bfloat16).astype(np.float32)
    sine = np.sin(phase).astype(ml_dtypes.bfloat16).astype(np.float32)
    return cosine, sine


def make_tables():
    base = np.arange(HALF)
    signed = np.where(base < K, base, base - HALF)
    cos, sin = wave(signed)
    cos_z, sin_z = wave(np.arange(K))
    double = np.where(np.arange(K) == 0, 1.0, 2.0)[:, None]
    table = {}
    table["pair_y"] = np.concatenate([cos, -sin], 0)
    table["fwd_x"] = np.concatenate(
        [np.concatenate([cos, sin], 1), np.concatenate([-sin, cos], 1)], 0
    )
    fwd_z = np.stack([np.stack([cos_z, sin_z], 1), np.stack([-sin_z, cos_z], 1)], 0)
    fwd_z = fwd_z.reshape(2, K, 2, SLABS, 2)
    full = np.einsum("gf,akrsz->gaksfrz", np.eye(4), fwd_z)
    full = full.reshape(4 * HALF, 8, LENGTH).transpose(1, 0, 2).reshape(1024, LENGTH)
    first = np.einsum("akrsz->zaksr", fwd_z).reshape(2 * HALF, SLABS * 2)
    cz, sz = cos_z * double * 0.25, sin_z * double * 0.25
    inv_z = np.stack([np.stack([cz, -sz], 0), np.stack([sz, cz], 0)], 0)
    inv_z = inv_z.reshape(2, 2, K, SLABS, 2)
    back = np.einsum("gf,arksz->sgazfrk", np.eye(4), inv_z).reshape(SLABS * 16, 4 * HALF)
    table["z"] = np.concatenate([back, full, first], 0)
    inv_x = np.stack([np.stack([cos, -sin], 0), np.stack([sin, cos], 0)], 0)
    table["inv_x"] = np.einsum("arpx->axrp", inv_x).reshape(2 * LENGTH, 2 * HALF) * 0.125
    table["x"] = np.concatenate([table["fwd_x"], np.pad(table.pop("inv_x"), ((0, 0), (0, 192)))], 0)
    one_x = (cos.sum(1) - 1j * sin.sum(1)) / math.sqrt(LENGTH)
    one_z = (cos_z.sum(1) - 1j * sin_z.sum(1)) / math.sqrt(LENGTH)
    return table, one_x, one_z


def split(value):
    return np.stack([value.real, value.imag], 0).astype(np.float32)


def dot(left, right):
    return jnp.dot(left, right, preferred_element_type=F32)


def nt_dot(left, right):
    return lax.dot_general(left, right, (((1,), (1,)), ((), ())), preferred_element_type=F32)


def picks(rows, cols):
    row = lax.broadcasted_iota(jnp.int32, (rows, cols), 0)
    col = lax.broadcasted_iota(jnp.int32, (rows, cols), 1)
    return row, col


def one_hot(mask):
    return jnp.where(mask, 1.0, 0.0).astype(BF)


def fetch(copies):
    started = [pltpu.make_async_copy(source, target, sem) for source, target, sem in copies]
    for copy in started:
        copy.start()
    return started


def spread_kernel(
    place_ref, one_x_ref, bypass_ref, lift_ref, bypass_bias_ref, lift_bias_ref, pair_y_ref,
    one_y_ref, one_z_ref, z_ref, x_ref, kb_ref, kl_ref, bias_ref, fwd_y_ref, inv_y_ref, ones_ref,
    z_out, x_out,
):
    z_out[...] = z_ref[...]
    x_out[...] = x_ref[...]
    row, col = picks(512, 32)
    expand = one_hot(row // 16 == col)
    row, col = picks(512, 512)
    same = (row % 16) == (col % 16)
    for layer in range(2):
        tall = nt_dot(expand, bypass_ref[layer]).astype(BF)
        kb_ref[layer] = jnp.where(same, nt_dot(tall, expand), 0.0).astype(BF)
    row, col = picks(64, 4)
    expand4 = one_hot(row // 16 == col)
    tall = nt_dot(expand, lift_ref[...]).astype(BF)
    row, col = picks(512, 64)
    kl_ref[:, :64] = jnp.where((row % 16) == (col % 16), nt_dot(tall, expand4), 0.0).astype(BF)
    kl_ref[:, 64:] = jnp.zeros((512, 64), BF)
    filled = jnp.ones((32, LENGTH), BF)
    expand = expand.astype(F32)
    for index in range(3):
        vector = bypass_bias_ref[index : index + 1] if index < 2 else lift_bias_ref[...]
        bias_ref[index] = dot((expand * vector.astype(F32)).astype(BF), filled)
    row, col = picks(512, 64)
    repeat = one_hot((row // 128 == col // 16) & (row % 16 == col % 16))
    tall = dot(repeat, pair_y_ref[...])
    back = (tall * 0.125).astype(BF)
    row, col = picks(512, LENGTH)
    for c in range(8):
        inv_y_ref[:, c * 128 : c * 128 + 128] = jnp.where((row // 16) % 8 == c, back, 0.0).astype(BF)
    wide = tall.T
    row, col = picks(LENGTH, 512)
    for c in range(8):
        block = jnp.where((col // 16) % 8 == c, wide, 0.0).astype(BF)
        fwd_y_ref[c * 128 : c * 128 + 128, :] = block
    place = place_ref[0]
    xr, xi = one_x_ref[place // 2, 0:1, :], one_x_ref[place // 2, 1:2, :]
    yr = jnp.where(place % 2 == 0, one_y_ref[0, 0:1, :], one_y_ref[1, 0:1, :])
    yi = jnp.where(place % 2 == 0, one_y_ref[0, 1:2, :], one_y_ref[1, 1:2, :])
    pr, pi = xr * yr - xi * yi, xr * yi + xi * yr
    zr, zi = one_z_ref[0], one_z_ref[1]
    ones_ref[...] = jnp.concatenate([zr * pr - zi * pi, zr * pi + zi * pr], axis=0)


def fold_kernel(lift_ref, lift_bias_ref, weight_hbm, out_ref, weight, sem):
    (copy,) = fetch([(weight_hbm.at[0], weight, sem.at[0])])
    row, col = picks(HALF, 4)
    pick = one_hot((row % 8 == col))
    row, col = picks(HALF, HALF)
    lift = dot(pick, lift_ref[...]) + jnp.where(row % 8 == 4, lift_bias_ref[...].astype(F32), 0.0)
    row, col = picks(HALF, LENGTH)
    lift = dot(lift.astype(BF), one_hot(row == col // 4))
    lift = jnp.where(row // 8 == col % 4, lift, 0.0).astype(BF)
    copy.wait()
    for r in range(2):
        folded = dot(lift, weight[r]).astype(BF)
        for section in range(8):
            out_ref[section, r * HALF : r * HALF + HALF, :] = folded


def start_kernel(fields_hbm, pair_y_hbm, fwd_x_hbm, out_ref, fields, pair_y, fwd_x, rows, sem):
    copies = fetch(
        [
            (pair_y_hbm, pair_y, sem.at[0]),
            (fields_hbm.at[0], fields, sem.at[1]),
            (fwd_x_hbm, fwd_x, sem.at[2]),
        ]
    )
    copies[0].wait()
    row, col = picks(256, 64)
    repeat = one_hot((row // 64 == col // 16) & (row % 16 == col % 16))
    wide = dot(repeat, pair_y[...]).T
    row, col = picks(LENGTH, 256)
    fwd_y = jnp.concatenate(
        [jnp.where((col // 16) % 4 == c, wide, 0.0).astype(BF) for c in range(4)], axis=0
    )
    lane = lax.broadcasted_iota(jnp.int32, (64, LENGTH), 1)
    copies[1].wait()
    copies[2].wait()
    made = []
    for z in range(2):
        wide = jnp.concatenate([fields[c, z] for c in range(4)], axis=1)
        along = dot(wide, fwd_y).astype(BF)
        stacked = jnp.concatenate([along[:, :128], along[:, 128:]], axis=0)
        made.append(dot(fwd_x[...], stacked) * (1.0 / LENGTH))
    first = jnp.where(lane < 64, made[0], pltpu.roll(made[1], 64, 1))
    second = jnp.where(lane < 64, pltpu.roll(made[0], 64, 1), made[1])
    for h, value in enumerate((first, second)):
        for r in range(2):
            rows[pl.ds(h * 2 + r, 32, stride=4), :] = value[r * 32 : r * 32 + 32]
    out_ref[...] = rows[...].astype(BF)


def mix(weight_ref, modes, pattern):
    low = lax.broadcasted_iota(jnp.int32, (8, LENGTH), 0) < 4
    for pair in range(16):
        for r in range(2):
            for half in range(2):
                even = jnp.broadcast_to(modes[r, half, 2 * pair : 2 * pair + 1, :], (8, LENGTH))
                odd = jnp.broadcast_to(modes[r, half, 2 * pair + 1 : 2 * pair + 2, :], (8, LENGTH))
                pattern[pair, r, half] = jnp.where(low, even, odd)
    mixed = {}
    for g in range(4):
        total = {}
        for side in range(2):
            section = 2 * g + side
            acc = [[jnp.zeros((8, LENGTH), F32) for _ in range(2)] for _ in range(2)]
            for quad in range(8):
                real = weight_ref[section, 0, quad * 16 : quad * 16 + 16, :].astype(F32)
                imag = weight_ref[section, 1, quad * 16 : quad * 16 + 16, :].astype(F32)
                for sub in range(2):
                    pair = quad * 2 + sub
                    for half in range(2):
                        wr = real[sub * 8 : sub * 8 + 8, half * 128 : half * 128 + 128]
                        wi = imag[sub * 8 : sub * 8 + 8, half * 128 : half * 128 + 128]
                        mr, mi = pattern[pair, 0, half], pattern[pair, 1, half]
                        acc[0][half] = acc[0][half] + wr * mr - wi * mi
                        acc[1][half] = acc[1][half] + wr * mi + wi * mr
            for r in range(2):
                for half in range(2):
                    value = acc[r][half]
                    total[side, r, half] = value + pltpu.roll(value, 4, 0)
        for r in range(2):
            for half in range(2):
                mixed[g, r, half] = jnp.where(low, total[0, r, half], total[1, r, half])
    return mixed


def first_mix(folded_ref, modes):
    sub = lax.broadcasted_iota(jnp.int32, (8, LENGTH), 0)
    mixed = {}
    for g in range(4):
        for row in range(0, 8, 2):
            section, o = 2 * g + row // 4, row % 4
            real = folded_ref[section, o * 8 : o * 8 + 16, :].astype(F32)
            imag = folded_ref[section, HALF + o * 8 : HALF + o * 8 + 16, :].astype(F32)
            for more in range(2):
                for half in range(2):
                    wr = real[more * 8 : more * 8 + 8, half * 128 : half * 128 + 128]
                    wi = imag[more * 8 : more * 8 + 8, half * 128 : half * 128 + 128]
                    mr, mi = modes[0, half], modes[1, half]
                    for r, value in enumerate((wr * mr - wi * mi, wr * mi + wi * mr)):
                        for step in (4, 2, 1):
                            value = value + pltpu.roll(value, step, 0)
                        if row + more:
                            value = jnp.where(sub == row + more, value, mixed[g, r, half])
                        mixed[g, r, half] = value
    return mixed


def evaluate(mixed, turned, z_ref, out_ref):
    slot = lax.broadcasted_iota(jnp.int32, (8, LENGTH), 1) // K
    for py in range(K):
        half, at = py // 8, py % 8
        value = None
        for g in range(4):
            for r in range(2):
                where = 2 * g + r
                moved = mixed[g, r, half]
                if where != at:
                    moved = pltpu.roll(moved, (where - at) * K % LENGTH, 1)
                value = moved if value is None else jnp.where(slot == where, moved, value)
        turned[pl.ds(py, 8, stride=K), :] = value
    out_ref[...] = nt_dot(z_ref[:1024], turned[...].astype(BF)).astype(BF)


def unravel(turned, groups, modes):
    slot = lax.broadcasted_iota(jnp.int32, (8, LENGTH), 1) // K
    parts = [turned[pl.ds(py, 8, stride=K), :] for py in range(K)]
    for g in range(groups):
        for r in range(2):
            source = 2 * g + r
            for half in range(2):
                value = None
                for at in range(8):
                    moved = parts[half * 8 + at]
                    if at != source:
                        moved = pltpu.roll(moved, (at - source) * K % LENGTH, 1)
                    value = moved if value is None else jnp.where(slot == at, moved, value)
                modes[r, half, g * 8 : g * 8 + 8, :] = value


def dropped(place_ref, shape):
    row = lax.broadcasted_iota(jnp.int32, shape, 0)
    lane = lax.broadcasted_iota(jnp.int32, shape, 1)
    origin = jnp.logical_and(row % K == 0, lane % K == 0)
    return jnp.logical_and(origin, place_ref[0] == 0)


def first_mix_kernel(
    place_ref, got_ref, folded_ref, ones_ref, z_ref, out_ref, turned, modes
):
    both = dot(z_ref[2048:], got_ref[...])
    lane = lax.broadcasted_iota(jnp.int32, (HALF, LENGTH), 1)
    value = both[:HALF] + pltpu.roll(both[HALF:], 64, 1)
    value = jnp.where(lane < 64, value, 0.0) * (1.0 / math.sqrt(LENGTH))
    value = jnp.where(lane // K == 4, ones_ref[...], value)
    value = jnp.where(dropped(place_ref, value.shape), 0.0, value)
    value = jnp.concatenate([value, jnp.zeros((LENGTH - HALF, LENGTH), F32)], axis=0)
    turned[...] = value.T
    unravel(turned, 1, modes)
    evaluate(first_mix(folded_ref, modes), turned, z_ref, out_ref)


def mix_kernel(
    place_ref, got_ref, z_ref, weight_hbm, out_ref, weight, turned, modes, pattern, sem
):
    (copy,) = fetch([(weight_hbm, weight, sem.at[0])])
    value = None
    for block in range(8):
        span = slice(block * 128, block * 128 + 128)
        part = dot(z_ref[1024 + block * 128 : 1152 + block * 128], got_ref[span])
        value = part if value is None else value + part
    value = value * (1.0 / math.sqrt(LENGTH))
    value = jnp.where(dropped(place_ref, value.shape), 0.0, value)
    turned[...] = value.T
    unravel(turned, 4, modes)
    copy.wait()
    evaluate(mix(weight, modes, pattern), turned, z_ref, out_ref)


def inverse(got_ref, x_ref, inv_y_ref, rows, field):
    rows[...] = got_ref[...].astype(F32)
    for g in range(4):
        for z in range(2):
            parts = []
            for h in range(2):
                pieces = [
                    rows[pl.ds(h * 16 + g * 4 + r * 2 + z, 32, stride=32), :] for r in range(2)
                ]
                parts.append(jnp.concatenate(pieces, axis=0).astype(BF))
            along = dot(x_ref[64:, :64], jnp.concatenate(parts, axis=1)).astype(BF)
            wide = jnp.concatenate([along[:128], along[128:]], axis=1)
            made = dot(wide, inv_y_ref[...])
            for o in range(8):
                field[g * 8 + o, z] = made[:, o * 128 : o * 128 + 128]


def activate(value):
    inner = value * (0.7978845608028654 + 0.035677408136300125 * value * value)
    half = 0.5 * value
    return half + half * jnp.tanh(inner)


def pointwise(block, hidden, kb_ref, bias, field):
    bypassed = dot(kb_ref[...], hidden)
    made = []
    for z in range(2):
        part = field[:, z, block * 16 : block * 16 + 16, :].reshape(512, LENGTH)
        value = bypassed[:, z * 128 : z * 128 + 128] + bias + part
        made.append(activate(value).astype(BF))
    return made


def middle_kernel(
    got_ref, kl_ref, kb_ref, bias_ref, inv_y_ref, fwd_y_ref, x_ref, fields_hbm, hidden_hbm, out_ref,
    fields, rows, field, hidden, sem,
):
    (copy,) = fetch([(fields_hbm.at[0], fields, sem.at[0])])
    inverse(got_ref, x_ref, inv_y_ref, rows, field)
    lift_bias = bias_ref[2]
    lift_bias = jnp.concatenate([lift_bias, lift_bias], axis=1)
    copy.wait()
    for block in range(8):
        span = slice(block * 16, block * 16 + 16)
        raw = [fields[:, z, span, :].reshape(64, LENGTH) for z in range(2)]
        lifted = dot(kl_ref[:, :64], jnp.concatenate(raw, axis=1)) + lift_bias
        made = pointwise(block, lifted.astype(BF), kb_ref.at[0], bias_ref[0], field)
        for z in range(2):
            hidden[:, z, span, :] = made[z].reshape(32, 16, LENGTH)
    (kept,) = fetch([(hidden, hidden_hbm, sem.at[1])])
    for g in range(4):
        for z in range(2):
            wide = jnp.concatenate([hidden[g * 8 + c, z] for c in range(8)], axis=1)
            along = dot(wide, fwd_y_ref[...]).astype(BF)
            stacked = jnp.concatenate([along[:, :256], along[:, 256:]], axis=0)
            spectrum = dot(x_ref[:64], stacked) * (1.0 / LENGTH)
            for h in range(2):
                for r in range(2):
                    at = h * 16 + g * 4 + r * 2 + z
                    rows[pl.ds(at, 32, stride=32), :] = spectrum[
                        r * 32 : r * 32 + 32, h * 128 : h * 128 + 128
                    ]
    out_ref[...] = rows[...].astype(BF)
    kept.wait()


def last_kernel(
    got_ref, kb_ref, bias_ref, inv_y_ref, x_ref, hidden_hbm, out_hbm, hidden, rows, field, made_ref,
    sem,
):
    (copy,) = fetch([(hidden_hbm, hidden, sem.at[0])])
    inverse(got_ref, x_ref, inv_y_ref, rows, field)
    copy.wait()
    kept = []
    for block in range(8):
        span = slice(block * 16, block * 16 + 16)
        raw = [hidden[:, z, span, :].reshape(512, LENGTH) for z in range(2)]
        made = pointwise(block, jnp.concatenate(raw, axis=1), kb_ref.at[1], bias_ref[1], field)
        for z in range(2):
            made_ref[:, z, span, :] = made[z].reshape(32, 16, LENGTH)
        kept += fetch([(made_ref.at[:, :, span, :], out_hbm.at[0, :, :, span, :], sem.at[1 + block])])
    for copy in kept:
        copy.wait()


def call(kernel, name, inputs, outputs, scratch, sems=0, limit=24):
    spaces = {"s": pltpu.SMEM, "v": pltpu.VMEM, "p": pltpu.VMEM, "h": pltpu.HBM, "f": pltpu.HBM}
    fetched = [index for index, letter in enumerate(inputs) if letter == "f"]

    def run(*arrays):
        buffers = [pltpu.VMEM(arrays[index].shape, arrays[index].dtype) for index in fetched]
        own = [pltpu.VMEM(shape, kind) for shape, kind in scratch]
        if sems:
            own.append(pltpu.SemaphoreType.DMA((sems,)))
        if fetched:
            buffers.append(pltpu.SemaphoreType.DMA((len(fetched),)))

        def body(*refs):
            refs = list(refs)
            if fetched:
                first = len(inputs) + len(outputs) + len(own)
                copies = []
                for order, index in enumerate(fetched):
                    copies.append((refs[index], refs[first + order], refs[-1].at[order]))
                    refs[index] = refs[first + order]
                for copy in fetch(copies):
                    copy.wait()
                refs = refs[:first]
            kernel(*refs)

        placed = []
        for letter, array in zip(inputs, arrays):
            if letter in "hfp":
                array = pltpu.with_memory_space_constraint(array, spaces[letter])
            placed.append(array)
        return pl.pallas_call(
            body,
            name=name,
            out_shape=[spaces[letter](shape, kind) for letter, shape, kind in outputs],
            in_specs=[pl.BlockSpec(memory_space=spaces[letter]) for letter in inputs],
            out_specs=[pl.BlockSpec(memory_space=spaces[letter]) for letter, _, _ in outputs],
            scratch_shapes=own + buffers,
            compiler_params=pltpu.CompilerParams(vmem_limit_bytes=limit << 20),
        )(*placed)

    return run


def exchange(value, axis="slab"):
    return lax.all_to_all(value, axis, split_axis=0, concat_axis=0, tiled=True)


tie = lax.optimization_barrier


def solution(mesh):
    table, one_x, one_z = make_tables()
    const = {name: value.astype(ml_dtypes.bfloat16) for name, value in table.items()}
    ones_x = np.repeat(split(one_x).T[:, :, None], LENGTH, axis=2)
    ones_y = np.tile(split(one_x).reshape(2, 2, 1, K), (1, 1, 8, 1)).reshape(2, 2, LENGTH)
    ones_y = ones_y.transpose(1, 0, 2)
    ones_z = np.repeat(split(one_z)[:, :, None], LENGTH, axis=2)

    def on_device(fields, lift_weight, lift_bias, spectral_weight, bypass_weight, bypass_bias):
        place = lax.axis_index("slab").reshape(1)
        lift_bias = lift_bias[None]
        packed, cube = (1024, LENGTH), (32, 2, 128, 128)
        (spectrum,) = call(
            start_kernel,
            "start",
            "hhh",
            [("v", (128, LENGTH), BF)],
            [((4, 2, 128, 128), BF), ((64, 128), BF), ((64, 256), BF), ((128, 128), F32)],
            sems=3,
        )(fields, const["pair_y"], const["fwd_x"])
        spectrum, spectral_weight, bypass_weight = tie((spectrum, spectral_weight, bypass_weight))
        spectrum = exchange(spectrum)
        weight = spectral_weight.reshape(2, 2, LENGTH, 256)
        (folded,) = call(
            fold_kernel, "fold", "ffh", [("v", (8, 64, 256), BF)], [((2, 128, 256), BF)], sems=1
        )(lift_weight, lift_bias, weight)
        kb, kl, bias, fwd_y, inv_y, ones, z_table, x_table = call(
            spread_kernel,
            "spread",
            "s" + "f" * 10,
            [
                ("v", (2, 512, 512), BF),
                ("v", (512, 128), BF),
                ("v", (3, 512, LENGTH), F32),
                ("v", (1024, 512), BF),
                ("v", (512, 1024), BF),
                ("v", (HALF, LENGTH), F32),
                ("v", (2112, 128), BF),
                ("v", (320, 256), BF),
            ],
            [],
        )(
            place, ones_x, bypass_weight, lift_weight, bypass_bias, lift_bias, const["pair_y"],
            ones_y, ones_z, const["z"], const["x"],
        )
        later = weight[1]
        folded, ones, later, _ = tie((folded, ones, later, spectrum))
        folded = exchange(folded.reshape(512, 256), "section").reshape(8, 64, 256)
        _, later = tie((folded, later))
        gathered = lax.all_gather(later, "section", axis=0)
        (planes,) = call(
            first_mix_kernel,
            "mix0",
            "spppp",
            [("v", packed, BF)],
            [((128, 128), F32), ((2, 2, 8, 128), F32)],
        )(place, spectrum, folded, ones, z_table)
        hidden, spectrum = call(
            middle_kernel,
            "middle",
            "ppppppph",
            [("h", cube, BF), ("v", packed, BF)],
            [((4, 2, 128, 128), BF), (packed, F32), (cube, F32), (cube, BF)],
            sems=2,
        )(exchange(planes), kl, kb, bias, inv_y, fwd_y, x_table, fields)
        (planes,) = call(
            mix_kernel,
            "mix1",
            "spph",
            [("v", packed, BF)],
            [
                ((8, 2, 128, 256), BF), ((128, 128), F32), ((2, 2, 32, 128), F32),
                ((16, 2, 2, 8, 128), F32),
            ],
            sems=1,
        )(place, exchange(spectrum), z_table, gathered)
        (features,) = call(
            last_kernel,
            "last",
            "ppppph",
            [("h", (1,) + cube, BF)],
            [(cube, BF), (packed, F32), (cube, F32), (cube, BF)],
            sems=9,
        )(exchange(planes), kb, bias, inv_y, x_table, hidden)
        return features

    placed = (
        P("section", None, "slab", None, None),
        P(),
        P(),
        P(None, None, None, "section", "slab"),
        P(),
        P(),
    )
    return jax.shard_map(
        on_device,
        mesh=mesh,
        in_specs=placed,
        out_specs=P("section", None, "slab", None, None),
        check_vma=False,
    )
```

```python
import math

import jax
import jax.numpy as jnp
import ml_dtypes
import numpy as np
from jax import lax
from jax.experimental import pallas as pl
from jax.experimental.pallas import tpu as pltpu
from jax.sharding import PartitionSpec as P

K = 16
HALF = 2 * K
LENGTH = 128
SLABS = 64
BF = jnp.bfloat16
F32 = jnp.float32


def wave(freqs):
    where = np.arange(LENGTH, dtype=np.int64)[None, :]
    step = (freqs % LENGTH)[:, None] * where % LENGTH
    phase = step.astype(np.float32) * np.float32(2.0 * math.pi / LENGTH)
    cosine = np.cos(phase).astype(ml_dtypes.bfloat16).astype(np.float32)
    sine = np.sin(phase).astype(ml_dtypes.bfloat16).astype(np.float32)
    return cosine, sine


def make_tables():
    base = np.arange(HALF)
    signed = np.where(base < K, base, base - HALF)
    cos, sin = wave(signed)
    cos_z, sin_z = wave(np.arange(K))
    double = np.where(np.arange(K) == 0, 1.0, 2.0)[:, None]
    table = {}
    table["pair_y"] = np.concatenate([cos, -sin], 0)
    table["fwd_x"] = np.concatenate(
        [np.concatenate([cos, sin], 1), np.concatenate([-sin, cos], 1)], 0
    )
    fwd_z = np.stack([np.stack([cos_z, sin_z], 1), np.stack([-sin_z, cos_z], 1)], 0)
    fwd_z = fwd_z.reshape(2, K, 2, SLABS, 2)
    full = np.einsum("gf,akrsz->gaksfrz", np.eye(4), fwd_z)
    full = full.reshape(4 * HALF, 8, LENGTH).transpose(1, 0, 2).reshape(1024, LENGTH)
    first = np.einsum("akrsz->zaksr", fwd_z).reshape(2 * HALF, SLABS * 2)
    cz, sz = cos_z * double * 0.25, sin_z * double * 0.25
    inv_z = np.stack([np.stack([cz, -sz], 0), np.stack([sz, cz], 0)], 0)
    inv_z = inv_z.reshape(2, 2, K, SLABS, 2)
    back = np.einsum("gf,arksz->sgazfrk", np.eye(4), inv_z).reshape(SLABS * 16, 4 * HALF)
    table["z"] = np.concatenate([back, full, first], 0)
    inv_x = np.stack([np.stack([cos, -sin], 0), np.stack([sin, cos], 0)], 0)
    table["inv_x"] = np.einsum("arpx->axrp", inv_x).reshape(2 * LENGTH, 2 * HALF) * 0.125
    table["x"] = np.concatenate([table["fwd_x"], np.pad(table.pop("inv_x"), ((0, 0), (0, 192)))], 0)
    one_x = (cos.sum(1) - 1j * sin.sum(1)) / math.sqrt(LENGTH)
    one_z = (cos_z.sum(1) - 1j * sin_z.sum(1)) / math.sqrt(LENGTH)
    return table, one_x, one_z


def split(value):
    return np.stack([value.real, value.imag], 0).astype(np.float32)


def dot(left, right):
    return jnp.dot(left, right, preferred_element_type=F32)


def nt_dot(left, right):
    return lax.dot_general(left, right, (((1,), (1,)), ((), ())), preferred_element_type=F32)


def picks(rows, cols):
    row = lax.broadcasted_iota(jnp.int32, (rows, cols), 0)
    col = lax.broadcasted_iota(jnp.int32, (rows, cols), 1)
    return row, col


def one_hot(mask):
    return jnp.where(mask, 1.0, 0.0).astype(BF)


def fetch(copies):
    started = [pltpu.make_async_copy(source, target, sem) for source, target, sem in copies]
    for copy in started:
        copy.start()
    return started


def spread_kernel(
    place_ref, one_x_ref, bypass_ref, lift_ref, bypass_bias_ref, lift_bias_ref, pair_y_ref,
    one_y_ref, one_z_ref, z_ref, x_ref, kb_ref, kc_ref, bias_ref, fwd_y_ref, inv_y_ref, ones_ref,
    z_out, x_out,
):
    z_out[...] = z_ref[...]
    x_out[...] = x_ref[...]
    row, col = picks(512, 32)
    expand = one_hot(row // 16 == col)
    row, col = picks(512, 512)
    tall = nt_dot(expand, bypass_ref[1]).astype(BF)
    kb_ref[...] = jnp.where((row % 16) == (col % 16), nt_dot(tall, expand), 0.0).astype(BF)
    joint = dot(lift_ref[...], bypass_ref[0])
    high = joint.astype(BF)
    low = (joint - high.astype(F32)).astype(BF)
    row, col = picks(64, 4)
    expand4 = one_hot(row // 16 == col)
    row, col = picks(512, 64)
    for index, part in enumerate((high, low)):
        wide = nt_dot(nt_dot(expand, part).astype(BF), expand4)
        wide = jnp.where((row % 16) == (col % 16), wide, 0.0).astype(BF)
        kc_ref[:, index * 64 : index * 64 + 64] = wide
    filled = jnp.ones((32, LENGTH), BF)
    row, col = picks(32, 32)
    eye = jnp.where(row == col, 1.0, 0.0)

    def column(vector):
        return dot((eye * vector.astype(F32)).astype(BF), filled)

    shift = column(bypass_bias_ref[0:1]) + lax.dot_general(
        bypass_ref[0], column(lift_bias_ref[...]).astype(BF), (((0,), (0,)), ((), ())),
        preferred_element_type=F32,
    )
    for index, value in enumerate((shift, column(bypass_bias_ref[1:2]))):
        bias_ref[index] = jnp.dot(
            expand.astype(F32), value, precision=lax.Precision.HIGHEST, preferred_element_type=F32
        )
    row, col = picks(256, 64)
    repeat = one_hot((row // 64 == col // 16) & (row % 16 == col % 16))
    tall = dot(repeat, pair_y_ref[...])
    back = tall * 0.125
    row, col = picks(256, LENGTH)
    for c in range(4):
        block = jnp.where((row // 16) % 4 == c, back, 0.0).astype(BF)
        inv_y_ref[:, c * 128 : c * 128 + 128] = block
    wide = tall.T
    row, col = picks(LENGTH, 256)
    for c in range(4):
        block = jnp.where((col // 16) % 4 == c, wide, 0.0).astype(BF)
        fwd_y_ref[c * 128 : c * 128 + 128, :] = block
    place = place_ref[0]
    xr, xi = one_x_ref[place // 2, 0:1, :], one_x_ref[place // 2, 1:2, :]
    yr = jnp.where(place % 2 == 0, one_y_ref[0, 0:1, :], one_y_ref[1, 0:1, :])
    yi = jnp.where(place % 2 == 0, one_y_ref[0, 1:2, :], one_y_ref[1, 1:2, :])
    pr, pi = xr * yr - xi * yi, xr * yi + xi * yr
    zr, zi = one_z_ref[0], one_z_ref[1]
    ones_ref[...] = jnp.concatenate([zr * pr - zi * pi, zr * pi + zi * pr], axis=0)


def fold_kernel(lift_ref, lift_bias_ref, weight_hbm, out_ref, weight, sem):
    (copy,) = fetch([(weight_hbm.at[0], weight, sem.at[0])])
    row, col = picks(HALF, 4)
    pick = one_hot((row % 8 == col))
    row, col = picks(HALF, HALF)
    lift = dot(pick, lift_ref[...]) + jnp.where(row % 8 == 4, lift_bias_ref[...].astype(F32), 0.0)
    row, col = picks(HALF, LENGTH)
    lift = dot(lift.astype(BF), one_hot(row == col // 4))
    lift = jnp.where(row // 8 == col % 4, lift, 0.0).astype(BF)
    copy.wait()
    for r in range(2):
        folded = dot(lift, weight[r]).astype(BF)
        for section in range(8):
            out_ref[section, r * HALF : r * HALF + HALF, :] = folded


def start_kernel(fields_hbm, pair_y_hbm, fwd_x_hbm, out_ref, fields, pair_y, fwd_x, rows, sem):
    copies = fetch(
        [
            (pair_y_hbm, pair_y, sem.at[0]),
            (fields_hbm.at[0], fields, sem.at[1]),
            (fwd_x_hbm, fwd_x, sem.at[2]),
        ]
    )
    copies[0].wait()
    row, col = picks(256, 64)
    repeat = one_hot((row // 64 == col // 16) & (row % 16 == col % 16))
    wide = dot(repeat, pair_y[...]).T
    row, col = picks(LENGTH, 256)
    fwd_y = jnp.concatenate(
        [jnp.where((col // 16) % 4 == c, wide, 0.0).astype(BF) for c in range(4)], axis=0
    )
    lane = lax.broadcasted_iota(jnp.int32, (64, LENGTH), 1)
    copies[1].wait()
    copies[2].wait()
    made = []
    for z in range(2):
        wide = jnp.concatenate([fields[c, z] for c in range(4)], axis=1)
        along = dot(wide, fwd_y).astype(BF)
        stacked = jnp.concatenate([along[:, :128], along[:, 128:]], axis=0)
        made.append(dot(fwd_x[...], stacked) * (1.0 / LENGTH))
    first = jnp.where(lane < 64, made[0], pltpu.roll(made[1], 64, 1))
    second = jnp.where(lane < 64, pltpu.roll(made[0], 64, 1), made[1])
    for h, value in enumerate((first, second)):
        for r in range(2):
            rows[pl.ds(h * 2 + r, 32, stride=4), :] = value[r * 32 : r * 32 + 32]
    out_ref[...] = rows[...].astype(BF)


def mix(weight_ref, modes, pattern):
    low = lax.broadcasted_iota(jnp.int32, (8, LENGTH), 0) < 4
    for pair in range(16):
        for r in range(2):
            for half in range(2):
                even = jnp.broadcast_to(modes[r, half, 2 * pair : 2 * pair + 1, :], (8, LENGTH))
                odd = jnp.broadcast_to(modes[r, half, 2 * pair + 1 : 2 * pair + 2, :], (8, LENGTH))
                pattern[pair, r, half] = jnp.where(low, even, odd)
    mixed = {}
    for g in range(4):
        total = {}
        for side in range(2):
            section = 2 * g + side
            acc = [[jnp.zeros((8, LENGTH), F32) for _ in range(2)] for _ in range(2)]
            for quad in range(8):
                real = weight_ref[section, 0, quad * 16 : quad * 16 + 16, :].astype(F32)
                imag = weight_ref[section, 1, quad * 16 : quad * 16 + 16, :].astype(F32)
                for sub in range(2):
                    pair = quad * 2 + sub
                    for half in range(2):
                        wr = real[sub * 8 : sub * 8 + 8, half * 128 : half * 128 + 128]
                        wi = imag[sub * 8 : sub * 8 + 8, half * 128 : half * 128 + 128]
                        mr, mi = pattern[pair, 0, half], pattern[pair, 1, half]
                        acc[0][half] = acc[0][half] + wr * mr - wi * mi
                        acc[1][half] = acc[1][half] + wr * mi + wi * mr
            for r in range(2):
                for half in range(2):
                    value = acc[r][half]
                    total[side, r, half] = value + pltpu.roll(value, 4, 0)
        for r in range(2):
            for half in range(2):
                mixed[g, r, half] = jnp.where(low, total[0, r, half], total[1, r, half])
    return mixed


def first_mix(folded_ref, modes):
    sub = lax.broadcasted_iota(jnp.int32, (8, LENGTH), 0)
    mixed = {}
    for g in range(4):
        for row in range(0, 8, 2):
            section, o = 2 * g + row // 4, row % 4
            real = folded_ref[section, o * 8 : o * 8 + 16, :].astype(F32)
            imag = folded_ref[section, HALF + o * 8 : HALF + o * 8 + 16, :].astype(F32)
            for more in range(2):
                for half in range(2):
                    wr = real[more * 8 : more * 8 + 8, half * 128 : half * 128 + 128]
                    wi = imag[more * 8 : more * 8 + 8, half * 128 : half * 128 + 128]
                    mr, mi = modes[0, half], modes[1, half]
                    for r, value in enumerate((wr * mr - wi * mi, wr * mi + wi * mr)):
                        for step in (4, 2, 1):
                            value = value + pltpu.roll(value, step, 0)
                        if row + more:
                            value = jnp.where(sub == row + more, value, mixed[g, r, half])
                        mixed[g, r, half] = value
    return mixed


def evaluate(mixed, turned, z_ref, out_ref):
    slot = lax.broadcasted_iota(jnp.int32, (8, LENGTH), 1) // K
    for py in range(K):
        half, at = py // 8, py % 8
        value = None
        for g in range(4):
            for r in range(2):
                where = 2 * g + r
                moved = mixed[g, r, half]
                if where != at:
                    moved = pltpu.roll(moved, (where - at) * K % LENGTH, 1)
                value = moved if value is None else jnp.where(slot == where, moved, value)
        turned[pl.ds(py, 8, stride=K), :] = value
    out_ref[...] = nt_dot(z_ref[:1024], turned[...].astype(BF)).astype(BF)


def unravel(turned, groups, modes):
    slot = lax.broadcasted_iota(jnp.int32, (8, LENGTH), 1) // K
    parts = [turned[pl.ds(py, 8, stride=K), :] for py in range(K)]
    for g in range(groups):
        for r in range(2):
            source = 2 * g + r
            for half in range(2):
                value = None
                for at in range(8):
                    moved = parts[half * 8 + at]
                    if at != source:
                        moved = pltpu.roll(moved, (at - source) * K % LENGTH, 1)
                    value = moved if value is None else jnp.where(slot == at, moved, value)
                modes[r, half, g * 8 : g * 8 + 8, :] = value


def dropped(place_ref, shape):
    row = lax.broadcasted_iota(jnp.int32, shape, 0)
    lane = lax.broadcasted_iota(jnp.int32, shape, 1)
    origin = jnp.logical_and(row % K == 0, lane % K == 0)
    return jnp.logical_and(origin, place_ref[0] == 0)


def first_mix_kernel(
    place_ref, got_ref, folded_ref, ones_ref, z_ref, out_ref, turned, modes
):
    both = dot(z_ref[2048:], got_ref[...])
    lane = lax.broadcasted_iota(jnp.int32, (HALF, LENGTH), 1)
    value = both[:HALF] + pltpu.roll(both[HALF:], 64, 1)
    value = jnp.where(lane < 64, value, 0.0) * (1.0 / math.sqrt(LENGTH))
    value = jnp.where(lane // K == 4, ones_ref[...], value)
    value = jnp.where(dropped(place_ref, value.shape), 0.0, value)
    value = jnp.concatenate([value, jnp.zeros((LENGTH - HALF, LENGTH), F32)], axis=0)
    turned[...] = value.T
    unravel(turned, 1, modes)
    evaluate(first_mix(folded_ref, modes), turned, z_ref, out_ref)


def mix_kernel(
    place_ref, got_ref, z_ref, weight_hbm, out_ref, weight, turned, modes, pattern, sem
):
    (copy,) = fetch([(weight_hbm, weight, sem.at[0])])
    value = None
    for block in range(8):
        span = slice(block * 128, block * 128 + 128)
        part = dot(z_ref[1024 + block * 128 : 1152 + block * 128], got_ref[span])
        value = part if value is None else value + part
    value = value * (1.0 / math.sqrt(LENGTH))
    value = jnp.where(dropped(place_ref, value.shape), 0.0, value)
    turned[...] = value.T
    unravel(turned, 4, modes)
    copy.wait()
    evaluate(mix(weight, modes, pattern), turned, z_ref, out_ref)


def swapped(first, second):
    low = lax.broadcasted_iota(jnp.int32, first.shape, 1) < 64
    return (
        jnp.where(low, first, pltpu.roll(second, 64, 1)),
        jnp.where(low, pltpu.roll(first, 64, 1), second),
    )


def inverse(got_ref, x_ref, inv_y_ref, rows, field):
    rows[...] = got_ref[...].astype(F32)
    for g in range(4):
        for z in range(2):
            parts = []
            for h in range(2):
                pieces = [
                    rows[pl.ds(h * 16 + g * 4 + r * 2 + z, 32, stride=32), :] for r in range(2)
                ]
                parts.append(jnp.concatenate(pieces, axis=0))
            parts = jnp.concatenate(swapped(*parts), axis=1).astype(BF)
            along = dot(x_ref[64:, :64], parts).astype(BF)
            for quad in range(2):
                lanes = slice(quad * 128, quad * 128 + 128)
                wide = jnp.concatenate([along[:128, lanes], along[128:, lanes]], axis=1)
                made = dot(wide, inv_y_ref[...])
                for o in range(4):
                    field[g * 8 + quad * 4 + o, z] = made[:, o * 128 : o * 128 + 128]


def activate(value):
    inner = value * (0.7978845608028654 + 0.035677408136300125 * value * value)
    half = 0.5 * value
    return half + half * jnp.tanh(inner)


def pointwise(block, hidden, map_ref, bias, field):
    bypassed = dot(map_ref[...], hidden)
    made = []
    for z in range(2):
        part = field[:, z, block * 16 : block * 16 + 16, :].reshape(512, LENGTH)
        value = bypassed[:, z * 128 : z * 128 + 128] + bias + part
        made.append(activate(value).astype(BF))
    return made


def middle_kernel(
    got_ref, kc_ref, bias_ref, inv_y_ref, fwd_y_ref, x_ref, fields_hbm, hidden_hbm, out_ref,
    fields, rows, field, hidden, sem,
):
    (copy,) = fetch([(fields_hbm.at[0], fields, sem.at[0])])
    inverse(got_ref, x_ref, inv_y_ref, rows, field)
    copy.wait()
    for block in range(8):
        span = slice(block * 16, block * 16 + 16)
        raw = [fields[:, z, span, :].reshape(64, LENGTH) for z in range(2)]
        raw = jnp.concatenate(raw, axis=1)
        made = pointwise(block, jnp.concatenate([raw, raw], axis=0), kc_ref, bias_ref[0], field)
        for z in range(2):
            hidden[:, z, span, :] = made[z].reshape(32, 16, LENGTH)
    (kept,) = fetch([(hidden, hidden_hbm, sem.at[1])])
    for g in range(4):
        for z in range(2):
            stacked = []
            for first in (g * 8, g * 8 + 4):
                wide = jnp.concatenate([hidden[first + c, z] for c in range(4)], axis=1)
                along = dot(wide, fwd_y_ref[...]).astype(BF)
                stacked.append(jnp.concatenate([along[:, :128], along[:, 128:]], axis=0))
            spectrum = dot(x_ref[:64], jnp.concatenate(stacked, axis=1)) * (1.0 / LENGTH)
            for h, value in enumerate(swapped(spectrum[:, :128], spectrum[:, 128:])):
                for r in range(2):
                    at = h * 16 + g * 4 + r * 2 + z
                    rows[pl.ds(at, 32, stride=32), :] = value[r * 32 : r * 32 + 32]
    out_ref[...] = rows[...].astype(BF)
    kept.wait()


def last_kernel(
    got_ref, kb_ref, bias_ref, inv_y_ref, x_ref, hidden_hbm, out_hbm, hidden, rows, field, made_ref,
    sem,
):
    (copy,) = fetch([(hidden_hbm, hidden, sem.at[0])])
    inverse(got_ref, x_ref, inv_y_ref, rows, field)
    copy.wait()
    kept = []
    for block in range(8):
        span = slice(block * 16, block * 16 + 16)
        raw = [hidden[:, z, span, :].reshape(512, LENGTH) for z in range(2)]
        made = pointwise(block, jnp.concatenate(raw, axis=1), kb_ref, bias_ref[1], field)
        for z in range(2):
            made_ref[:, z, span, :] = made[z].reshape(32, 16, LENGTH)
        kept += fetch([(made_ref.at[:, :, span, :], out_hbm.at[0, :, :, span, :], sem.at[1 + block])])
    for copy in kept:
        copy.wait()


def call(kernel, name, inputs, outputs, scratch, sems=0, limit=24):
    spaces = {"s": pltpu.SMEM, "v": pltpu.VMEM, "p": pltpu.VMEM, "h": pltpu.HBM, "f": pltpu.HBM}
    fetched = [index for index, letter in enumerate(inputs) if letter == "f"]

    def run(*arrays):
        buffers = [pltpu.VMEM(arrays[index].shape, arrays[index].dtype) for index in fetched]
        own = [pltpu.VMEM(shape, kind) for shape, kind in scratch]
        if sems:
            own.append(pltpu.SemaphoreType.DMA((sems,)))
        if fetched:
            buffers.append(pltpu.SemaphoreType.DMA((len(fetched),)))

        def body(*refs):
            refs = list(refs)
            if fetched:
                first = len(inputs) + len(outputs) + len(own)
                copies = []
                for order, index in enumerate(fetched):
                    copies.append((refs[index], refs[first + order], refs[-1].at[order]))
                    refs[index] = refs[first + order]
                for copy in fetch(copies):
                    copy.wait()
                refs = refs[:first]
            kernel(*refs)

        placed = []
        for letter, array in zip(inputs, arrays):
            if letter in "hfp":
                array = pltpu.with_memory_space_constraint(array, spaces[letter])
            placed.append(array)
        return pl.pallas_call(
            body,
            name=name,
            out_shape=[spaces[letter](shape, kind) for letter, shape, kind in outputs],
            in_specs=[pl.BlockSpec(memory_space=spaces[letter]) for letter in inputs],
            out_specs=[pl.BlockSpec(memory_space=spaces[letter]) for letter, _, _ in outputs],
            scratch_shapes=own + buffers,
            compiler_params=pltpu.CompilerParams(vmem_limit_bytes=limit << 20),
        )(*placed)

    return run


def exchange(value, axis="slab"):
    return lax.all_to_all(value, axis, split_axis=0, concat_axis=0, tiled=True)


tie = lax.optimization_barrier


def solution(mesh):
    table, one_x, one_z = make_tables()
    const = {name: value.astype(ml_dtypes.bfloat16) for name, value in table.items()}
    ones_x = np.repeat(split(one_x).T[:, :, None], LENGTH, axis=2)
    ones_y = np.tile(split(one_x).reshape(2, 2, 1, K), (1, 1, 8, 1)).reshape(2, 2, LENGTH)
    ones_y = ones_y.transpose(1, 0, 2)
    ones_z = np.repeat(split(one_z)[:, :, None], LENGTH, axis=2)

    def on_device(fields, lift_weight, lift_bias, spectral_weight, bypass_weight, bypass_bias):
        place = lax.axis_index("slab").reshape(1)
        lift_bias = lift_bias[None]
        packed, cube = (1024, LENGTH), (32, 2, 128, 128)
        (spectrum,) = call(
            start_kernel,
            "start",
            "hhh",
            [("v", (128, LENGTH), BF)],
            [((4, 2, 128, 128), BF), ((64, 128), BF), ((64, 256), BF), ((128, 128), F32)],
            sems=3,
        )(fields, const["pair_y"], const["fwd_x"])
        spectrum, spectral_weight = tie((spectrum, spectral_weight))
        spectrum = exchange(spectrum)
        weight = spectral_weight.reshape(2, 2, LENGTH, 256)
        (folded,) = call(
            fold_kernel, "fold", "ffh", [("v", (8, 64, 256), BF)], [((2, 128, 256), BF)], sems=1
        )(lift_weight, lift_bias, weight)
        folded, bypass_weight, weight, _ = tie((folded, bypass_weight, weight, spectrum))
        gathered = lax.all_gather(weight[1], "section", axis=0)
        folded = exchange(folded.reshape(512, 256), "section").reshape(8, 64, 256)
        kb, kc, bias, fwd_y, inv_y, ones, z_table, x_table = call(
            spread_kernel,
            "spread",
            "s" + "f" * 10,
            [
                ("v", (512, 512), BF),
                ("v", (512, 128), BF),
                ("v", (2, 512, LENGTH), F32),
                ("v", (512, 256), BF),
                ("v", (256, 512), BF),
                ("v", (HALF, LENGTH), F32),
                ("v", (2112, 128), BF),
                ("v", (320, 256), BF),
            ],
            [],
        )(
            place, ones_x, bypass_weight, lift_weight, bypass_bias, lift_bias, const["pair_y"],
            ones_y, ones_z, const["z"], const["x"],
        )
        (planes,) = call(
            first_mix_kernel,
            "mix0",
            "spppp",
            [("v", packed, BF)],
            [((128, 128), F32), ((2, 2, 8, 128), F32)],
        )(place, spectrum, folded, ones, z_table)
        hidden, spectrum = call(
            middle_kernel,
            "middle",
            "pppppph",
            [("h", cube, BF), ("v", packed, BF)],
            [((4, 2, 128, 128), BF), (packed, F32), (cube, F32), (cube, BF)],
            sems=2,
        )(exchange(planes), kc, bias, inv_y, fwd_y, x_table, fields)
        (planes,) = call(
            mix_kernel,
            "mix1",
            "spph",
            [("v", packed, BF)],
            [
                ((8, 2, 128, 256), BF), ((128, 128), F32), ((2, 2, 32, 128), F32),
                ((16, 2, 2, 8, 128), F32),
            ],
            sems=1,
        )(place, exchange(spectrum), z_table, gathered)
        (features,) = call(
            last_kernel,
            "last",
            "ppppph",
            [("h", (1,) + cube, BF)],
            [(cube, BF), (packed, F32), (cube, F32), (cube, BF)],
            sems=9,
        )(exchange(planes), kb, bias, inv_y, x_table, hidden)
        return features

    placed = (
        P("section", None, "slab", None, None),
        P(),
        P(),
        P(None, None, None, "section", "slab"),
        P(),
        P(),
    )
    return jax.shard_map(
        on_device,
        mesh=mesh,
        in_specs=placed,
        out_specs=P("section", None, "slab", None, None),
        check_vma=False,
    )
```

```python
import math

import jax
import jax.numpy as jnp
import ml_dtypes
import numpy as np
from jax import lax
from jax.experimental import pallas as pl
from jax.experimental.pallas import tpu as pltpu
from jax.sharding import PartitionSpec as P

K = 16
HALF = 2 * K
LENGTH = 128
SLABS = 64
UNROLL_A = 4
UNROLL_B = 8
BF = jnp.bfloat16
F32 = jnp.float32


def wave(freqs):
    where = np.arange(LENGTH, dtype=np.int64)[None, :]
    step = (freqs % LENGTH)[:, None] * where % LENGTH
    phase = step.astype(np.float32) * np.float32(2.0 * math.pi / LENGTH)
    cosine = np.cos(phase).astype(ml_dtypes.bfloat16).astype(np.float32)
    sine = np.sin(phase).astype(ml_dtypes.bfloat16).astype(np.float32)
    return cosine, sine


def make_tables():
    base = np.arange(HALF)
    signed = np.where(base < K, base, base - HALF)
    cos, sin = wave(signed)
    cos_z, sin_z = wave(np.arange(K))
    double = np.where(np.arange(K) == 0, 1.0, 2.0)[:, None]
    table = {}
    table["pair_y"] = np.concatenate([cos, -sin], 0)
    table["fwd_x"] = np.concatenate(
        [np.concatenate([cos, sin], 1), np.concatenate([-sin, cos], 1)], 0
    )
    fwd_z = np.stack([np.stack([cos_z, sin_z], 1), np.stack([-sin_z, cos_z], 1)], 0)
    fwd_z = fwd_z.reshape(2, K, 2, SLABS, 2)
    full = np.einsum("gf,akrsz->gaksfrz", np.eye(4), fwd_z)
    full = full.reshape(4 * HALF, 8, LENGTH).transpose(1, 0, 2).reshape(1024, LENGTH)
    first = np.einsum("akrsz->zaksr", fwd_z).reshape(2 * HALF, SLABS * 2)
    cz, sz = cos_z * double * 0.25, sin_z * double * 0.25
    inv_z = np.stack([np.stack([cz, -sz], 0), np.stack([sz, cz], 0)], 0)
    inv_z = inv_z.reshape(2, 2, K, SLABS, 2)
    back = np.einsum("gf,arksz->sgazfrk", np.eye(4), inv_z).reshape(SLABS * 16, 4 * HALF)
    table["z"] = np.concatenate([back, full, first], 0)
    inv_x = np.stack([np.stack([cos, -sin], 0), np.stack([sin, cos], 0)], 0)
    table["inv_x"] = np.einsum("arpx->axrp", inv_x).reshape(2 * LENGTH, 2 * HALF) * 0.125
    table["x"] = np.concatenate([table["fwd_x"], np.pad(table.pop("inv_x"), ((0, 0), (0, 192)))], 0)
    one_x = (cos.sum(1) - 1j * sin.sum(1)) / math.sqrt(LENGTH)
    one_z = (cos_z.sum(1) - 1j * sin_z.sum(1)) / math.sqrt(LENGTH)
    return table, one_x, one_z


def split(value):
    return np.stack([value.real, value.imag], 0).astype(np.float32)


def dot(left, right):
    return jnp.dot(left, right, preferred_element_type=F32)


def nt_dot(left, right):
    return lax.dot_general(left, right, (((1,), (1,)), ((), ())), preferred_element_type=F32)


def picks(rows, cols):
    row = lax.broadcasted_iota(jnp.int32, (rows, cols), 0)
    col = lax.broadcasted_iota(jnp.int32, (rows, cols), 1)
    return row, col


def one_hot(mask):
    return jnp.where(mask, 1.0, 0.0).astype(BF)


def fetch(copies):
    started = [pltpu.make_async_copy(source, target, sem) for source, target, sem in copies]
    for copy in started:
        copy.start()
    return started


def spread_kernel(
    place_ref, one_x_ref, bypass_ref, lift_ref, bypass_bias_ref, lift_bias_ref, pair_y_ref,
    one_y_ref, one_z_ref, z_ref, x_ref, kb_ref, kc_ref, bias_ref, fwd_y_ref, inv_y_ref, ones_ref,
    z_out, x_out,
):
    z_out[...] = z_ref[...]
    x_out[...] = x_ref[...]
    row, col = picks(512, 32)
    expand = one_hot(row // 16 == col)
    row, col = picks(512, 512)
    tall = nt_dot(expand, bypass_ref[1]).astype(BF)
    kb_ref[...] = jnp.where((row % 16) == (col % 16), nt_dot(tall, expand), 0.0).astype(BF)
    joint = dot(lift_ref[...], bypass_ref[0])
    high = joint.astype(BF)
    low = (joint - high.astype(F32)).astype(BF)
    row, col = picks(64, 4)
    expand4 = one_hot(row // 16 == col)
    row, col = picks(512, 64)
    for index, part in enumerate((high, low)):
        wide = nt_dot(nt_dot(expand, part).astype(BF), expand4)
        wide = jnp.where((row % 16) == (col % 16), wide, 0.0).astype(BF)
        kc_ref[:, index * 64 : index * 64 + 64] = wide
    filled = jnp.ones((32, LENGTH), BF)
    row, col = picks(32, 32)
    eye = jnp.where(row == col, 1.0, 0.0)

    def column(vector):
        return dot((eye * vector.astype(F32)).astype(BF), filled)

    shift = column(bypass_bias_ref[0:1]) + lax.dot_general(
        bypass_ref[0], column(lift_bias_ref[...]).astype(BF), (((0,), (0,)), ((), ())),
        preferred_element_type=F32,
    )
    for index, value in enumerate((shift, column(bypass_bias_ref[1:2]))):
        bias_ref[index] = jnp.dot(
            expand.astype(F32), value, precision=lax.Precision.HIGHEST, preferred_element_type=F32
        )
    row, col = picks(256, 64)
    repeat = one_hot((row // 64 == col // 16) & (row % 16 == col % 16))
    tall = dot(repeat, pair_y_ref[...])
    back = tall * 0.125
    row, col = picks(256, LENGTH)
    for c in range(4):
        block = jnp.where((row // 16) % 4 == c, back, 0.0).astype(BF)
        inv_y_ref[:, c * 128 : c * 128 + 128] = block
    wide = tall.T
    row, col = picks(LENGTH, 256)
    for c in range(4):
        block = jnp.where((col // 16) % 4 == c, wide, 0.0).astype(BF)
        fwd_y_ref[c * 128 : c * 128 + 128, :] = block
    place = place_ref[0]
    xr, xi = one_x_ref[place // 2, 0:1, :], one_x_ref[place // 2, 1:2, :]
    yr = jnp.where(place % 2 == 0, one_y_ref[0, 0:1, :], one_y_ref[1, 0:1, :])
    yi = jnp.where(place % 2 == 0, one_y_ref[0, 1:2, :], one_y_ref[1, 1:2, :])
    pr, pi = xr * yr - xi * yi, xr * yi + xi * yr
    zr, zi = one_z_ref[0], one_z_ref[1]
    ones_ref[...] = jnp.concatenate([zr * pr - zi * pi, zr * pi + zi * pr], axis=0)


def fold_kernel(lift_ref, lift_bias_ref, weight_hbm, out_ref, later_hbm, weight, sem):
    copy, kept = fetch(
        [(weight_hbm.at[0], weight, sem.at[0]), (weight_hbm.at[1], later_hbm, sem.at[1])]
    )
    row, col = picks(HALF, 4)
    pick = one_hot((row % 8 == col))
    row, col = picks(HALF, HALF)
    lift = dot(pick, lift_ref[...]) + jnp.where(row % 8 == 4, lift_bias_ref[...].astype(F32), 0.0)
    row, col = picks(HALF, LENGTH)
    lift = dot(lift.astype(BF), one_hot(row == col // 4))
    lift = jnp.where(row // 8 == col % 4, lift, 0.0).astype(BF)
    copy.wait()
    for r in range(2):
        folded = dot(lift, weight[r]).astype(BF)
        for section in range(8):
            out_ref[section, r * HALF : r * HALF + HALF, :] = folded
    kept.wait()


def start_kernel(fields_hbm, pair_y_hbm, fwd_x_hbm, out_ref, fields, pair_y, fwd_x, rows, sem):
    copies = fetch(
        [
            (pair_y_hbm, pair_y, sem.at[0]),
            (fields_hbm.at[0], fields, sem.at[1]),
            (fwd_x_hbm, fwd_x, sem.at[2]),
        ]
    )
    copies[0].wait()
    row, col = picks(256, 64)
    repeat = one_hot((row // 64 == col // 16) & (row % 16 == col % 16))
    wide = dot(repeat, pair_y[...]).T
    row, col = picks(LENGTH, 256)
    fwd_y = jnp.concatenate(
        [jnp.where((col // 16) % 4 == c, wide, 0.0).astype(BF) for c in range(4)], axis=0
    )
    lane = lax.broadcasted_iota(jnp.int32, (64, LENGTH), 1)
    copies[1].wait()
    copies[2].wait()
    made = []
    for z in range(2):
        wide = jnp.concatenate([fields[c, z] for c in range(4)], axis=1)
        along = dot(wide, fwd_y).astype(BF)
        stacked = jnp.concatenate([along[:, :128], along[:, 128:]], axis=0)
        made.append(dot(fwd_x[...], stacked) * (1.0 / LENGTH))
    first = jnp.where(lane < 64, made[0], pltpu.roll(made[1], 64, 1))
    second = jnp.where(lane < 64, pltpu.roll(made[0], 64, 1), made[1])
    for h, value in enumerate((first, second)):
        for r in range(2):
            rows[pl.ds(h * 2 + r, 32, stride=4), :] = value[r * 32 : r * 32 + 32]
    out_ref[...] = rows[...].astype(BF)


def mix(weight_ref, modes, pattern):
    low = lax.broadcasted_iota(jnp.int32, (8, LENGTH), 0) < 4
    for pair in range(16):
        for r in range(2):
            for half in range(2):
                even = jnp.broadcast_to(modes[r, half, 2 * pair : 2 * pair + 1, :], (8, LENGTH))
                odd = jnp.broadcast_to(modes[r, half, 2 * pair + 1 : 2 * pair + 2, :], (8, LENGTH))
                pattern[pair, r, half] = jnp.where(low, even, odd)
    mixed = {}
    for g in range(4):
        total = {}
        for side in range(2):
            section = 2 * g + side
            acc = [[jnp.zeros((8, LENGTH), F32) for _ in range(2)] for _ in range(2)]
            for quad in range(8):
                real = weight_ref[section, 0, quad * 16 : quad * 16 + 16, :].astype(F32)
                imag = weight_ref[section, 1, quad * 16 : quad * 16 + 16, :].astype(F32)
                for sub in range(2):
                    pair = quad * 2 + sub
                    for half in range(2):
                        wr = real[sub * 8 : sub * 8 + 8, half * 128 : half * 128 + 128]
                        wi = imag[sub * 8 : sub * 8 + 8, half * 128 : half * 128 + 128]
                        mr, mi = pattern[pair, 0, half], pattern[pair, 1, half]
                        acc[0][half] = acc[0][half] + wr * mr - wi * mi
                        acc[1][half] = acc[1][half] + wr * mi + wi * mr
            for r in range(2):
                for half in range(2):
                    value = acc[r][half]
                    total[side, r, half] = value + pltpu.roll(value, 4, 0)
        for r in range(2):
            for half in range(2):
                mixed[g, r, half] = jnp.where(low, total[0, r, half], total[1, r, half])
    return mixed


def first_mix(folded_ref, modes):
    sub = lax.broadcasted_iota(jnp.int32, (8, LENGTH), 0)
    mixed = {}
    for g in range(4):
        for row in range(0, 8, 2):
            section, o = 2 * g + row // 4, row % 4
            real = folded_ref[section, o * 8 : o * 8 + 16, :].astype(F32)
            imag = folded_ref[section, HALF + o * 8 : HALF + o * 8 + 16, :].astype(F32)
            for more in range(2):
                for half in range(2):
                    wr = real[more * 8 : more * 8 + 8, half * 128 : half * 128 + 128]
                    wi = imag[more * 8 : more * 8 + 8, half * 128 : half * 128 + 128]
                    mr, mi = modes[0, half], modes[1, half]
                    for r, value in enumerate((wr * mr - wi * mi, wr * mi + wi * mr)):
                        for step in (4, 2, 1):
                            value = value + pltpu.roll(value, step, 0)
                        if row + more:
                            value = jnp.where(sub == row + more, value, mixed[g, r, half])
                        mixed[g, r, half] = value
    return mixed


def evaluate(mixed, turned, z_ref, out_ref):
    slot = lax.broadcasted_iota(jnp.int32, (8, LENGTH), 1) // K
    for py in range(K):
        half, at = py // 8, py % 8
        value = None
        for g in range(4):
            for r in range(2):
                where = 2 * g + r
                moved = mixed[g, r, half]
                if where != at:
                    moved = pltpu.roll(moved, (where - at) * K % LENGTH, 1)
                value = moved if value is None else jnp.where(slot == where, moved, value)
        turned[pl.ds(py, 8, stride=K), :] = value
    out_ref[...] = nt_dot(z_ref[:1024], turned[...].astype(BF)).astype(BF)


def unravel(turned, groups, modes):
    slot = lax.broadcasted_iota(jnp.int32, (8, LENGTH), 1) // K
    parts = [turned[pl.ds(py, 8, stride=K), :] for py in range(K)]
    for g in range(groups):
        for r in range(2):
            source = 2 * g + r
            for half in range(2):
                value = None
                for at in range(8):
                    moved = parts[half * 8 + at]
                    if at != source:
                        moved = pltpu.roll(moved, (at - source) * K % LENGTH, 1)
                    value = moved if value is None else jnp.where(slot == at, moved, value)
                modes[r, half, g * 8 : g * 8 + 8, :] = value


def dropped(place_ref, shape):
    row = lax.broadcasted_iota(jnp.int32, shape, 0)
    lane = lax.broadcasted_iota(jnp.int32, shape, 1)
    origin = jnp.logical_and(row % K == 0, lane % K == 0)
    return jnp.logical_and(origin, place_ref[0] == 0)


def first_mix_kernel(
    place_ref, got_ref, folded_ref, ones_ref, z_ref, out_ref, turned, modes
):
    both = dot(z_ref[2048:], got_ref[...])
    lane = lax.broadcasted_iota(jnp.int32, (HALF, LENGTH), 1)
    value = both[:HALF] + pltpu.roll(both[HALF:], 64, 1)
    value = jnp.where(lane < 64, value, 0.0) * (1.0 / math.sqrt(LENGTH))
    value = jnp.where(lane // K == 4, ones_ref[...], value)
    value = jnp.where(dropped(place_ref, value.shape), 0.0, value)
    value = jnp.concatenate([value, jnp.zeros((LENGTH - HALF, LENGTH), F32)], axis=0)
    turned[...] = value.T
    unravel(turned, 1, modes)
    evaluate(first_mix(folded_ref, modes), turned, z_ref, out_ref)


def mix_kernel(
    place_ref, got_ref, z_ref, weight_hbm, out_ref, weight, turned, modes, pattern, sem
):
    (copy,) = fetch([(weight_hbm, weight, sem.at[0])])
    value = None
    for block in range(8):
        span = slice(block * 128, block * 128 + 128)
        part = dot(z_ref[1024 + block * 128 : 1152 + block * 128], got_ref[span])
        value = part if value is None else value + part
    value = value * (1.0 / math.sqrt(LENGTH))
    value = jnp.where(dropped(place_ref, value.shape), 0.0, value)
    turned[...] = value.T
    unravel(turned, 4, modes)
    copy.wait()
    evaluate(mix(weight, modes, pattern), turned, z_ref, out_ref)


def swapped(first, second):
    low = lax.broadcasted_iota(jnp.int32, first.shape, 1) < 64
    return (
        jnp.where(low, first, pltpu.roll(second, 64, 1)),
        jnp.where(low, pltpu.roll(first, 64, 1), second),
    )


def inverse(got_ref, x_ref, inv_y_ref, rows, field):
    rows[...] = got_ref[...].astype(F32)

    def step(index, carry):
        g, z = index // 2, index % 2
        parts = []
        for h in range(2):
            pieces = [rows[pl.ds(h * 16 + g * 4 + r * 2 + z, 32, stride=32), :] for r in range(2)]
            parts.append(jnp.concatenate(pieces, axis=0))
        parts = jnp.concatenate(swapped(*parts), axis=1).astype(BF)
        along = dot(x_ref[64:, :64], parts).astype(BF)
        for quad in range(2):
            lanes = slice(quad * 128, quad * 128 + 128)
            wide = jnp.concatenate([along[:128, lanes], along[128:, lanes]], axis=1)
            made = dot(wide, inv_y_ref[...])
            for o in range(4):
                field[g * 8 + quad * 4 + o, z] = made[:, o * 128 : o * 128 + 128]
        return carry

    lax.fori_loop(0, 8, step, 0, unroll=UNROLL_A)


def activate(value):
    inner = value * (0.7978845608028654 + 0.035677408136300125 * value * value)
    half = 0.5 * value
    return half + half * jnp.tanh(inner)


def pointwise(span, hidden, map_ref, bias, field):
    bypassed = dot(map_ref[...], hidden)
    made = []
    for z in range(2):
        part = field[:, z, span, :].reshape(512, LENGTH)
        value = bypassed[:, z * 128 : z * 128 + 128] + bias + part
        made.append(activate(value).astype(BF))
    return made


def middle_kernel(
    got_ref, kc_ref, bias_ref, inv_y_ref, fwd_y_ref, x_ref, fields_hbm, hidden_hbm, out_ref,
    fields, rows, field, hidden, sem,
):
    (copy,) = fetch([(fields_hbm.at[0], fields, sem.at[0])])
    inverse(got_ref, x_ref, inv_y_ref, rows, field)
    copy.wait()
    def apply(block, carry):
        span = pl.ds(pl.multiple_of(block * 16, 16), 16)
        raw = [fields[:, z, span, :].reshape(64, LENGTH) for z in range(2)]
        raw = jnp.concatenate(raw, axis=1)
        made = pointwise(span, jnp.concatenate([raw, raw], axis=0), kc_ref, bias_ref[0], field)
        for z in range(2):
            hidden[:, z, span, :] = made[z].reshape(32, 16, LENGTH)
        return carry

    lax.fori_loop(0, 8, apply, 0, unroll=UNROLL_B)
    (kept,) = fetch([(hidden, hidden_hbm, sem.at[1])])
    def forward(index, carry):
        g, z = index // 2, index % 2
        stacked = []
        for quad in range(2):
            wide = jnp.concatenate([hidden[g * 8 + quad * 4 + c, z] for c in range(4)], axis=1)
            along = dot(wide, fwd_y_ref[...]).astype(BF)
            stacked.append(jnp.concatenate([along[:, :128], along[:, 128:]], axis=0))
        spectrum = dot(x_ref[:64], jnp.concatenate(stacked, axis=1)) * (1.0 / LENGTH)
        for h, value in enumerate(swapped(spectrum[:, :128], spectrum[:, 128:])):
            for r in range(2):
                at = h * 16 + g * 4 + r * 2 + z
                rows[pl.ds(at, 32, stride=32), :] = value[r * 32 : r * 32 + 32]
        return carry

    lax.fori_loop(0, 8, forward, 0, unroll=UNROLL_A)
    out_ref[...] = rows[...].astype(BF)
    kept.wait()


def last_kernel(
    got_ref, kb_ref, bias_ref, inv_y_ref, x_ref, hidden_hbm, out_hbm, hidden, rows, field, made_ref,
    sem,
):
    (copy,) = fetch([(hidden_hbm, hidden, sem.at[0])])
    inverse(got_ref, x_ref, inv_y_ref, rows, field)
    copy.wait()

    def keep(block):
        span = pl.ds(pl.multiple_of(block * 16, 16), 16)
        source, target = made_ref.at[:, :, span, :], out_hbm.at[0, :, :, span, :]
        return pltpu.make_async_copy(source, target, sem.at[1 + block])

    def apply(block, carry):
        span = pl.ds(pl.multiple_of(block * 16, 16), 16)
        raw = [hidden[:, z, span, :].reshape(512, LENGTH) for z in range(2)]
        made = pointwise(span, jnp.concatenate(raw, axis=1), kb_ref, bias_ref[1], field)
        for z in range(2):
            made_ref[:, z, span, :] = made[z].reshape(32, 16, LENGTH)
        keep(block).start()
        return carry

    lax.fori_loop(0, 8, apply, 0, unroll=UNROLL_B)
    for block in range(8):
        keep(block).wait()


def call(kernel, name, inputs, outputs, scratch, sems=0, limit=24):
    spaces = {"s": pltpu.SMEM, "v": pltpu.VMEM, "p": pltpu.VMEM, "h": pltpu.HBM, "f": pltpu.HBM}
    fetched = [index for index, letter in enumerate(inputs) if letter == "f"]

    def run(*arrays):
        buffers = [pltpu.VMEM(arrays[index].shape, arrays[index].dtype) for index in fetched]
        own = [pltpu.VMEM(shape, kind) for shape, kind in scratch]
        if sems:
            own.append(pltpu.SemaphoreType.DMA((sems,)))
        if fetched:
            buffers.append(pltpu.SemaphoreType.DMA((len(fetched),)))

        def body(*refs):
            refs = list(refs)
            if fetched:
                first = len(inputs) + len(outputs) + len(own)
                copies = []
                for order, index in enumerate(fetched):
                    copies.append((refs[index], refs[first + order], refs[-1].at[order]))
                    refs[index] = refs[first + order]
                for copy in fetch(copies):
                    copy.wait()
                refs = refs[:first]
            kernel(*refs)

        placed = []
        for letter, array in zip(inputs, arrays):
            if letter in "hfp":
                array = pltpu.with_memory_space_constraint(array, spaces[letter])
            placed.append(array)
        return pl.pallas_call(
            body,
            name=name,
            out_shape=[spaces[letter](shape, kind) for letter, shape, kind in outputs],
            in_specs=[pl.BlockSpec(memory_space=spaces[letter]) for letter in inputs],
            out_specs=[pl.BlockSpec(memory_space=spaces[letter]) for letter, _, _ in outputs],
            scratch_shapes=own + buffers,
            compiler_params=pltpu.CompilerParams(vmem_limit_bytes=limit << 20),
        )(*placed)

    return run


def exchange(value, axis="slab"):
    return lax.all_to_all(value, axis, split_axis=0, concat_axis=0, tiled=True)


tie = lax.optimization_barrier


def solution(mesh):
    table, one_x, one_z = make_tables()
    const = {name: value.astype(ml_dtypes.bfloat16) for name, value in table.items()}
    ones_x = np.repeat(split(one_x).T[:, :, None], LENGTH, axis=2)
    ones_y = np.tile(split(one_x).reshape(2, 2, 1, K), (1, 1, 8, 1)).reshape(2, 2, LENGTH)
    ones_y = ones_y.transpose(1, 0, 2)
    ones_z = np.repeat(split(one_z)[:, :, None], LENGTH, axis=2)

    def on_device(fields, lift_weight, lift_bias, spectral_weight, bypass_weight, bypass_bias):
        place = lax.axis_index("slab").reshape(1)
        lift_bias = lift_bias[None]
        packed, cube = (1024, LENGTH), (32, 2, 128, 128)
        (spectrum,) = call(
            start_kernel,
            "start",
            "hhh",
            [("v", (128, LENGTH), BF)],
            [((4, 2, 128, 128), BF), ((64, 128), BF), ((64, 256), BF), ((128, 128), F32)],
            sems=3,
        )(fields, const["pair_y"], const["fwd_x"])
        spectrum, spectral_weight = tie((spectrum, spectral_weight))
        spectrum = exchange(spectrum)
        weight = spectral_weight.reshape(2, 2, LENGTH, 256)
        folded, later = call(
            fold_kernel,
            "fold",
            "ffh",
            [("v", (8, 64, 256), BF), ("h", (2, LENGTH, 256), BF)],
            [((2, 128, 256), BF)],
            sems=2,
        )(lift_weight, lift_bias, weight)
        folded, bypass_weight, later, _ = tie((folded, bypass_weight, later, spectrum))
        gathered = lax.all_gather(later, "section", axis=0)
        folded = exchange(folded.reshape(512, 256), "section").reshape(8, 64, 256)
        kb, kc, bias, fwd_y, inv_y, ones, z_table, x_table = call(
            spread_kernel,
            "spread",
            "s" + "f" * 10,
            [
                ("v", (512, 512), BF),
                ("v", (512, 128), BF),
                ("v", (2, 512, LENGTH), F32),
                ("v", (512, 256), BF),
                ("v", (256, 512), BF),
                ("v", (HALF, LENGTH), F32),
                ("v", (2112, 128), BF),
                ("v", (320, 256), BF),
            ],
            [],
        )(
            place, ones_x, bypass_weight, lift_weight, bypass_bias, lift_bias, const["pair_y"],
            ones_y, ones_z, const["z"], const["x"],
        )
        (planes,) = call(
            first_mix_kernel,
            "mix0",
            "spppp",
            [("v", packed, BF)],
            [((128, 128), F32), ((2, 2, 8, 128), F32)],
        )(place, spectrum, folded, ones, z_table)
        hidden, spectrum = call(
            middle_kernel,
            "middle",
            "pppppph",
            [("h", cube, BF), ("v", packed, BF)],
            [((4, 2, 128, 128), BF), (packed, F32), (cube, F32), (cube, BF)],
            sems=2,
        )(exchange(planes), kc, bias, inv_y, fwd_y, x_table, fields)
        (planes,) = call(
            mix_kernel,
            "mix1",
            "spph",
            [("v", packed, BF)],
            [
                ((8, 2, 128, 256), BF), ((128, 128), F32), ((2, 2, 32, 128), F32),
                ((16, 2, 2, 8, 128), F32),
            ],
            sems=1,
        )(place, exchange(spectrum), z_table, gathered)
        (features,) = call(
            last_kernel,
            "last",
            "ppppph",
            [("h", (1,) + cube, BF)],
            [(cube, BF), (packed, F32), (cube, F32), (cube, BF)],
            sems=9,
        )(exchange(planes), kb, bias, inv_y, x_table, hidden)
        return features

    placed = (
        P("section", None, "slab", None, None),
        P(),
        P(),
        P(None, None, None, "section", "slab"),
        P(),
        P(),
    )
    return jax.shard_map(
        on_device,
        mesh=mesh,
        in_specs=placed,
        out_specs=P("section", None, "slab", None, None),
        check_vma=False,
    )
```

```python
import math

import jax
import jax.numpy as jnp
import ml_dtypes
import numpy as np
from jax import lax
from jax.experimental import pallas as pl
from jax.experimental.pallas import tpu as pltpu
from jax.sharding import PartitionSpec as P

K = 16
HALF = 2 * K
LENGTH = 128
SLABS = 64
UNROLL_A = 4
UNROLL_B = 8
BF = jnp.bfloat16
F32 = jnp.float32


def wave(freqs):
    where = np.arange(LENGTH, dtype=np.int64)[None, :]
    step = (freqs % LENGTH)[:, None] * where % LENGTH
    phase = step.astype(np.float32) * np.float32(2.0 * math.pi / LENGTH)
    cosine = np.cos(phase).astype(ml_dtypes.bfloat16).astype(np.float32)
    sine = np.sin(phase).astype(ml_dtypes.bfloat16).astype(np.float32)
    return cosine, sine


def make_tables():
    base = np.arange(HALF)
    signed = np.where(base < K, base, base - HALF)
    cos, sin = wave(signed)
    cos_z, sin_z = wave(np.arange(K))
    double = np.where(np.arange(K) == 0, 1.0, 2.0)[:, None]
    table = {}
    table["pair_y"] = np.concatenate([cos, -sin], 0)
    table["fwd_x"] = np.concatenate(
        [np.concatenate([cos, sin], 1), np.concatenate([-sin, cos], 1)], 0
    )
    fwd_z = np.stack([np.stack([cos_z, sin_z], 1), np.stack([-sin_z, cos_z], 1)], 0)
    fwd_z = fwd_z.reshape(2, K, 2, SLABS, 2)
    full = np.einsum("gf,akrsz->gaksfrz", np.eye(4), fwd_z)
    full = full.reshape(4 * HALF, 8, LENGTH).transpose(1, 0, 2).reshape(1024, LENGTH)
    first = np.einsum("akrsz->zaksr", fwd_z).reshape(2 * HALF, SLABS * 2)
    cz, sz = cos_z * double * 0.25, sin_z * double * 0.25
    inv_z = np.stack([np.stack([cz, -sz], 0), np.stack([sz, cz], 0)], 0)
    inv_z = inv_z.reshape(2, 2, K, SLABS, 2)
    back = np.einsum("gf,arksz->sgazfrk", np.eye(4), inv_z).reshape(SLABS * 16, 4 * HALF)
    table["z"] = np.concatenate([back, full, first], 0)
    inv_x = np.stack([np.stack([cos, -sin], 0), np.stack([sin, cos], 0)], 0)
    table["inv_x"] = np.einsum("arpx->axrp", inv_x).reshape(2 * LENGTH, 2 * HALF) * 0.125
    table["x"] = np.concatenate([table["fwd_x"], np.pad(table.pop("inv_x"), ((0, 0), (0, 192)))], 0)
    one_x = (cos.sum(1) - 1j * sin.sum(1)) / math.sqrt(LENGTH)
    one_z = (cos_z.sum(1) - 1j * sin_z.sum(1)) / math.sqrt(LENGTH)
    return table, one_x, one_z


def split(value):
    return np.stack([value.real, value.imag], 0).astype(np.float32)


def dot(left, right):
    return jnp.dot(left, right, preferred_element_type=F32)


def nt_dot(left, right):
    return lax.dot_general(left, right, (((1,), (1,)), ((), ())), preferred_element_type=F32)


def picks(rows, cols):
    row = lax.broadcasted_iota(jnp.int32, (rows, cols), 0)
    col = lax.broadcasted_iota(jnp.int32, (rows, cols), 1)
    return row, col


def one_hot(mask):
    return jnp.where(mask, 1.0, 0.0).astype(BF)


def fetch(copies):
    started = [pltpu.make_async_copy(source, target, sem) for source, target, sem in copies]
    for copy in started:
        copy.start()
    return started


def spread_kernel(
    place_ref, one_x_ref, bypass_ref, lift_ref, bypass_bias_ref, lift_bias_ref, pair_y_ref,
    one_y_ref, one_z_ref, z_ref, x_ref, kb_ref, kc_ref, bias_ref, fwd_y_ref, inv_y_ref, ones_ref,
    z_out, x_out,
):
    z_out[...] = z_ref[...]
    x_out[...] = x_ref[...]
    row, col = picks(512, 32)
    expand = one_hot(row // 16 == col)
    row, col = picks(512, 512)
    tall = nt_dot(expand, bypass_ref[1]).astype(BF)
    kb_ref[...] = jnp.where((row % 16) == (col % 16), nt_dot(tall, expand), 0.0).astype(BF)
    joint = dot(lift_ref[...], bypass_ref[0])
    high = joint.astype(BF)
    low = (joint - high.astype(F32)).astype(BF)
    row, col = picks(64, 4)
    expand4 = one_hot(row // 16 == col)
    row, col = picks(512, 64)
    for index, part in enumerate((high, low)):
        wide = nt_dot(nt_dot(expand, part).astype(BF), expand4)
        wide = jnp.where((row % 16) == (col % 16), wide, 0.0).astype(BF)
        kc_ref[:, index * 64 : index * 64 + 64] = wide
    filled = jnp.ones((32, LENGTH), BF)
    row, col = picks(32, 32)
    eye = jnp.where(row == col, 1.0, 0.0)

    def column(vector):
        return dot((eye * vector.astype(F32)).astype(BF), filled)

    shift = column(bypass_bias_ref[0:1]) + lax.dot_general(
        bypass_ref[0], column(lift_bias_ref[...]).astype(BF), (((0,), (0,)), ((), ())),
        preferred_element_type=F32,
    )
    for index, value in enumerate((shift, column(bypass_bias_ref[1:2]))):
        bias_ref[index] = jnp.dot(
            expand.astype(F32), value, precision=lax.Precision.HIGHEST, preferred_element_type=F32
        )
    row, col = picks(256, 64)
    repeat = one_hot((row // 64 == col // 16) & (row % 16 == col % 16))
    tall = dot(repeat, pair_y_ref[...])
    back = tall * 0.125
    row, col = picks(256, LENGTH)
    for c in range(4):
        block = jnp.where((row // 16) % 4 == c, back, 0.0).astype(BF)
        inv_y_ref[:, c * 128 : c * 128 + 128] = block
    wide = tall.T
    row, col = picks(LENGTH, 256)
    for c in range(4):
        block = jnp.where((col // 16) % 4 == c, wide, 0.0).astype(BF)
        fwd_y_ref[c * 128 : c * 128 + 128, :] = block
    place = place_ref[0]
    xr, xi = one_x_ref[place // 2, 0:1, :], one_x_ref[place // 2, 1:2, :]
    yr = jnp.where(place % 2 == 0, one_y_ref[0, 0:1, :], one_y_ref[1, 0:1, :])
    yi = jnp.where(place % 2 == 0, one_y_ref[0, 1:2, :], one_y_ref[1, 1:2, :])
    pr, pi = xr * yr - xi * yi, xr * yi + xi * yr
    zr, zi = one_z_ref[0], one_z_ref[1]
    ones_ref[...] = jnp.concatenate([zr * pr - zi * pi, zr * pi + zi * pr], axis=0)


def fold_kernel(lift_ref, lift_bias_ref, weight_hbm, out_ref, later_hbm, weight, later, sem):
    copy, passed = fetch([(weight_hbm.at[0], weight, sem.at[0]), (weight_hbm.at[1], later, sem.at[1])])
    row, col = picks(HALF, 4)
    pick = one_hot((row % 8 == col))
    row, col = picks(HALF, HALF)
    lift = dot(pick, lift_ref[...]) + jnp.where(row % 8 == 4, lift_bias_ref[...].astype(F32), 0.0)
    row, col = picks(HALF, LENGTH)
    lift = dot(lift.astype(BF), one_hot(row == col // 4))
    lift = jnp.where(row // 8 == col % 4, lift, 0.0).astype(BF)
    passed.wait()
    (kept,) = fetch([(later, later_hbm, sem.at[2])])
    copy.wait()
    for r in range(2):
        folded = dot(lift, weight[r]).astype(BF)
        for section in range(8):
            out_ref[section, r * HALF : r * HALF + HALF, :] = folded
    kept.wait()


def start_kernel(fields_hbm, pair_y_hbm, fwd_x_hbm, out_ref, fields, pair_y, fwd_x, rows, sem):
    copies = fetch(
        [
            (pair_y_hbm, pair_y, sem.at[0]),
            (fields_hbm.at[0], fields, sem.at[1]),
            (fwd_x_hbm, fwd_x, sem.at[2]),
        ]
    )
    copies[0].wait()
    row, col = picks(256, 64)
    repeat = one_hot((row // 64 == col // 16) & (row % 16 == col % 16))
    wide = dot(repeat, pair_y[...]).T
    row, col = picks(LENGTH, 256)
    fwd_y = jnp.concatenate(
        [jnp.where((col // 16) % 4 == c, wide, 0.0).astype(BF) for c in range(4)], axis=0
    )
    lane = lax.broadcasted_iota(jnp.int32, (64, LENGTH), 1)
    copies[1].wait()
    copies[2].wait()
    made = []
    for z in range(2):
        wide = jnp.concatenate([fields[c, z] for c in range(4)], axis=1)
        along = dot(wide, fwd_y).astype(BF)
        stacked = jnp.concatenate([along[:, :128], along[:, 128:]], axis=0)
        made.append(dot(fwd_x[...], stacked) * (1.0 / LENGTH))
    first = jnp.where(lane < 64, made[0], pltpu.roll(made[1], 64, 1))
    second = jnp.where(lane < 64, pltpu.roll(made[0], 64, 1), made[1])
    for h, value in enumerate((first, second)):
        for r in range(2):
            rows[pl.ds(h * 2 + r, 32, stride=4), :] = value[r * 32 : r * 32 + 32]
    out_ref[...] = rows[...].astype(BF)


def mix(weight_ref, modes, pattern, copies):
    low = lax.broadcasted_iota(jnp.int32, (8, LENGTH), 0) < 4
    for pair in range(16):
        for r in range(2):
            for half in range(2):
                even = jnp.broadcast_to(modes[r, half, 2 * pair : 2 * pair + 1, :], (8, LENGTH))
                odd = jnp.broadcast_to(modes[r, half, 2 * pair + 1 : 2 * pair + 2, :], (8, LENGTH))
                pattern[pair, r, half] = jnp.where(low, even, odd)
    mixed = {}
    for g in range(4):
        copies[g].wait()
        total = {}
        for side in range(2):
            section = 2 * g + side
            acc = [[jnp.zeros((8, LENGTH), F32) for _ in range(2)] for _ in range(2)]
            for quad in range(8):
                real = weight_ref[section, 0, quad * 16 : quad * 16 + 16, :].astype(F32)
                imag = weight_ref[section, 1, quad * 16 : quad * 16 + 16, :].astype(F32)
                for sub in range(2):
                    pair = quad * 2 + sub
                    for half in range(2):
                        wr = real[sub * 8 : sub * 8 + 8, half * 128 : half * 128 + 128]
                        wi = imag[sub * 8 : sub * 8 + 8, half * 128 : half * 128 + 128]
                        mr, mi = pattern[pair, 0, half], pattern[pair, 1, half]
                        acc[0][half] = acc[0][half] + wr * mr - wi * mi
                        acc[1][half] = acc[1][half] + wr * mi + wi * mr
            for r in range(2):
                for half in range(2):
                    value = acc[r][half]
                    total[side, r, half] = value + pltpu.roll(value, 4, 0)
        for r in range(2):
            for half in range(2):
                mixed[g, r, half] = jnp.where(low, total[0, r, half], total[1, r, half])
    return mixed


def first_mix(folded_ref, modes):
    sub = lax.broadcasted_iota(jnp.int32, (8, LENGTH), 0)
    mixed = {}
    for g in range(4):
        for row in range(0, 8, 2):
            section, o = 2 * g + row // 4, row % 4
            real = folded_ref[section, o * 8 : o * 8 + 16, :].astype(F32)
            imag = folded_ref[section, HALF + o * 8 : HALF + o * 8 + 16, :].astype(F32)
            for more in range(2):
                for half in range(2):
                    wr = real[more * 8 : more * 8 + 8, half * 128 : half * 128 + 128]
                    wi = imag[more * 8 : more * 8 + 8, half * 128 : half * 128 + 128]
                    mr, mi = modes[0, half], modes[1, half]
                    for r, value in enumerate((wr * mr - wi * mi, wr * mi + wi * mr)):
                        for step in (4, 2, 1):
                            value = value + pltpu.roll(value, step, 0)
                        if row + more:
                            value = jnp.where(sub == row + more, value, mixed[g, r, half])
                        mixed[g, r, half] = value
    return mixed


def evaluate(mixed, turned, z_ref, out_ref):
    slot = lax.broadcasted_iota(jnp.int32, (8, LENGTH), 1) // K
    for py in range(K):
        half, at = py // 8, py % 8
        value = None
        for g in range(4):
            for r in range(2):
                where = 2 * g + r
                moved = mixed[g, r, half]
                if where != at:
                    moved = pltpu.roll(moved, (where - at) * K % LENGTH, 1)
                value = moved if value is None else jnp.where(slot == where, moved, value)
        turned[pl.ds(py, 8, stride=K), :] = value
    out_ref[...] = nt_dot(z_ref[:1024], turned[...].astype(BF)).astype(BF)


def unravel(turned, groups, modes):
    slot = lax.broadcasted_iota(jnp.int32, (8, LENGTH), 1) // K
    parts = [turned[pl.ds(py, 8, stride=K), :] for py in range(K)]
    for g in range(groups):
        for r in range(2):
            source = 2 * g + r
            for half in range(2):
                value = None
                for at in range(8):
                    moved = parts[half * 8 + at]
                    if at != source:
                        moved = pltpu.roll(moved, (at - source) * K % LENGTH, 1)
                    value = moved if value is None else jnp.where(slot == at, moved, value)
                modes[r, half, g * 8 : g * 8 + 8, :] = value


def dropped(place_ref, shape):
    row = lax.broadcasted_iota(jnp.int32, shape, 0)
    lane = lax.broadcasted_iota(jnp.int32, shape, 1)
    origin = jnp.logical_and(row % K == 0, lane % K == 0)
    return jnp.logical_and(origin, place_ref[0] == 0)


def first_mix_kernel(
    place_ref, got_ref, folded_ref, ones_ref, z_ref, out_ref, turned, modes
):
    both = dot(z_ref[2048:], got_ref[...])
    lane = lax.broadcasted_iota(jnp.int32, (HALF, LENGTH), 1)
    value = both[:HALF] + pltpu.roll(both[HALF:], 64, 1)
    value = jnp.where(lane < 64, value, 0.0) * (1.0 / math.sqrt(LENGTH))
    value = jnp.where(lane // K == 4, ones_ref[...], value)
    value = jnp.where(dropped(place_ref, value.shape), 0.0, value)
    value = jnp.concatenate([value, jnp.zeros((LENGTH - HALF, LENGTH), F32)], axis=0)
    turned[...] = value.T
    unravel(turned, 1, modes)
    evaluate(first_mix(folded_ref, modes), turned, z_ref, out_ref)


def mix_kernel(
    place_ref, got_ref, z_ref, weight_hbm, out_ref, weight, turned, modes, pattern, sem
):
    copies = fetch([(weight_hbm.at[pl.ds(2 * g, 2)], weight.at[pl.ds(2 * g, 2)], sem.at[g]) for g in range(4)])
    value = None
    for block in range(8):
        span = slice(block * 128, block * 128 + 128)
        part = dot(z_ref[1024 + block * 128 : 1152 + block * 128], got_ref[span])
        value = part if value is None else value + part
    value = value * (1.0 / math.sqrt(LENGTH))
    value = jnp.where(dropped(place_ref, value.shape), 0.0, value)
    turned[...] = value.T
    unravel(turned, 4, modes)
    evaluate(mix(weight, modes, pattern, copies), turned, z_ref, out_ref)


def swapped(first, second):
    low = lax.broadcasted_iota(jnp.int32, first.shape, 1) < 64
    return (
        jnp.where(low, first, pltpu.roll(second, 64, 1)),
        jnp.where(low, pltpu.roll(first, 64, 1), second),
    )


def inverse(got_ref, x_ref, inv_y_ref, rows, field):
    rows[...] = got_ref[...].astype(F32)

    def step(index, carry):
        g, z = index // 2, index % 2
        parts = []
        for h in range(2):
            pieces = [rows[pl.ds(h * 16 + g * 4 + r * 2 + z, 32, stride=32), :] for r in range(2)]
            parts.append(jnp.concatenate(pieces, axis=0))
        parts = jnp.concatenate(swapped(*parts), axis=1).astype(BF)
        along = dot(x_ref[64:, :64], parts).astype(BF)
        for quad in range(2):
            lanes = slice(quad * 128, quad * 128 + 128)
            wide = jnp.concatenate([along[:128, lanes], along[128:, lanes]], axis=1)
            made = dot(wide, inv_y_ref[...])
            for o in range(4):
                field[g * 8 + quad * 4 + o, z] = made[:, o * 128 : o * 128 + 128]
        return carry

    lax.fori_loop(0, 8, step, 0, unroll=UNROLL_A)


def activate(value):
    inner = value * (0.7978845608028654 + 0.035677408136300125 * value * value)
    half = 0.5 * value
    return half + half * jnp.tanh(inner)


def pointwise(span, hidden, map_ref, bias, field):
    bypassed = dot(map_ref[...], hidden)
    made = []
    for z in range(2):
        part = field[:, z, span, :].reshape(512, LENGTH)
        value = bypassed[:, z * 128 : z * 128 + 128] + bias + part
        made.append(activate(value).astype(BF))
    return made


def middle_kernel(
    got_ref, kc_ref, bias_ref, inv_y_ref, fwd_y_ref, x_ref, fields_hbm, hidden_hbm, out_ref,
    fields, rows, field, hidden, sem,
):
    (copy,) = fetch([(fields_hbm.at[0], fields, sem.at[0])])
    inverse(got_ref, x_ref, inv_y_ref, rows, field)
    copy.wait()
    def apply(block, carry):
        span = pl.ds(pl.multiple_of(block * 16, 16), 16)
        raw = [fields[:, z, span, :].reshape(64, LENGTH) for z in range(2)]
        raw = jnp.concatenate(raw, axis=1)
        made = pointwise(span, jnp.concatenate([raw, raw], axis=0), kc_ref, bias_ref[0], field)
        for z in range(2):
            hidden[:, z, span, :] = made[z].reshape(32, 16, LENGTH)
        return carry

    lax.fori_loop(0, 8, apply, 0, unroll=UNROLL_B)
    (kept,) = fetch([(hidden, hidden_hbm, sem.at[1])])
    def forward(index, carry):
        g, z = index // 2, index % 2
        stacked = []
        for quad in range(2):
            wide = jnp.concatenate([hidden[g * 8 + quad * 4 + c, z] for c in range(4)], axis=1)
            along = dot(wide, fwd_y_ref[...]).astype(BF)
            stacked.append(jnp.concatenate([along[:, :128], along[:, 128:]], axis=0))
        spectrum = dot(x_ref[:64], jnp.concatenate(stacked, axis=1)) * (1.0 / LENGTH)
        for h, value in enumerate(swapped(spectrum[:, :128], spectrum[:, 128:])):
            for r in range(2):
                at = h * 16 + g * 4 + r * 2 + z
                rows[pl.ds(at, 32, stride=32), :] = value[r * 32 : r * 32 + 32]
        return carry

    lax.fori_loop(0, 8, forward, 0, unroll=UNROLL_A)
    out_ref[...] = rows[...].astype(BF)
    kept.wait()


def last_kernel(
    got_ref, kb_ref, bias_ref, inv_y_ref, x_ref, hidden_hbm, out_hbm, hidden, rows, field, made_ref,
    sem,
):
    (copy,) = fetch([(hidden_hbm, hidden, sem.at[0])])
    inverse(got_ref, x_ref, inv_y_ref, rows, field)
    copy.wait()

    def keep(block):
        span = pl.ds(pl.multiple_of(block * 16, 16), 16)
        source, target = made_ref.at[:, :, span, :], out_hbm.at[0, :, :, span, :]
        return pltpu.make_async_copy(source, target, sem.at[1 + block])

    def apply(block, carry):
        span = pl.ds(pl.multiple_of(block * 16, 16), 16)
        raw = [hidden[:, z, span, :].reshape(512, LENGTH) for z in range(2)]
        made = pointwise(span, jnp.concatenate(raw, axis=1), kb_ref, bias_ref[1], field)
        for z in range(2):
            made_ref[:, z, span, :] = made[z].reshape(32, 16, LENGTH)
        keep(block).start()
        return carry

    lax.fori_loop(0, 8, apply, 0, unroll=UNROLL_B)
    for block in range(8):
        keep(block).wait()


def call(kernel, name, inputs, outputs, scratch, sems=0, limit=24):
    spaces = {"s": pltpu.SMEM, "v": pltpu.VMEM, "p": pltpu.VMEM, "h": pltpu.HBM, "f": pltpu.HBM}
    fetched = [index for index, letter in enumerate(inputs) if letter == "f"]

    def run(*arrays):
        buffers = [pltpu.VMEM(arrays[index].shape, arrays[index].dtype) for index in fetched]
        own = [pltpu.VMEM(shape, kind) for shape, kind in scratch]
        if sems:
            own.append(pltpu.SemaphoreType.DMA((sems,)))
        if fetched:
            buffers.append(pltpu.SemaphoreType.DMA((len(fetched),)))

        def body(*refs):
            refs = list(refs)
            if fetched:
                first = len(inputs) + len(outputs) + len(own)
                copies = []
                for order, index in enumerate(fetched):
                    copies.append((refs[index], refs[first + order], refs[-1].at[order]))
                    refs[index] = refs[first + order]
                for copy in fetch(copies):
                    copy.wait()
                refs = refs[:first]
            kernel(*refs)

        placed = []
        for letter, array in zip(inputs, arrays):
            if letter in "hfp":
                array = pltpu.with_memory_space_constraint(array, spaces[letter])
            placed.append(array)
        return pl.pallas_call(
            body,
            name=name,
            out_shape=[spaces[letter](shape, kind) for letter, shape, kind in outputs],
            in_specs=[pl.BlockSpec(memory_space=spaces[letter]) for letter in inputs],
            out_specs=[pl.BlockSpec(memory_space=spaces[letter]) for letter, _, _ in outputs],
            scratch_shapes=own + buffers,
            compiler_params=pltpu.CompilerParams(vmem_limit_bytes=limit << 20),
        )(*placed)

    return run


def exchange(value, axis="slab"):
    return lax.all_to_all(value, axis, split_axis=0, concat_axis=0, tiled=True)


tie = lax.optimization_barrier


def solution(mesh):
    table, one_x, one_z = make_tables()
    const = {name: value.astype(ml_dtypes.bfloat16) for name, value in table.items()}
    ones_x = np.repeat(split(one_x).T[:, :, None], LENGTH, axis=2)
    ones_y = np.tile(split(one_x).reshape(2, 2, 1, K), (1, 1, 8, 1)).reshape(2, 2, LENGTH)
    ones_y = ones_y.transpose(1, 0, 2)
    ones_z = np.repeat(split(one_z)[:, :, None], LENGTH, axis=2)

    def on_device(fields, lift_weight, lift_bias, spectral_weight, bypass_weight, bypass_bias):
        place = lax.axis_index("slab").reshape(1)
        lift_bias = lift_bias[None]
        packed, cube = (1024, LENGTH), (32, 2, 128, 128)
        (spectrum,) = call(
            start_kernel,
            "start",
            "hhh",
            [("v", (128, LENGTH), BF)],
            [((4, 2, 128, 128), BF), ((64, 128), BF), ((64, 256), BF), ((128, 128), F32)],
            sems=3,
        )(fields, const["pair_y"], const["fwd_x"])
        spectrum, spectral_weight = tie((spectrum, spectral_weight))
        spectrum = exchange(spectrum)
        weight = spectral_weight.reshape(2, 2, LENGTH, 256)
        folded, later = call(
            fold_kernel,
            "fold",
            "ffh",
            [("v", (8, 64, 256), BF), ("h", (2, LENGTH, 256), BF)],
            [((2, 128, 256), BF), ((2, 128, 256), BF)],
            sems=3,
        )(lift_weight, lift_bias, weight)
        folded, bypass_weight, later, _ = tie((folded, bypass_weight, later, spectrum))
        gathered = lax.all_gather(later, "section", axis=0)
        folded = exchange(folded.reshape(512, 256), "section").reshape(8, 64, 256)
        kb, kc, bias, fwd_y, inv_y, ones, z_table, x_table = call(
            spread_kernel,
            "spread",
            "s" + "f" * 10,
            [
                ("v", (512, 512), BF),
                ("v", (512, 128), BF),
                ("v", (2, 512, LENGTH), F32),
                ("v", (512, 256), BF),
                ("v", (256, 512), BF),
                ("v", (HALF, LENGTH), F32),
                ("v", (2112, 128), BF),
                ("v", (320, 256), BF),
            ],
            [],
        )(
            place, ones_x, bypass_weight, lift_weight, bypass_bias, lift_bias, const["pair_y"],
            ones_y, ones_z, const["z"], const["x"],
        )
        (planes,) = call(
            first_mix_kernel,
            "mix0",
            "spppp",
            [("v", packed, BF)],
            [((128, 128), F32), ((2, 2, 8, 128), F32)],
        )(place, spectrum, folded, ones, z_table)
        hidden, spectrum = call(
            middle_kernel,
            "middle",
            "pppppph",
            [("h", cube, BF), ("v", packed, BF)],
            [((4, 2, 128, 128), BF), (packed, F32), (cube, F32), (cube, BF)],
            sems=2,
        )(exchange(planes), kc, bias, inv_y, fwd_y, x_table, fields)
        (planes,) = call(
            mix_kernel,
            "mix1",
            "spph",
            [("v", packed, BF)],
            [
                ((8, 2, 128, 256), BF), ((128, 128), F32), ((2, 2, 32, 128), F32),
                ((16, 2, 2, 8, 128), F32),
            ],
            sems=4,
        )(place, exchange(spectrum), z_table, gathered)
        (features,) = call(
            last_kernel,
            "last",
            "ppppph",
            [("h", (1,) + cube, BF)],
            [(cube, BF), (packed, F32), (cube, F32), (cube, BF)],
            sems=9,
        )(exchange(planes), kb, bias, inv_y, x_table, hidden)
        return features

    placed = (
        P("section", None, "slab", None, None),
        P(),
        P(),
        P(None, None, None, "section", "slab"),
        P(),
        P(),
    )
    return jax.shard_map(
        on_device,
        mesh=mesh,
        in_specs=placed,
        out_specs=P("section", None, "slab", None, None),
        check_vma=False,
    )
```

```python
import math

import jax
import jax.numpy as jnp
import ml_dtypes
import numpy as np
from jax import lax
from jax.experimental import pallas as pl
from jax.experimental.pallas import tpu as pltpu
from jax.sharding import PartitionSpec as P

K = 16
HALF = 2 * K
LENGTH = 128
SLABS = 64
UNROLL_A = 4
UNROLL_B = 8
BF = jnp.bfloat16
F32 = jnp.float32


def wave(freqs):
    where = np.arange(LENGTH, dtype=np.int64)[None, :]
    step = (freqs % LENGTH)[:, None] * where % LENGTH
    phase = step.astype(np.float32) * np.float32(2.0 * math.pi / LENGTH)
    cosine = np.cos(phase).astype(ml_dtypes.bfloat16).astype(np.float32)
    sine = np.sin(phase).astype(ml_dtypes.bfloat16).astype(np.float32)
    return cosine, sine


def make_tables():
    base = np.arange(HALF)
    signed = np.where(base < K, base, base - HALF)
    cos, sin = wave(signed)
    cos_z, sin_z = wave(np.arange(K))
    double = np.where(np.arange(K) == 0, 1.0, 2.0)[:, None]
    table = {}
    table["pair_y"] = np.concatenate([cos, -sin], 0)
    table["fwd_x"] = np.concatenate(
        [np.concatenate([cos, sin], 1), np.concatenate([-sin, cos], 1)], 0
    )
    fwd_z = np.stack([np.stack([cos_z, sin_z], 1), np.stack([-sin_z, cos_z], 1)], 0)
    fwd_z = fwd_z.reshape(2, K, 2, SLABS, 2)
    full = np.einsum("gf,akrsz->gaksfrz", np.eye(4), fwd_z)
    full = full.reshape(4 * HALF, 8, LENGTH).transpose(1, 0, 2).reshape(1024, LENGTH)
    first = np.einsum("akrsz->zaksr", fwd_z).reshape(2 * HALF, SLABS * 2)
    cz, sz = cos_z * double * 0.25, sin_z * double * 0.25
    inv_z = np.stack([np.stack([cz, -sz], 0), np.stack([sz, cz], 0)], 0)
    inv_z = inv_z.reshape(2, 2, K, SLABS, 2)
    back = np.einsum("gf,arksz->sgazfrk", np.eye(4), inv_z).reshape(SLABS * 16, 4 * HALF)
    table["z"] = np.concatenate([back, full, first], 0)
    inv_x = np.stack([np.stack([cos, -sin], 0), np.stack([sin, cos], 0)], 0)
    table["inv_x"] = np.einsum("arpx->axrp", inv_x).reshape(2 * LENGTH, 2 * HALF) * 0.125
    table["x"] = np.concatenate([table["fwd_x"], np.pad(table.pop("inv_x"), ((0, 0), (0, 192)))], 0)
    one_x = (cos.sum(1) - 1j * sin.sum(1)) / math.sqrt(LENGTH)
    one_z = (cos_z.sum(1) - 1j * sin_z.sum(1)) / math.sqrt(LENGTH)
    return table, one_x, one_z


def split(value):
    return np.stack([value.real, value.imag], 0).astype(np.float32)


def dot(left, right):
    return jnp.dot(left, right, preferred_element_type=F32)


def nt_dot(left, right):
    return lax.dot_general(left, right, (((1,), (1,)), ((), ())), preferred_element_type=F32)


def picks(rows, cols):
    row = lax.broadcasted_iota(jnp.int32, (rows, cols), 0)
    col = lax.broadcasted_iota(jnp.int32, (rows, cols), 1)
    return row, col


def one_hot(mask):
    return jnp.where(mask, 1.0, 0.0).astype(BF)


def fetch(copies):
    started = [pltpu.make_async_copy(source, target, sem) for source, target, sem in copies]
    for copy in started:
        copy.start()
    return started


def spread_kernel(
    place_ref, one_x_ref, bypass_ref, lift_ref, bypass_bias_ref, lift_bias_ref, pair_y_ref,
    one_y_ref, one_z_ref, z_ref, x_ref, kb_hbm, kc_ref, bias0_ref, bias1_hbm, fwd_y_hbm,
    inv_y_ref, ones_ref, z_out, x_out, kb_ref, bias1_ref, fwd_y_ref, sem,
):
    z_out[...] = z_ref[...]
    x_out[...] = x_ref[...]
    row, col = picks(512, 32)
    expand = one_hot(row // 16 == col)
    row, col = picks(512, 512)
    tall = nt_dot(expand, bypass_ref[1]).astype(BF)
    kb_ref[...] = jnp.where((row % 16) == (col % 16), nt_dot(tall, expand), 0.0).astype(BF)
    kept = fetch([(kb_ref, kb_hbm, sem.at[0])])
    joint = dot(lift_ref[...], bypass_ref[0])
    high = joint.astype(BF)
    low = (joint - high.astype(F32)).astype(BF)
    row, col = picks(64, 4)
    expand4 = one_hot(row // 16 == col)
    row, col = picks(512, 64)
    for index, part in enumerate((high, low)):
        wide = nt_dot(nt_dot(expand, part).astype(BF), expand4)
        wide = jnp.where((row % 16) == (col % 16), wide, 0.0).astype(BF)
        kc_ref[:, index * 64 : index * 64 + 64] = wide
    filled = jnp.ones((32, LENGTH), BF)
    row, col = picks(32, 32)
    eye = jnp.where(row == col, 1.0, 0.0)

    def column(vector):
        return dot((eye * vector.astype(F32)).astype(BF), filled)

    shift = column(bypass_bias_ref[0:1]) + lax.dot_general(
        bypass_ref[0], column(lift_bias_ref[...]).astype(BF), (((0,), (0,)), ((), ())),
        preferred_element_type=F32,
    )
    for bias_ref, value in ((bias0_ref, shift), (bias1_ref, column(bypass_bias_ref[1:2]))):
        bias_ref[...] = jnp.dot(
            expand.astype(F32), value, precision=lax.Precision.HIGHEST, preferred_element_type=F32
        )
    kept += fetch([(bias1_ref, bias1_hbm, sem.at[1])])
    row, col = picks(256, 64)
    repeat = one_hot((row // 64 == col // 16) & (row % 16 == col % 16))
    tall = dot(repeat, pair_y_ref[...])
    back = tall * 0.125
    row, col = picks(256, LENGTH)
    for c in range(4):
        block = jnp.where((row // 16) % 4 == c, back, 0.0).astype(BF)
        inv_y_ref[:, c * 128 : c * 128 + 128] = block
    wide = tall.T
    row, col = picks(LENGTH, 256)
    for c in range(4):
        block = jnp.where((col // 16) % 4 == c, wide, 0.0).astype(BF)
        fwd_y_ref[c * 128 : c * 128 + 128, :] = block
    kept += fetch([(fwd_y_ref, fwd_y_hbm, sem.at[2])])
    place = place_ref[0]
    xr, xi = one_x_ref[place // 2, 0:1, :], one_x_ref[place // 2, 1:2, :]
    yr = jnp.where(place % 2 == 0, one_y_ref[0, 0:1, :], one_y_ref[1, 0:1, :])
    yi = jnp.where(place % 2 == 0, one_y_ref[0, 1:2, :], one_y_ref[1, 1:2, :])
    pr, pi = xr * yr - xi * yi, xr * yi + xi * yr
    zr, zi = one_z_ref[0], one_z_ref[1]
    ones_ref[...] = jnp.concatenate([zr * pr - zi * pi, zr * pi + zi * pr], axis=0)
    for copy in kept:
        copy.wait()


def fold_kernel(lift_ref, lift_bias_ref, weight_hbm, out_ref, weight, sem):
    (copy,) = fetch([(weight_hbm.at[0], weight, sem.at[0])])
    row, col = picks(HALF, 4)
    pick = one_hot((row % 8 == col))
    row, col = picks(HALF, HALF)
    lift = dot(pick, lift_ref[...]) + jnp.where(row % 8 == 4, lift_bias_ref[...].astype(F32), 0.0)
    row, col = picks(HALF, LENGTH)
    lift = dot(lift.astype(BF), one_hot(row == col // 4))
    lift = jnp.where(row // 8 == col % 4, lift, 0.0).astype(BF)
    copy.wait()
    for r in range(2):
        folded = dot(lift, weight[r]).astype(BF)
        for section in range(8):
            out_ref[section, r * HALF : r * HALF + HALF, :] = folded


def start_kernel(fields_hbm, pair_y_hbm, fwd_x_hbm, out_ref, fields, pair_y, fwd_x, rows, sem):
    copies = fetch(
        [
            (pair_y_hbm, pair_y, sem.at[0]),
            (fields_hbm.at[0], fields, sem.at[1]),
            (fwd_x_hbm, fwd_x, sem.at[2]),
        ]
    )
    copies[0].wait()
    row, col = picks(256, 64)
    repeat = one_hot((row // 64 == col // 16) & (row % 16 == col % 16))
    wide = dot(repeat, pair_y[...]).T
    row, col = picks(LENGTH, 256)
    fwd_y = jnp.concatenate(
        [jnp.where((col // 16) % 4 == c, wide, 0.0).astype(BF) for c in range(4)], axis=0
    )
    lane = lax.broadcasted_iota(jnp.int32, (64, LENGTH), 1)
    copies[1].wait()
    copies[2].wait()
    made = []
    for z in range(2):
        wide = jnp.concatenate([fields[c, z] for c in range(4)], axis=1)
        along = dot(wide, fwd_y).astype(BF)
        stacked = jnp.concatenate([along[:, :128], along[:, 128:]], axis=0)
        made.append(dot(fwd_x[...], stacked) * (1.0 / LENGTH))
    first = jnp.where(lane < 64, made[0], pltpu.roll(made[1], 64, 1))
    second = jnp.where(lane < 64, pltpu.roll(made[0], 64, 1), made[1])
    for h, value in enumerate((first, second)):
        for r in range(2):
            rows[pl.ds(h * 2 + r, 32, stride=4), :] = value[r * 32 : r * 32 + 32]
    out_ref[...] = rows[...].astype(BF)


def mix(weight_ref, modes, pattern, copies):
    low = lax.broadcasted_iota(jnp.int32, (8, LENGTH), 0) < 4
    for pair in range(16):
        for r in range(2):
            for half in range(2):
                even = jnp.broadcast_to(modes[r, half, 2 * pair : 2 * pair + 1, :], (8, LENGTH))
                odd = jnp.broadcast_to(modes[r, half, 2 * pair + 1 : 2 * pair + 2, :], (8, LENGTH))
                pattern[pair, r, half] = jnp.where(low, even, odd)
    mixed = {}
    for g in range(4):
        copies[g].wait()
        total = {}
        for side in range(2):
            section = 2 * g + side
            acc = [[jnp.zeros((8, LENGTH), F32) for _ in range(2)] for _ in range(2)]
            for quad in range(8):
                real = weight_ref[section, 0, quad * 16 : quad * 16 + 16, :].astype(F32)
                imag = weight_ref[section, 1, quad * 16 : quad * 16 + 16, :].astype(F32)
                for sub in range(2):
                    pair = quad * 2 + sub
                    for half in range(2):
                        wr = real[sub * 8 : sub * 8 + 8, half * 128 : half * 128 + 128]
                        wi = imag[sub * 8 : sub * 8 + 8, half * 128 : half * 128 + 128]
                        mr, mi = pattern[pair, 0, half], pattern[pair, 1, half]
                        acc[0][half] = acc[0][half] + wr * mr - wi * mi
                        acc[1][half] = acc[1][half] + wr * mi + wi * mr
            for r in range(2):
                for half in range(2):
                    value = acc[r][half]
                    total[side, r, half] = value + pltpu.roll(value, 4, 0)
        for r in range(2):
            for half in range(2):
                mixed[g, r, half] = jnp.where(low, total[0, r, half], total[1, r, half])
    return mixed


def first_mix(folded_ref, modes):
    sub = lax.broadcasted_iota(jnp.int32, (8, LENGTH), 0)
    mixed = {}
    for g in range(4):
        for row in range(0, 8, 2):
            section, o = 2 * g + row // 4, row % 4
            real = folded_ref[section, o * 8 : o * 8 + 16, :].astype(F32)
            imag = folded_ref[section, HALF + o * 8 : HALF + o * 8 + 16, :].astype(F32)
            for more in range(2):
                for half in range(2):
                    wr = real[more * 8 : more * 8 + 8, half * 128 : half * 128 + 128]
                    wi = imag[more * 8 : more * 8 + 8, half * 128 : half * 128 + 128]
                    mr, mi = modes[0, half], modes[1, half]
                    for r, value in enumerate((wr * mr - wi * mi, wr * mi + wi * mr)):
                        for step in (4, 2, 1):
                            value = value + pltpu.roll(value, step, 0)
                        if row + more:
                            value = jnp.where(sub == row + more, value, mixed[g, r, half])
                        mixed[g, r, half] = value
    return mixed


def evaluate(mixed, turned, z_ref, out_ref):
    slot = lax.broadcasted_iota(jnp.int32, (8, LENGTH), 1) // K
    for py in range(K):
        half, at = py // 8, py % 8
        value = None
        for g in range(4):
            for r in range(2):
                where = 2 * g + r
                moved = mixed[g, r, half]
                if where != at:
                    moved = pltpu.roll(moved, (where - at) * K % LENGTH, 1)
                value = moved if value is None else jnp.where(slot == where, moved, value)
        turned[pl.ds(py, 8, stride=K), :] = value
    out_ref[...] = nt_dot(z_ref[:1024], turned[...].astype(BF)).astype(BF)


def unravel(turned, groups, modes):
    slot = lax.broadcasted_iota(jnp.int32, (8, LENGTH), 1) // K
    parts = [turned[pl.ds(py, 8, stride=K), :] for py in range(K)]
    for g in range(groups):
        for r in range(2):
            source = 2 * g + r
            for half in range(2):
                value = None
                for at in range(8):
                    moved = parts[half * 8 + at]
                    if at != source:
                        moved = pltpu.roll(moved, (at - source) * K % LENGTH, 1)
                    value = moved if value is None else jnp.where(slot == at, moved, value)
                modes[r, half, g * 8 : g * 8 + 8, :] = value


def dropped(place_ref, shape):
    row = lax.broadcasted_iota(jnp.int32, shape, 0)
    lane = lax.broadcasted_iota(jnp.int32, shape, 1)
    origin = jnp.logical_and(row % K == 0, lane % K == 0)
    return jnp.logical_and(origin, place_ref[0] == 0)


def first_mix_kernel(
    place_ref, got_ref, folded_ref, ones_ref, z_ref, out_ref, turned, modes
):
    both = dot(z_ref[2048:], got_ref[...])
    lane = lax.broadcasted_iota(jnp.int32, (HALF, LENGTH), 1)
    value = both[:HALF] + pltpu.roll(both[HALF:], 64, 1)
    value = jnp.where(lane < 64, value, 0.0) * (1.0 / math.sqrt(LENGTH))
    value = jnp.where(lane // K == 4, ones_ref[...], value)
    value = jnp.where(dropped(place_ref, value.shape), 0.0, value)
    value = jnp.concatenate([value, jnp.zeros((LENGTH - HALF, LENGTH), F32)], axis=0)
    turned[...] = value.T
    unravel(turned, 1, modes)
    evaluate(first_mix(folded_ref, modes), turned, z_ref, out_ref)


def mix_kernel(
    place_ref, got_ref, z_ref, weight_hbm, out_ref, weight, turned, modes, pattern, sem
):
    copies = fetch(
        [(weight_hbm.at[pl.ds(2 * g, 2), 1], weight.at[pl.ds(2 * g, 2)], sem.at[g]) for g in range(4)]
    )
    value = None
    for block in range(8):
        span = slice(block * 128, block * 128 + 128)
        part = dot(z_ref[1024 + block * 128 : 1152 + block * 128], got_ref[span])
        value = part if value is None else value + part
    value = value * (1.0 / math.sqrt(LENGTH))
    value = jnp.where(dropped(place_ref, value.shape), 0.0, value)
    turned[...] = value.T
    unravel(turned, 4, modes)
    evaluate(mix(weight, modes, pattern, copies), turned, z_ref, out_ref)


def swapped(first, second):
    low = lax.broadcasted_iota(jnp.int32, first.shape, 1) < 64
    return (
        jnp.where(low, first, pltpu.roll(second, 64, 1)),
        jnp.where(low, pltpu.roll(first, 64, 1), second),
    )


def inverse(got_ref, x_ref, inv_y_ref, rows, field):
    rows[...] = got_ref[...].astype(F32)

    def step(index, carry):
        g, z = index // 2, index % 2
        parts = []
        for h in range(2):
            pieces = [rows[pl.ds(h * 16 + g * 4 + r * 2 + z, 32, stride=32), :] for r in range(2)]
            parts.append(jnp.concatenate(pieces, axis=0))
        parts = jnp.concatenate(swapped(*parts), axis=1).astype(BF)
        along = dot(x_ref[64:, :64], parts).astype(BF)
        for quad in range(2):
            lanes = slice(quad * 128, quad * 128 + 128)
            wide = jnp.concatenate([along[:128, lanes], along[128:, lanes]], axis=1)
            made = dot(wide, inv_y_ref[...])
            for o in range(4):
                field[g * 8 + quad * 4 + o, z] = made[:, o * 128 : o * 128 + 128]
        return carry

    lax.fori_loop(0, 8, step, 0, unroll=UNROLL_A)


def activate(value):
    inner = value * (0.7978845608028654 + 0.035677408136300125 * value * value)
    half = 0.5 * value
    return half + half * jnp.tanh(inner)


def pointwise(span, hidden, map_ref, bias, field):
    bypassed = dot(map_ref[...], hidden)
    made = []
    for z in range(2):
        part = field[:, z, span, :].reshape(512, LENGTH)
        value = bypassed[:, z * 128 : z * 128 + 128] + bias[...] + part
        made.append(activate(value).astype(BF))
    return made


def middle_kernel(
    got_ref, kc_ref, bias_ref, inv_y_ref, fwd_y_hbm, x_ref, fields_hbm, hidden, out_ref, fields,
    fwd_y_ref, rows, field, sem,
):
    copies = fetch([(fields_hbm.at[0], fields, sem.at[0]), (fwd_y_hbm, fwd_y_ref, sem.at[1])])
    inverse(got_ref, x_ref, inv_y_ref, rows, field)
    for copy in copies:
        copy.wait()
    def apply(block, carry):
        span = pl.ds(pl.multiple_of(block * 16, 16), 16)
        raw = [fields[:, z, span, :].reshape(64, LENGTH) for z in range(2)]
        raw = jnp.concatenate(raw, axis=1)
        made = pointwise(span, jnp.concatenate([raw, raw], axis=0), kc_ref, bias_ref, field)
        for z in range(2):
            hidden[:, z, span, :] = made[z].reshape(32, 16, LENGTH)
        return carry

    lax.fori_loop(0, 8, apply, 0, unroll=UNROLL_B)
    def forward(index, carry):
        g, z = index // 2, index % 2
        stacked = []
        for quad in range(2):
            wide = jnp.concatenate([hidden[g * 8 + quad * 4 + c, z] for c in range(4)], axis=1)
            along = dot(wide, fwd_y_ref[...]).astype(BF)
            stacked.append(jnp.concatenate([along[:, :128], along[:, 128:]], axis=0))
        spectrum = dot(x_ref[:64], jnp.concatenate(stacked, axis=1)) * (1.0 / LENGTH)
        for h, value in enumerate(swapped(spectrum[:, :128], spectrum[:, 128:])):
            for r in range(2):
                at = h * 16 + g * 4 + r * 2 + z
                rows[pl.ds(at, 32, stride=32), :] = value[r * 32 : r * 32 + 32]
        return carry

    lax.fori_loop(0, 8, forward, 0, unroll=UNROLL_A)
    out_ref[...] = rows[...].astype(BF)


def last_kernel(
    got_ref, kb_hbm, bias_hbm, inv_y_ref, x_ref, hidden, out_hbm, kb, bias, rows, field, made_ref, sem
):
    copies = fetch([(kb_hbm, kb, sem.at[8]), (bias_hbm, bias, sem.at[9])])
    inverse(got_ref, x_ref, inv_y_ref, rows, field)
    for copy in copies:
        copy.wait()

    def keep(block):
        span = pl.ds(pl.multiple_of(block * 16, 16), 16)
        source, target = made_ref.at[:, :, span, :], out_hbm.at[0, :, :, span, :]
        return pltpu.make_async_copy(source, target, sem.at[block])

    def apply(block, carry):
        span = pl.ds(pl.multiple_of(block * 16, 16), 16)
        raw = [hidden[:, z, span, :].reshape(512, LENGTH) for z in range(2)]
        made = pointwise(span, jnp.concatenate(raw, axis=1), kb, bias, field)
        for z in range(2):
            made_ref[:, z, span, :] = made[z].reshape(32, 16, LENGTH)
        keep(block).start()
        return carry

    lax.fori_loop(0, 8, apply, 0, unroll=UNROLL_B)
    for block in range(8):
        keep(block).wait()


def call(kernel, name, inputs, outputs, scratch, sems=0, limit=24):
    spaces = {"s": pltpu.SMEM, "v": pltpu.VMEM, "p": pltpu.VMEM, "h": pltpu.HBM, "f": pltpu.HBM}
    fetched = [index for index, letter in enumerate(inputs) if letter == "f"]

    def run(*arrays):
        buffers = [pltpu.VMEM(arrays[index].shape, arrays[index].dtype) for index in fetched]
        own = [pltpu.VMEM(shape, kind) for shape, kind in scratch]
        if sems:
            own.append(pltpu.SemaphoreType.DMA((sems,)))
        if fetched:
            buffers.append(pltpu.SemaphoreType.DMA((len(fetched),)))

        def body(*refs):
            refs = list(refs)
            if fetched:
                first = len(inputs) + len(outputs) + len(own)
                copies = []
                for order, index in enumerate(fetched):
                    copies.append((refs[index], refs[first + order], refs[-1].at[order]))
                    refs[index] = refs[first + order]
                for copy in fetch(copies):
                    copy.wait()
                refs = refs[:first]
            kernel(*refs)

        placed = []
        for letter, array in zip(inputs, arrays):
            if letter in "hfp":
                array = pltpu.with_memory_space_constraint(array, spaces[letter])
            placed.append(array)
        return pl.pallas_call(
            body,
            name=name,
            out_shape=[spaces[letter](shape, kind) for letter, shape, kind in outputs],
            in_specs=[pl.BlockSpec(memory_space=spaces[letter]) for letter in inputs],
            out_specs=[pl.BlockSpec(memory_space=spaces[letter]) for letter, _, _ in outputs],
            scratch_shapes=own + buffers,
            compiler_params=pltpu.CompilerParams(vmem_limit_bytes=limit << 20),
        )(*placed)

    return run


def exchange(value, axis="slab"):
    return lax.all_to_all(value, axis, split_axis=0, concat_axis=0, tiled=True)


tie = lax.optimization_barrier


def solution(mesh):
    table, one_x, one_z = make_tables()
    const = {name: value.astype(ml_dtypes.bfloat16) for name, value in table.items()}
    ones_x = np.repeat(split(one_x).T[:, :, None], LENGTH, axis=2)
    ones_y = np.tile(split(one_x).reshape(2, 2, 1, K), (1, 1, 8, 1)).reshape(2, 2, LENGTH)
    ones_y = ones_y.transpose(1, 0, 2)
    ones_z = np.repeat(split(one_z)[:, :, None], LENGTH, axis=2)

    def on_device(fields, lift_weight, lift_bias, spectral_weight, bypass_weight, bypass_bias):
        place = lax.axis_index("slab").reshape(1)
        lift_bias = lift_bias[None]
        packed, cube = (1024, LENGTH), (32, 2, 128, 128)
        (spectrum,) = call(
            start_kernel,
            "start",
            "hhh",
            [("v", (128, LENGTH), BF)],
            [((4, 2, 128, 128), BF), ((64, 128), BF), ((64, 256), BF), ((128, 128), F32)],
            sems=3,
        )(fields, const["pair_y"], const["fwd_x"])
        spectrum, spectral_weight = tie((spectrum, spectral_weight))
        spectrum = exchange(spectrum)
        weight = spectral_weight.reshape(2, 2, LENGTH, 256)
        (folded,) = call(
            fold_kernel, "fold", "ffh", [("v", (8, 64, 256), BF)], [((2, 128, 256), BF)], sems=1
        )(lift_weight, lift_bias, weight)
        folded, bypass_weight, weight, _ = tie((folded, bypass_weight, weight, spectrum))
        gathered = lax.all_gather(weight, "section", axis=0)
        folded = exchange(folded.reshape(512, 256), "section").reshape(8, 64, 256)
        kb, kc, bias0, bias1, fwd_y, inv_y, ones, z_table, x_table = call(
            spread_kernel,
            "spread",
            "s" + "f" * 10,
            [
                ("h", (512, 512), BF),
                ("v", (512, 128), BF),
                ("v", (512, LENGTH), F32),
                ("h", (512, LENGTH), F32),
                ("h", (512, 256), BF),
                ("v", (256, 512), BF),
                ("v", (HALF, LENGTH), F32),
                ("v", (2112, 128), BF),
                ("v", (320, 256), BF),
            ],
            [((512, 512), BF), ((512, LENGTH), F32), ((512, 256), BF)],
            sems=3,
        )(
            place, ones_x, bypass_weight, lift_weight, bypass_bias, lift_bias, const["pair_y"],
            ones_y, ones_z, const["z"], const["x"],
        )
        (planes,) = call(
            first_mix_kernel,
            "mix0",
            "spppp",
            [("v", packed, BF)],
            [((128, 128), F32), ((2, 2, 8, 128), F32)],
        )(place, spectrum, folded, ones, z_table)
        hidden, spectrum = call(
            middle_kernel,
            "middle",
            "pppphph",
            [("v", cube, BF), ("v", packed, BF)],
            [((4, 2, 128, 128), BF), ((512, 256), BF), (packed, F32), (cube, F32)],
            sems=2,
        )(exchange(planes), kc, bias0, inv_y, fwd_y, x_table, fields)
        (planes,) = call(
            mix_kernel,
            "mix1",
            "spph",
            [("v", packed, BF)],
            [
                ((8, 2, 128, 256), BF), ((128, 128), F32), ((2, 2, 32, 128), F32),
                ((16, 2, 2, 8, 128), F32),
            ],
            sems=4,
        )(place, exchange(spectrum), z_table, gathered)
        (features,) = call(
            last_kernel,
            "last",
            "phhppp",
            [("h", (1,) + cube, BF)],
            [((512, 512), BF), ((512, LENGTH), F32), (packed, F32), (cube, F32), (cube, BF)],
            sems=10,
        )(exchange(planes), kb, bias1, inv_y, x_table, hidden)
        return features

    placed = (
        P("section", None, "slab", None, None),
        P(),
        P(),
        P(None, None, None, "section", "slab"),
        P(),
        P(),
    )
    return jax.shard_map(
        on_device,
        mesh=mesh,
        in_specs=placed,
        out_specs=P("section", None, "slab", None, None),
        check_vma=False,
    )
```

```python
import math

import jax
import jax.numpy as jnp
import ml_dtypes
import numpy as np
from jax import lax
from jax.experimental import pallas as pl
from jax.experimental.pallas import tpu as pltpu
from jax.sharding import PartitionSpec as P

K = 16
HALF = 2 * K
LENGTH = 128
SLABS = 64
UNROLL_A = 4
UNROLL_F = 8
UNROLL_B = 8
BF = jnp.bfloat16
F32 = jnp.float32


def wave(freqs):
    where = np.arange(LENGTH, dtype=np.int64)[None, :]
    step = (freqs % LENGTH)[:, None] * where % LENGTH
    phase = step.astype(np.float32) * np.float32(2.0 * math.pi / LENGTH)
    cosine = np.cos(phase).astype(ml_dtypes.bfloat16).astype(np.float32)
    sine = np.sin(phase).astype(ml_dtypes.bfloat16).astype(np.float32)
    return cosine, sine


def make_tables():
    base = np.arange(HALF)
    signed = np.where(base < K, base, base - HALF)
    cos, sin = wave(signed)
    cos_z, sin_z = wave(np.arange(K))
    double = np.where(np.arange(K) == 0, 1.0, 2.0)[:, None]
    table = {}
    table["pair_y"] = np.concatenate([cos, -sin], 0)
    table["fwd_x"] = np.concatenate(
        [np.concatenate([cos, sin], 1), np.concatenate([-sin, cos], 1)], 0
    )
    fwd_z = np.stack([np.stack([cos_z, sin_z], 1), np.stack([-sin_z, cos_z], 1)], 0)
    fwd_z = fwd_z.reshape(2, K, 2, SLABS, 2)
    full = np.einsum("gf,akrsz->gaksfrz", np.eye(4), fwd_z)
    full = full.reshape(4 * HALF, 8, LENGTH).transpose(1, 0, 2).reshape(1024, LENGTH)
    first = np.einsum("akrsz->zaksr", fwd_z).reshape(2 * HALF, SLABS * 2)
    cz, sz = cos_z * double * 0.25, sin_z * double * 0.25
    inv_z = np.stack([np.stack([cz, -sz], 0), np.stack([sz, cz], 0)], 0)
    inv_z = inv_z.reshape(2, 2, K, SLABS, 2)
    back = np.einsum("gf,arksz->sgazfrk", np.eye(4), inv_z).reshape(SLABS * 16, 4 * HALF)
    table["z"] = np.concatenate([back, full, first], 0)
    inv_x = np.stack([np.stack([cos, -sin], 0), np.stack([sin, cos], 0)], 0)
    table["inv_x"] = np.einsum("arpx->axrp", inv_x).reshape(2 * LENGTH, 2 * HALF) * 0.125
    table["x"] = np.concatenate([table["fwd_x"], np.pad(table.pop("inv_x"), ((0, 0), (0, 192)))], 0)
    one_x = (cos.sum(1) - 1j * sin.sum(1)) / math.sqrt(LENGTH)
    one_z = (cos_z.sum(1) - 1j * sin_z.sum(1)) / math.sqrt(LENGTH)
    return table, one_x, one_z


def split(value):
    return np.stack([value.real, value.imag], 0).astype(np.float32)


def dot(left, right):
    return jnp.dot(left, right, preferred_element_type=F32)


def nt_dot(left, right):
    return lax.dot_general(left, right, (((1,), (1,)), ((), ())), preferred_element_type=F32)


def picks(rows, cols):
    row = lax.broadcasted_iota(jnp.int32, (rows, cols), 0)
    col = lax.broadcasted_iota(jnp.int32, (rows, cols), 1)
    return row, col


def one_hot(mask):
    return jnp.where(mask, 1.0, 0.0).astype(BF)


def fetch(copies):
    started = [pltpu.make_async_copy(source, target, sem) for source, target, sem in copies]
    for copy in started:
        copy.start()
    return started


def spread_kernel(
    place_ref, one_x_ref, bypass_ref, lift_ref, bypass_bias_ref, lift_bias_ref, pair_y_ref,
    one_y_ref, one_z_ref, z_ref, x_ref, kb_hbm, kc_ref, bias0_ref, bias1_hbm, fwd_y_hbm,
    inv_y_ref, ones_ref, z_out, x_out, kb_ref, bias1_ref, fwd_y_ref, sem,
):
    z_out[...] = z_ref[...]
    x_out[...] = x_ref[...]
    row, col = picks(512, 32)
    expand = one_hot(row // 16 == col)
    row, col = picks(512, 512)
    tall = nt_dot(expand, bypass_ref[1]).astype(BF)
    kb_ref[...] = jnp.where((row % 16) == (col % 16), nt_dot(tall, expand), 0.0).astype(BF)
    kept = fetch([(kb_ref, kb_hbm, sem.at[0])])
    joint = dot(lift_ref[...], bypass_ref[0])
    high = joint.astype(BF)
    low = (joint - high.astype(F32)).astype(BF)
    row, col = picks(64, 4)
    expand4 = one_hot(row // 16 == col)
    row, col = picks(512, 64)
    for index, part in enumerate((high, low)):
        wide = nt_dot(nt_dot(expand, part).astype(BF), expand4)
        wide = jnp.where((row % 16) == (col % 16), wide, 0.0).astype(BF)
        kc_ref[:, index * 64 : index * 64 + 64] = wide
    filled = jnp.ones((32, LENGTH), BF)
    row, col = picks(32, 32)
    eye = jnp.where(row == col, 1.0, 0.0)

    def column(vector):
        return dot((eye * vector.astype(F32)).astype(BF), filled)

    shift = column(bypass_bias_ref[0:1]) + lax.dot_general(
        bypass_ref[0], column(lift_bias_ref[...]).astype(BF), (((0,), (0,)), ((), ())),
        preferred_element_type=F32,
    )
    for bias_ref, value in ((bias0_ref, shift), (bias1_ref, column(bypass_bias_ref[1:2]))):
        bias_ref[...] = jnp.dot(
            expand.astype(F32), value, precision=lax.Precision.HIGHEST, preferred_element_type=F32
        )
    kept += fetch([(bias1_ref, bias1_hbm, sem.at[1])])
    row, col = picks(256, 64)
    repeat = one_hot((row // 64 == col // 16) & (row % 16 == col % 16))
    tall = dot(repeat, pair_y_ref[...])
    back = tall * 0.125
    row, col = picks(256, LENGTH)
    for c in range(4):
        block = jnp.where((row // 16) % 4 == c, back, 0.0).astype(BF)
        inv_y_ref[:, c * 128 : c * 128 + 128] = block
    wide = tall.T
    row, col = picks(LENGTH, 256)
    for c in range(4):
        block = jnp.where((col // 16) % 4 == c, wide, 0.0).astype(BF)
        fwd_y_ref[c * 128 : c * 128 + 128, :] = block
    kept += fetch([(fwd_y_ref, fwd_y_hbm, sem.at[2])])
    place = place_ref[0]
    xr, xi = one_x_ref[place // 2, 0:1, :], one_x_ref[place // 2, 1:2, :]
    yr = jnp.where(place % 2 == 0, one_y_ref[0, 0:1, :], one_y_ref[1, 0:1, :])
    yi = jnp.where(place % 2 == 0, one_y_ref[0, 1:2, :], one_y_ref[1, 1:2, :])
    pr, pi = xr * yr - xi * yi, xr * yi + xi * yr
    zr, zi = one_z_ref[0], one_z_ref[1]
    ones_ref[...] = jnp.concatenate([zr * pr - zi * pi, zr * pi + zi * pr], axis=0)
    for copy in kept:
        copy.wait()


def fold_kernel(lift_hbm, lift_bias_hbm, weight_hbm, out_ref, lift_ref, lift_bias_ref, weight, sem):
    copy, *small = fetch(
        [
            (weight_hbm.at[0], weight, sem.at[0]),
            (lift_hbm, lift_ref, sem.at[1]),
            (lift_bias_hbm, lift_bias_ref, sem.at[2]),
        ]
    )
    for part in small:
        part.wait()
    row, col = picks(HALF, 4)
    pick = one_hot((row % 8 == col))
    row, col = picks(HALF, HALF)
    lift = dot(pick, lift_ref[...]) + jnp.where(row % 8 == 4, lift_bias_ref[...].astype(F32), 0.0)
    row, col = picks(HALF, LENGTH)
    lift = dot(lift.astype(BF), one_hot(row == col // 4))
    lift = jnp.where(row // 8 == col % 4, lift, 0.0).astype(BF)
    copy.wait()
    for r in range(2):
        folded = dot(lift, weight[r]).astype(BF)
        for section in range(8):
            out_ref[section, r * HALF : r * HALF + HALF, :] = folded


def start_kernel(fields_hbm, pair_y_hbm, fwd_x_hbm, out_ref, fields, pair_y, fwd_x, rows, sem):
    copies = fetch(
        [
            (pair_y_hbm, pair_y, sem.at[0]),
            (fields_hbm.at[0], fields, sem.at[1]),
            (fwd_x_hbm, fwd_x, sem.at[2]),
        ]
    )
    copies[0].wait()
    row, col = picks(256, 64)
    repeat = one_hot((row // 64 == col // 16) & (row % 16 == col % 16))
    wide = dot(repeat, pair_y[...]).T
    row, col = picks(LENGTH, 256)
    fwd_y = jnp.concatenate(
        [jnp.where((col // 16) % 4 == c, wide, 0.0).astype(BF) for c in range(4)], axis=0
    )
    lane = lax.broadcasted_iota(jnp.int32, (64, LENGTH), 1)
    copies[1].wait()
    copies[2].wait()
    made = []
    for z in range(2):
        wide = jnp.concatenate([fields[c, z] for c in range(4)], axis=1)
        along = dot(wide, fwd_y).astype(BF)
        stacked = jnp.concatenate([along[:, :128], along[:, 128:]], axis=0)
        made.append(dot(fwd_x[...], stacked) * (1.0 / LENGTH))
    first = jnp.where(lane < 64, made[0], pltpu.roll(made[1], 64, 1))
    second = jnp.where(lane < 64, pltpu.roll(made[0], 64, 1), made[1])
    for h, value in enumerate((first, second)):
        for r in range(2):
            rows[pl.ds(h * 2 + r, 32, stride=4), :] = value[r * 32 : r * 32 + 32]
    out_ref[...] = rows[...].astype(BF)


def mix(weight_ref, modes, pattern, copies):
    low = lax.broadcasted_iota(jnp.int32, (8, LENGTH), 0) < 4
    for pair in range(16):
        for r in range(2):
            for half in range(2):
                even = jnp.broadcast_to(modes[r, half, 2 * pair : 2 * pair + 1, :], (8, LENGTH))
                odd = jnp.broadcast_to(modes[r, half, 2 * pair + 1 : 2 * pair + 2, :], (8, LENGTH))
                pattern[pair, r, half] = jnp.where(low, even, odd)
    mixed = {}
    for g in range(4):
        copies[g].wait()
        total = {}
        for side in range(2):
            section = 2 * g + side
            acc = [[jnp.zeros((8, LENGTH), F32) for _ in range(2)] for _ in range(2)]
            for quad in range(8):
                real = weight_ref[section, 0, quad * 16 : quad * 16 + 16, :].astype(F32)
                imag = weight_ref[section, 1, quad * 16 : quad * 16 + 16, :].astype(F32)
                for sub in range(2):
                    pair = quad * 2 + sub
                    for half in range(2):
                        wr = real[sub * 8 : sub * 8 + 8, half * 128 : half * 128 + 128]
                        wi = imag[sub * 8 : sub * 8 + 8, half * 128 : half * 128 + 128]
                        mr, mi = pattern[pair, 0, half], pattern[pair, 1, half]
                        acc[0][half] = acc[0][half] + wr * mr - wi * mi
                        acc[1][half] = acc[1][half] + wr * mi + wi * mr
            for r in range(2):
                for half in range(2):
                    value = acc[r][half]
                    total[side, r, half] = value + pltpu.roll(value, 4, 0)
        for r in range(2):
            for half in range(2):
                mixed[g, r, half] = jnp.where(low, total[0, r, half], total[1, r, half])
    return mixed


def first_mix(folded_ref, modes):
    sub = lax.broadcasted_iota(jnp.int32, (8, LENGTH), 0)
    mixed = {}
    for g in range(4):
        for row in range(0, 8, 2):
            section, o = 2 * g + row // 4, row % 4
            real = folded_ref[section, o * 8 : o * 8 + 16, :].astype(F32)
            imag = folded_ref[section, HALF + o * 8 : HALF + o * 8 + 16, :].astype(F32)
            for more in range(2):
                for half in range(2):
                    wr = real[more * 8 : more * 8 + 8, half * 128 : half * 128 + 128]
                    wi = imag[more * 8 : more * 8 + 8, half * 128 : half * 128 + 128]
                    mr, mi = modes[0, half], modes[1, half]
                    for r, value in enumerate((wr * mr - wi * mi, wr * mi + wi * mr)):
                        for step in (4, 2, 1):
                            value = value + pltpu.roll(value, step, 0)
                        if row + more:
                            value = jnp.where(sub == row + more, value, mixed[g, r, half])
                        mixed[g, r, half] = value
    return mixed


def evaluate(mixed, turned, z_ref, out_ref):
    slot = lax.broadcasted_iota(jnp.int32, (8, LENGTH), 1) // K
    for py in range(K):
        half, at = py // 8, py % 8
        value = None
        for g in range(4):
            for r in range(2):
                where = 2 * g + r
                moved = mixed[g, r, half]
                if where != at:
                    moved = pltpu.roll(moved, (where - at) * K % LENGTH, 1)
                value = moved if value is None else jnp.where(slot == where, moved, value)
        turned[pl.ds(py, 8, stride=K), :] = value
    out_ref[...] = nt_dot(z_ref[:1024], turned[...].astype(BF)).astype(BF)


def unravel(turned, groups, modes):
    slot = lax.broadcasted_iota(jnp.int32, (8, LENGTH), 1) // K
    parts = [turned[pl.ds(py, 8, stride=K), :] for py in range(K)]
    for g in range(groups):
        for r in range(2):
            source = 2 * g + r
            for half in range(2):
                value = None
                for at in range(8):
                    moved = parts[half * 8 + at]
                    if at != source:
                        moved = pltpu.roll(moved, (at - source) * K % LENGTH, 1)
                    value = moved if value is None else jnp.where(slot == at, moved, value)
                modes[r, half, g * 8 : g * 8 + 8, :] = value


def dropped(place_ref, shape):
    row = lax.broadcasted_iota(jnp.int32, shape, 0)
    lane = lax.broadcasted_iota(jnp.int32, shape, 1)
    origin = jnp.logical_and(row % K == 0, lane % K == 0)
    return jnp.logical_and(origin, place_ref[0] == 0)


def first_mix_kernel(
    place_ref, got_ref, folded_ref, ones_ref, z_ref, out_ref, turned, modes
):
    both = dot(z_ref[2048:], got_ref[...])
    lane = lax.broadcasted_iota(jnp.int32, (HALF, LENGTH), 1)
    value = both[:HALF] + pltpu.roll(both[HALF:], 64, 1)
    value = jnp.where(lane < 64, value, 0.0) * (1.0 / math.sqrt(LENGTH))
    value = jnp.where(lane // K == 4, ones_ref[...], value)
    value = jnp.where(dropped(place_ref, value.shape), 0.0, value)
    value = jnp.concatenate([value, jnp.zeros((LENGTH - HALF, LENGTH), F32)], axis=0)
    turned[...] = value.T
    unravel(turned, 1, modes)
    evaluate(first_mix(folded_ref, modes), turned, z_ref, out_ref)


def mix_kernel(
    place_ref, got_ref, z_ref, weight_hbm, out_ref, weight, turned, modes, pattern, sem
):
    copies = fetch(
        [(weight_hbm.at[pl.ds(2 * g, 2), 1], weight.at[pl.ds(2 * g, 2)], sem.at[g]) for g in range(4)]
    )
    value = None
    for block in range(8):
        span = slice(block * 128, block * 128 + 128)
        part = dot(z_ref[1024 + block * 128 : 1152 + block * 128], got_ref[span])
        value = part if value is None else value + part
    value = value * (1.0 / math.sqrt(LENGTH))
    value = jnp.where(dropped(place_ref, value.shape), 0.0, value)
    turned[...] = value.T
    unravel(turned, 4, modes)
    evaluate(mix(weight, modes, pattern, copies), turned, z_ref, out_ref)


def swapped(first, second):
    low = lax.broadcasted_iota(jnp.int32, first.shape, 1) < 64
    return (
        jnp.where(low, first, pltpu.roll(second, 64, 1)),
        jnp.where(low, pltpu.roll(first, 64, 1), second),
    )


def inverse(got_ref, x_ref, inv_y_ref, rows, field):
    rows[...] = got_ref[...].astype(F32)

    def step(index, carry):
        g, z = index // 2, index % 2
        parts = []
        for h in range(2):
            pieces = [rows[pl.ds(h * 16 + g * 4 + r * 2 + z, 32, stride=32), :] for r in range(2)]
            parts.append(jnp.concatenate(pieces, axis=0))
        parts = jnp.concatenate(swapped(*parts), axis=1).astype(BF)
        along = dot(x_ref[64:, :64], parts).astype(BF)
        for quad in range(2):
            lanes = slice(quad * 128, quad * 128 + 128)
            wide = jnp.concatenate([along[:128, lanes], along[128:, lanes]], axis=1)
            made = dot(wide, inv_y_ref[...])
            for o in range(4):
                field[g * 8 + quad * 4 + o, z] = made[:, o * 128 : o * 128 + 128]
        return carry

    lax.fori_loop(0, 8, step, 0, unroll=UNROLL_A)


def activate(value):
    inner = value * (0.7978845608028654 + 0.035677408136300125 * value * value)
    half = 0.5 * value
    return half + half * jnp.tanh(inner)


def pointwise(span, hidden, map_ref, bias, field):
    bypassed = dot(map_ref[...], hidden)
    made = []
    for z in range(2):
        part = field[:, z, span, :].reshape(512, LENGTH)
        value = bypassed[:, z * 128 : z * 128 + 128] + bias[...] + part
        made.append(activate(value).astype(BF))
    return made


def middle_kernel(
    got_ref, kc_ref, bias_ref, inv_y_ref, fwd_y_hbm, x_ref, fields_hbm, hidden, out_ref, fields,
    fwd_y_ref, rows, field, sem,
):
    copies = fetch([(fields_hbm.at[0], fields, sem.at[0]), (fwd_y_hbm, fwd_y_ref, sem.at[1])])
    inverse(got_ref, x_ref, inv_y_ref, rows, field)
    for copy in copies:
        copy.wait()
    def apply(block, carry):
        span = pl.ds(pl.multiple_of(block * 16, 16), 16)
        raw = [fields[:, z, span, :].reshape(64, LENGTH) for z in range(2)]
        raw = jnp.concatenate(raw, axis=1)
        made = pointwise(span, jnp.concatenate([raw, raw], axis=0), kc_ref, bias_ref, field)
        for z in range(2):
            hidden[:, z, span, :] = made[z].reshape(32, 16, LENGTH)
        return carry

    lax.fori_loop(0, 8, apply, 0, unroll=UNROLL_B)
    def forward(index, carry):
        g, z = index // 2, index % 2
        stacked = []
        for quad in range(2):
            wide = jnp.concatenate([hidden[g * 8 + quad * 4 + c, z] for c in range(4)], axis=1)
            along = dot(wide, fwd_y_ref[...]).astype(BF)
            stacked.append(jnp.concatenate([along[:, :128], along[:, 128:]], axis=0))
        spectrum = dot(x_ref[:64], jnp.concatenate(stacked, axis=1)) * (1.0 / LENGTH)
        for h, value in enumerate(swapped(spectrum[:, :128], spectrum[:, 128:])):
            for r in range(2):
                at = h * 16 + g * 4 + r * 2 + z
                rows[pl.ds(at, 32, stride=32), :] = value[r * 32 : r * 32 + 32]
        return carry

    lax.fori_loop(0, 8, forward, 0, unroll=UNROLL_F)
    out_ref[...] = rows[...].astype(BF)


def last_kernel(
    got_ref, kb_hbm, bias_hbm, inv_y_ref, x_ref, hidden, out_hbm, kb, bias, rows, field, made_ref, sem
):
    copies = fetch([(kb_hbm, kb, sem.at[8]), (bias_hbm, bias, sem.at[9])])
    inverse(got_ref, x_ref, inv_y_ref, rows, field)
    for copy in copies:
        copy.wait()

    def keep(block):
        span = pl.ds(pl.multiple_of(block * 16, 16), 16)
        source, target = made_ref.at[:, :, span, :], out_hbm.at[0, :, :, span, :]
        return pltpu.make_async_copy(source, target, sem.at[block])

    def apply(block, carry):
        span = pl.ds(pl.multiple_of(block * 16, 16), 16)
        raw = [hidden[:, z, span, :].reshape(512, LENGTH) for z in range(2)]
        made = pointwise(span, jnp.concatenate(raw, axis=1), kb, bias, field)
        for z in range(2):
            made_ref[:, z, span, :] = made[z].reshape(32, 16, LENGTH)
        keep(block).start()
        return carry

    lax.fori_loop(0, 8, apply, 0, unroll=UNROLL_B)
    for block in range(8):
        keep(block).wait()


def call(kernel, name, inputs, outputs, scratch, sems=0, limit=24):
    spaces = {"s": pltpu.SMEM, "v": pltpu.VMEM, "p": pltpu.VMEM, "h": pltpu.HBM, "f": pltpu.HBM}
    fetched = [index for index, letter in enumerate(inputs) if letter == "f"]

    def run(*arrays):
        buffers = [pltpu.VMEM(arrays[index].shape, arrays[index].dtype) for index in fetched]
        own = [pltpu.VMEM(shape, kind) for shape, kind in scratch]
        if sems:
            own.append(pltpu.SemaphoreType.DMA((sems,)))
        if fetched:
            buffers.append(pltpu.SemaphoreType.DMA((len(fetched),)))

        def body(*refs):
            refs = list(refs)
            if fetched:
                first = len(inputs) + len(outputs) + len(own)
                copies = []
                for order, index in enumerate(fetched):
                    copies.append((refs[index], refs[first + order], refs[-1].at[order]))
                    refs[index] = refs[first + order]
                for copy in fetch(copies):
                    copy.wait()
                refs = refs[:first]
            kernel(*refs)

        placed = []
        for letter, array in zip(inputs, arrays):
            if letter in "hfp":
                array = pltpu.with_memory_space_constraint(array, spaces[letter])
            placed.append(array)
        return pl.pallas_call(
            body,
            name=name,
            out_shape=[spaces[letter](shape, kind) for letter, shape, kind in outputs],
            in_specs=[pl.BlockSpec(memory_space=spaces[letter]) for letter in inputs],
            out_specs=[pl.BlockSpec(memory_space=spaces[letter]) for letter, _, _ in outputs],
            scratch_shapes=own + buffers,
            compiler_params=pltpu.CompilerParams(vmem_limit_bytes=limit << 20),
        )(*placed)

    return run


def exchange(value, axis="slab"):
    return lax.all_to_all(value, axis, split_axis=0, concat_axis=0, tiled=True)


tie = lax.optimization_barrier


def solution(mesh):
    table, one_x, one_z = make_tables()
    const = {name: value.astype(ml_dtypes.bfloat16) for name, value in table.items()}
    ones_x = np.repeat(split(one_x).T[:, :, None], LENGTH, axis=2)
    ones_y = np.tile(split(one_x).reshape(2, 2, 1, K), (1, 1, 8, 1)).reshape(2, 2, LENGTH)
    ones_y = ones_y.transpose(1, 0, 2)
    ones_z = np.repeat(split(one_z)[:, :, None], LENGTH, axis=2)

    def on_device(fields, lift_weight, lift_bias, spectral_weight, bypass_weight, bypass_bias):
        place = lax.axis_index("slab").reshape(1)
        lift_bias = lift_bias[None]
        packed, cube = (1024, LENGTH), (32, 2, 128, 128)
        (spectrum,) = call(
            start_kernel,
            "start",
            "hhh",
            [("v", (128, LENGTH), BF)],
            [((4, 2, 128, 128), BF), ((64, 128), BF), ((64, 256), BF), ((128, 128), F32)],
            sems=3,
        )(fields, const["pair_y"], const["fwd_x"])
        spectrum, spectral_weight = tie((spectrum, spectral_weight))
        spectrum = exchange(spectrum)
        weight = spectral_weight.reshape(2, 2, LENGTH, 256)
        (folded,) = call(
            fold_kernel,
            "fold",
            "hhh",
            [("v", (8, 64, 256), BF)],
            [((4, 32), BF), ((1, 32), BF), ((2, 128, 256), BF)],
            sems=3,
        )(lift_weight, lift_bias, weight)
        folded, bypass_weight, weight, _ = tie((folded, bypass_weight, weight, spectrum))
        gathered = lax.all_gather(weight, "section", axis=0)
        folded = exchange(folded.reshape(512, 256), "section").reshape(8, 64, 256)
        kb, kc, bias0, bias1, fwd_y, inv_y, ones, z_table, x_table = call(
            spread_kernel,
            "spread",
            "s" + "f" * 10,
            [
                ("h", (512, 512), BF),
                ("v", (512, 128), BF),
                ("v", (512, LENGTH), F32),
                ("h", (512, LENGTH), F32),
                ("h", (512, 256), BF),
                ("v", (256, 512), BF),
                ("v", (HALF, LENGTH), F32),
                ("v", (2112, 128), BF),
                ("v", (320, 256), BF),
            ],
            [((512, 512), BF), ((512, LENGTH), F32), ((512, 256), BF)],
            sems=3,
        )(
            place, ones_x, bypass_weight, lift_weight, bypass_bias, lift_bias, const["pair_y"],
            ones_y, ones_z, const["z"], const["x"],
        )
        (planes,) = call(
            first_mix_kernel,
            "mix0",
            "spppp",
            [("v", packed, BF)],
            [((128, 128), F32), ((2, 2, 8, 128), F32)],
        )(place, spectrum, folded, ones, z_table)
        hidden, spectrum = call(
            middle_kernel,
            "middle",
            "pppphph",
            [("v", cube, BF), ("v", packed, BF)],
            [((4, 2, 128, 128), BF), ((512, 256), BF), (packed, F32), (cube, F32)],
            sems=2,
        )(exchange(planes), kc, bias0, inv_y, fwd_y, x_table, fields)
        (planes,) = call(
            mix_kernel,
            "mix1",
            "spph",
            [("v", packed, BF)],
            [
                ((8, 2, 128, 256), BF), ((128, 128), F32), ((2, 2, 32, 128), F32),
                ((16, 2, 2, 8, 128), F32),
            ],
            sems=4,
        )(place, exchange(spectrum), z_table, gathered)
        (features,) = call(
            last_kernel,
            "last",
            "phhppp",
            [("h", (1,) + cube, BF)],
            [((512, 512), BF), ((512, LENGTH), F32), (packed, F32), (cube, F32), (cube, BF)],
            sems=10,
        )(exchange(planes), kb, bias1, inv_y, x_table, hidden)
        return features

    placed = (
        P("section", None, "slab", None, None),
        P(),
        P(),
        P(None, None, None, "section", "slab"),
        P(),
        P(),
    )
    return jax.shard_map(
        on_device,
        mesh=mesh,
        in_specs=placed,
        out_specs=P("section", None, "slab", None, None),
        check_vma=False,
    )
```

```python
import math

import jax
import jax.numpy as jnp
import ml_dtypes
import numpy as np
from jax import lax
from jax.experimental import pallas as pl
from jax.experimental.pallas import tpu as pltpu
from jax.sharding import PartitionSpec as P

K = 16
HALF = 2 * K
LENGTH = 128
SLABS = 64
UNROLL_A = 4
UNROLL_F = 8
UNROLL_B = 8
BF = jnp.bfloat16
F32 = jnp.float32


def wave(freqs):
    where = np.arange(LENGTH, dtype=np.int64)[None, :]
    step = (freqs % LENGTH)[:, None] * where % LENGTH
    phase = step.astype(np.float32) * np.float32(2.0 * math.pi / LENGTH)
    cosine = np.cos(phase).astype(ml_dtypes.bfloat16).astype(np.float32)
    sine = np.sin(phase).astype(ml_dtypes.bfloat16).astype(np.float32)
    return cosine, sine


def make_tables():
    base = np.arange(HALF)
    signed = np.where(base < K, base, base - HALF)
    cos, sin = wave(signed)
    cos_z, sin_z = wave(np.arange(K))
    double = np.where(np.arange(K) == 0, 1.0, 2.0)[:, None]
    table = {}
    table["pair_y"] = np.concatenate([cos, -sin], 0)
    table["fwd_x"] = np.concatenate(
        [np.concatenate([cos, sin], 1), np.concatenate([-sin, cos], 1)], 0
    )
    fwd_z = np.stack([np.stack([cos_z, sin_z], 1), np.stack([-sin_z, cos_z], 1)], 0)
    fwd_z = fwd_z.reshape(2, K, 2, SLABS, 2)
    full = np.einsum("gf,akrsz->gaksfrz", np.eye(4), fwd_z)
    full = full.reshape(4 * HALF, 8, LENGTH).transpose(1, 0, 2).reshape(1024, LENGTH)
    first = np.einsum("akrsz->zaksr", fwd_z).reshape(2 * HALF, SLABS * 2)
    cz, sz = cos_z * double * 0.25, sin_z * double * 0.25
    inv_z = np.stack([np.stack([cz, -sz], 0), np.stack([sz, cz], 0)], 0)
    inv_z = inv_z.reshape(2, 2, K, SLABS, 2)
    back = np.einsum("gf,arksz->sgazfrk", np.eye(4), inv_z).reshape(SLABS * 16, 4 * HALF)
    table["z"] = np.concatenate([back, full, first], 0)
    inv_x = np.stack([np.stack([cos, -sin], 0), np.stack([sin, cos], 0)], 0)
    table["inv_x"] = np.einsum("arpx->axrp", inv_x).reshape(2 * LENGTH, 2 * HALF) * 0.125
    table["x"] = np.concatenate([table["fwd_x"], np.pad(table.pop("inv_x"), ((0, 0), (0, 192)))], 0)
    one_x = (cos.sum(1) - 1j * sin.sum(1)) / math.sqrt(LENGTH)
    one_z = (cos_z.sum(1) - 1j * sin_z.sum(1)) / math.sqrt(LENGTH)
    return table, one_x, one_z


def split(value):
    return np.stack([value.real, value.imag], 0).astype(np.float32)


def dot(left, right):
    return jnp.dot(left, right, preferred_element_type=F32)


def nt_dot(left, right):
    return lax.dot_general(left, right, (((1,), (1,)), ((), ())), preferred_element_type=F32)


def picks(rows, cols):
    row = lax.broadcasted_iota(jnp.int32, (rows, cols), 0)
    col = lax.broadcasted_iota(jnp.int32, (rows, cols), 1)
    return row, col


def one_hot(mask):
    return jnp.where(mask, 1.0, 0.0).astype(BF)


def fetch(copies):
    started = [pltpu.make_async_copy(source, target, sem) for source, target, sem in copies]
    for copy in started:
        copy.start()
    return started


def spread_kernel(
    place_ref, one_x_ref, bypass_ref, lift_ref, bypass_bias_ref, lift_bias_ref, pair_y_ref,
    one_y_ref, one_z_ref, z_ref, x_ref, kb_hbm, kc_ref, bias0_ref, bias1_hbm, fwd_y_hbm,
    inv_y_ref, ones_ref, z_out, x_out, kb_ref, bias1_ref, fwd_y_ref, sem,
):
    z_out[...] = z_ref[...]
    x_out[...] = x_ref[...]
    row, col = picks(512, 32)
    expand = one_hot(row // 16 == col)
    row, col = picks(512, 512)
    tall = nt_dot(expand, bypass_ref[1]).astype(BF)
    kb_ref[...] = jnp.where((row % 16) == (col % 16), nt_dot(tall, expand), 0.0).astype(BF)
    kept = fetch([(kb_ref, kb_hbm, sem.at[0])])
    joint = dot(lift_ref[...], bypass_ref[0])
    high = joint.astype(BF)
    low = (joint - high.astype(F32)).astype(BF)
    row, col = picks(64, 4)
    expand4 = one_hot(row // 16 == col)
    row, col = picks(512, 64)
    for index, part in enumerate((high, low)):
        wide = nt_dot(nt_dot(expand, part).astype(BF), expand4)
        wide = jnp.where((row % 16) == (col % 16), wide, 0.0).astype(BF)
        kc_ref[:, index * 64 : index * 64 + 64] = wide
    filled = jnp.ones((32, LENGTH), BF)
    row, col = picks(32, 32)
    eye = jnp.where(row == col, 1.0, 0.0)

    def column(vector):
        return dot((eye * vector.astype(F32)).astype(BF), filled)

    shift = column(bypass_bias_ref[0:1]) + lax.dot_general(
        bypass_ref[0], column(lift_bias_ref[...]).astype(BF), (((0,), (0,)), ((), ())),
        preferred_element_type=F32,
    )
    for bias_ref, value in ((bias0_ref, shift), (bias1_ref, column(bypass_bias_ref[1:2]))):
        bias_ref[...] = jnp.dot(
            expand.astype(F32), value, precision=lax.Precision.HIGHEST, preferred_element_type=F32
        )
    kept += fetch([(bias1_ref, bias1_hbm, sem.at[1])])
    row, col = picks(256, 64)
    repeat = one_hot((row // 64 == col // 16) & (row % 16 == col % 16))
    tall = dot(repeat, pair_y_ref[...])
    back = tall * 0.125
    row, col = picks(256, LENGTH)
    for c in range(4):
        block = jnp.where((row // 16) % 4 == c, back, 0.0).astype(BF)
        inv_y_ref[:, c * 128 : c * 128 + 128] = block
    wide = tall.T
    row, col = picks(LENGTH, 256)
    for c in range(4):
        block = jnp.where((col // 16) % 4 == c, wide, 0.0).astype(BF)
        fwd_y_ref[c * 128 : c * 128 + 128, :] = block
    kept += fetch([(fwd_y_ref, fwd_y_hbm, sem.at[2])])
    place = place_ref[0]
    xr, xi = one_x_ref[place // 2, 0:1, :], one_x_ref[place // 2, 1:2, :]
    yr = jnp.where(place % 2 == 0, one_y_ref[0, 0:1, :], one_y_ref[1, 0:1, :])
    yi = jnp.where(place % 2 == 0, one_y_ref[0, 1:2, :], one_y_ref[1, 1:2, :])
    pr, pi = xr * yr - xi * yi, xr * yi + xi * yr
    zr, zi = one_z_ref[0], one_z_ref[1]
    ones_ref[...] = jnp.concatenate([zr * pr - zi * pi, zr * pi + zi * pr], axis=0)
    for copy in kept:
        copy.wait()


def fold_kernel(
    lift_hbm, lift_bias_hbm, weight_hbm, out_ref, later_hbm, lift_ref, lift_bias_ref, weight, later, sem
):
    passed, copy, *small = fetch(
        [
            (weight_hbm.at[1], later, sem.at[3]),
            (weight_hbm.at[0], weight, sem.at[0]),
            (lift_hbm, lift_ref, sem.at[1]),
            (lift_bias_hbm, lift_bias_ref, sem.at[2]),
        ]
    )
    passed.wait()
    (kept,) = fetch([(later, later_hbm, sem.at[4])])
    for part in small:
        part.wait()
    row, col = picks(HALF, 4)
    pick = one_hot((row % 8 == col))
    row, col = picks(HALF, HALF)
    lift = dot(pick, lift_ref[...]) + jnp.where(row % 8 == 4, lift_bias_ref[...].astype(F32), 0.0)
    row, col = picks(HALF, LENGTH)
    lift = dot(lift.astype(BF), one_hot(row == col // 4))
    lift = jnp.where(row // 8 == col % 4, lift, 0.0).astype(BF)
    copy.wait()
    for r in range(2):
        folded = dot(lift, weight[r]).astype(BF)
        for section in range(8):
            out_ref[section, r * HALF : r * HALF + HALF, :] = folded
    kept.wait()


def start_kernel(fields_hbm, pair_y_hbm, fwd_x_hbm, out_ref, fields, pair_y, fwd_x, rows, sem):
    copies = fetch(
        [
            (pair_y_hbm, pair_y, sem.at[0]),
            (fields_hbm.at[0], fields, sem.at[1]),
            (fwd_x_hbm, fwd_x, sem.at[2]),
        ]
    )
    copies[0].wait()
    row, col = picks(256, 64)
    repeat = one_hot((row // 64 == col // 16) & (row % 16 == col % 16))
    wide = dot(repeat, pair_y[...]).T
    row, col = picks(LENGTH, 256)
    fwd_y = jnp.concatenate(
        [jnp.where((col // 16) % 4 == c, wide, 0.0).astype(BF) for c in range(4)], axis=0
    )
    lane = lax.broadcasted_iota(jnp.int32, (64, LENGTH), 1)
    copies[1].wait()
    copies[2].wait()
    made = []
    for z in range(2):
        wide = jnp.concatenate([fields[c, z] for c in range(4)], axis=1)
        along = dot(wide, fwd_y).astype(BF)
        stacked = jnp.concatenate([along[:, :128], along[:, 128:]], axis=0)
        made.append(dot(fwd_x[...], stacked) * (1.0 / LENGTH))
    first = jnp.where(lane < 64, made[0], pltpu.roll(made[1], 64, 1))
    second = jnp.where(lane < 64, pltpu.roll(made[0], 64, 1), made[1])
    for h, value in enumerate((first, second)):
        for r in range(2):
            rows[pl.ds(h * 2 + r, 32, stride=4), :] = value[r * 32 : r * 32 + 32]
    out_ref[...] = rows[...].astype(BF)


def mix(weight_ref, modes, pattern, copies):
    low = lax.broadcasted_iota(jnp.int32, (8, LENGTH), 0) < 4
    for pair in range(16):
        for r in range(2):
            for half in range(2):
                even = jnp.broadcast_to(modes[r, half, 2 * pair : 2 * pair + 1, :], (8, LENGTH))
                odd = jnp.broadcast_to(modes[r, half, 2 * pair + 1 : 2 * pair + 2, :], (8, LENGTH))
                pattern[pair, r, half] = jnp.where(low, even, odd)
    mixed = {}
    for g in range(4):
        copies[g].wait()
        total = {}
        for side in range(2):
            section = 2 * g + side
            acc = [[jnp.zeros((8, LENGTH), F32) for _ in range(2)] for _ in range(2)]
            for quad in range(8):
                real = weight_ref[section, 0, quad * 16 : quad * 16 + 16, :].astype(F32)
                imag = weight_ref[section, 1, quad * 16 : quad * 16 + 16, :].astype(F32)
                for sub in range(2):
                    pair = quad * 2 + sub
                    for half in range(2):
                        wr = real[sub * 8 : sub * 8 + 8, half * 128 : half * 128 + 128]
                        wi = imag[sub * 8 : sub * 8 + 8, half * 128 : half * 128 + 128]
                        mr, mi = pattern[pair, 0, half], pattern[pair, 1, half]
                        acc[0][half] = acc[0][half] + wr * mr - wi * mi
                        acc[1][half] = acc[1][half] + wr * mi + wi * mr
            for r in range(2):
                for half in range(2):
                    value = acc[r][half]
                    total[side, r, half] = value + pltpu.roll(value, 4, 0)
        for r in range(2):
            for half in range(2):
                mixed[g, r, half] = jnp.where(low, total[0, r, half], total[1, r, half])
    return mixed


def first_mix(folded_ref, modes):
    sub = lax.broadcasted_iota(jnp.int32, (8, LENGTH), 0)
    mixed = {}
    for g in range(4):
        for row in range(0, 8, 2):
            section, o = 2 * g + row // 4, row % 4
            real = folded_ref[section, o * 8 : o * 8 + 16, :].astype(F32)
            imag = folded_ref[section, HALF + o * 8 : HALF + o * 8 + 16, :].astype(F32)
            for more in range(2):
                for half in range(2):
                    wr = real[more * 8 : more * 8 + 8, half * 128 : half * 128 + 128]
                    wi = imag[more * 8 : more * 8 + 8, half * 128 : half * 128 + 128]
                    mr, mi = modes[0, half], modes[1, half]
                    for r, value in enumerate((wr * mr - wi * mi, wr * mi + wi * mr)):
                        for step in (4, 2, 1):
                            value = value + pltpu.roll(value, step, 0)
                        if row + more:
                            value = jnp.where(sub == row + more, value, mixed[g, r, half])
                        mixed[g, r, half] = value
    return mixed


def evaluate(mixed, turned, z_ref, out_ref):
    slot = lax.broadcasted_iota(jnp.int32, (8, LENGTH), 1) // K
    for py in range(K):
        half, at = py // 8, py % 8
        value = None
        for g in range(4):
            for r in range(2):
                where = 2 * g + r
                moved = mixed[g, r, half]
                if where != at:
                    moved = pltpu.roll(moved, (where - at) * K % LENGTH, 1)
                value = moved if value is None else jnp.where(slot == where, moved, value)
        turned[pl.ds(py, 8, stride=K), :] = value
    out_ref[...] = nt_dot(z_ref[:1024], turned[...].astype(BF)).astype(BF)


def unravel(turned, groups, modes):
    slot = lax.broadcasted_iota(jnp.int32, (8, LENGTH), 1) // K
    parts = [turned[pl.ds(py, 8, stride=K), :] for py in range(K)]
    for g in range(groups):
        for r in range(2):
            source = 2 * g + r
            for half in range(2):
                value = None
                for at in range(8):
                    moved = parts[half * 8 + at]
                    if at != source:
                        moved = pltpu.roll(moved, (at - source) * K % LENGTH, 1)
                    value = moved if value is None else jnp.where(slot == at, moved, value)
                modes[r, half, g * 8 : g * 8 + 8, :] = value


def dropped(place_ref, shape):
    row = lax.broadcasted_iota(jnp.int32, shape, 0)
    lane = lax.broadcasted_iota(jnp.int32, shape, 1)
    origin = jnp.logical_and(row % K == 0, lane % K == 0)
    return jnp.logical_and(origin, place_ref[0] == 0)


def first_mix_kernel(
    place_ref, got_ref, folded_ref, ones_ref, z_ref, out_ref, turned, modes
):
    both = dot(z_ref[2048:], got_ref[...])
    lane = lax.broadcasted_iota(jnp.int32, (HALF, LENGTH), 1)
    value = both[:HALF] + pltpu.roll(both[HALF:], 64, 1)
    value = jnp.where(lane < 64, value, 0.0) * (1.0 / math.sqrt(LENGTH))
    value = jnp.where(lane // K == 4, ones_ref[...], value)
    value = jnp.where(dropped(place_ref, value.shape), 0.0, value)
    value = jnp.concatenate([value, jnp.zeros((LENGTH - HALF, LENGTH), F32)], axis=0)
    turned[...] = value.T
    unravel(turned, 1, modes)
    evaluate(first_mix(folded_ref, modes), turned, z_ref, out_ref)


def mix_kernel(
    place_ref, got_ref, z_ref, weight_hbm, out_ref, weight, turned, modes, pattern, sem
):
    copies = fetch(
        [(weight_hbm.at[pl.ds(2 * g, 2)], weight.at[pl.ds(2 * g, 2)], sem.at[g]) for g in range(4)]
    )
    value = None
    for block in range(8):
        span = slice(block * 128, block * 128 + 128)
        part = dot(z_ref[1024 + block * 128 : 1152 + block * 128], got_ref[span])
        value = part if value is None else value + part
    value = value * (1.0 / math.sqrt(LENGTH))
    value = jnp.where(dropped(place_ref, value.shape), 0.0, value)
    turned[...] = value.T
    unravel(turned, 4, modes)
    evaluate(mix(weight, modes, pattern, copies), turned, z_ref, out_ref)


def swapped(first, second):
    low = lax.broadcasted_iota(jnp.int32, first.shape, 1) < 64
    return (
        jnp.where(low, first, pltpu.roll(second, 64, 1)),
        jnp.where(low, pltpu.roll(first, 64, 1), second),
    )


def inverse(got_ref, x_ref, inv_y_ref, rows, field):
    rows[...] = got_ref[...].astype(F32)

    def step(index, carry):
        g, z = index // 2, index % 2
        parts = []
        for h in range(2):
            pieces = [rows[pl.ds(h * 16 + g * 4 + r * 2 + z, 32, stride=32), :] for r in range(2)]
            parts.append(jnp.concatenate(pieces, axis=0))
        parts = jnp.concatenate(swapped(*parts), axis=1).astype(BF)
        along = dot(x_ref[64:, :64], parts).astype(BF)
        for quad in range(2):
            lanes = slice(quad * 128, quad * 128 + 128)
            wide = jnp.concatenate([along[:128, lanes], along[128:, lanes]], axis=1)
            made = dot(wide, inv_y_ref[...])
            for o in range(4):
                field[g * 8 + quad * 4 + o, z] = made[:, o * 128 : o * 128 + 128]
        return carry

    lax.fori_loop(0, 8, step, 0, unroll=UNROLL_A)


def activate(value):
    inner = value * (0.7978845608028654 + 0.035677408136300125 * value * value)
    half = 0.5 * value
    return half + half * jnp.tanh(inner)


def pointwise(span, hidden, map_ref, bias, field):
    bypassed = dot(map_ref[...], hidden)
    made = []
    for z in range(2):
        part = field[:, z, span, :].reshape(512, LENGTH)
        value = bypassed[:, z * 128 : z * 128 + 128] + bias[...] + part
        made.append(activate(value).astype(BF))
    return made


def middle_kernel(
    got_ref, kc_ref, bias_ref, inv_y_ref, fwd_y_hbm, x_ref, fields_hbm, hidden, out_ref, fields,
    fwd_y_ref, rows, field, sem,
):
    copies = fetch([(fields_hbm.at[0], fields, sem.at[0]), (fwd_y_hbm, fwd_y_ref, sem.at[1])])
    inverse(got_ref, x_ref, inv_y_ref, rows, field)
    for copy in copies:
        copy.wait()
    def apply(block, carry):
        span = pl.ds(pl.multiple_of(block * 16, 16), 16)
        raw = [fields[:, z, span, :].reshape(64, LENGTH) for z in range(2)]
        raw = jnp.concatenate(raw, axis=1)
        made = pointwise(span, jnp.concatenate([raw, raw], axis=0), kc_ref, bias_ref, field)
        for z in range(2):
            hidden[:, z, span, :] = made[z].reshape(32, 16, LENGTH)
        return carry

    lax.fori_loop(0, 8, apply, 0, unroll=UNROLL_B)
    def forward(index, carry):
        g, z = index // 2, index % 2
        stacked = []
        for quad in range(2):
            wide = jnp.concatenate([hidden[g * 8 + quad * 4 + c, z] for c in range(4)], axis=1)
            along = dot(wide, fwd_y_ref[...]).astype(BF)
            stacked.append(jnp.concatenate([along[:, :128], along[:, 128:]], axis=0))
        spectrum = dot(x_ref[:64], jnp.concatenate(stacked, axis=1)) * (1.0 / LENGTH)
        for h, value in enumerate(swapped(spectrum[:, :128], spectrum[:, 128:])):
            for r in range(2):
                at = h * 16 + g * 4 + r * 2 + z
                rows[pl.ds(at, 32, stride=32), :] = value[r * 32 : r * 32 + 32]
        return carry

    lax.fori_loop(0, 8, forward, 0, unroll=UNROLL_F)
    out_ref[...] = rows[...].astype(BF)


def last_kernel(
    got_ref, kb_hbm, bias_hbm, inv_y_ref, x_ref, hidden, out_hbm, kb, bias, rows, field, made_ref, sem
):
    copies = fetch([(kb_hbm, kb, sem.at[8]), (bias_hbm, bias, sem.at[9])])
    inverse(got_ref, x_ref, inv_y_ref, rows, field)
    for copy in copies:
        copy.wait()

    def keep(block):
        span = pl.ds(pl.multiple_of(block * 16, 16), 16)
        source, target = made_ref.at[:, :, span, :], out_hbm.at[0, :, :, span, :]
        return pltpu.make_async_copy(source, target, sem.at[block])

    def apply(block, carry):
        span = pl.ds(pl.multiple_of(block * 16, 16), 16)
        raw = [hidden[:, z, span, :].reshape(512, LENGTH) for z in range(2)]
        made = pointwise(span, jnp.concatenate(raw, axis=1), kb, bias, field)
        for z in range(2):
            made_ref[:, z, span, :] = made[z].reshape(32, 16, LENGTH)
        keep(block).start()
        return carry

    lax.fori_loop(0, 8, apply, 0, unroll=UNROLL_B)
    for block in range(8):
        keep(block).wait()


def call(kernel, name, inputs, outputs, scratch, sems=0, limit=24):
    spaces = {"s": pltpu.SMEM, "v": pltpu.VMEM, "p": pltpu.VMEM, "h": pltpu.HBM, "f": pltpu.HBM}
    fetched = [index for index, letter in enumerate(inputs) if letter == "f"]

    def run(*arrays):
        buffers = [pltpu.VMEM(arrays[index].shape, arrays[index].dtype) for index in fetched]
        own = [pltpu.VMEM(shape, kind) for shape, kind in scratch]
        if sems:
            own.append(pltpu.SemaphoreType.DMA((sems,)))
        if fetched:
            buffers.append(pltpu.SemaphoreType.DMA((len(fetched),)))

        def body(*refs):
            refs = list(refs)
            if fetched:
                first = len(inputs) + len(outputs) + len(own)
                copies = []
                for order, index in enumerate(fetched):
                    copies.append((refs[index], refs[first + order], refs[-1].at[order]))
                    refs[index] = refs[first + order]
                for copy in fetch(copies):
                    copy.wait()
                refs = refs[:first]
            kernel(*refs)

        placed = []
        for letter, array in zip(inputs, arrays):
            if letter in "hfp":
                array = pltpu.with_memory_space_constraint(array, spaces[letter])
            placed.append(array)
        return pl.pallas_call(
            body,
            name=name,
            out_shape=[spaces[letter](shape, kind) for letter, shape, kind in outputs],
            in_specs=[pl.BlockSpec(memory_space=spaces[letter]) for letter in inputs],
            out_specs=[pl.BlockSpec(memory_space=spaces[letter]) for letter, _, _ in outputs],
            scratch_shapes=own + buffers,
            compiler_params=pltpu.CompilerParams(vmem_limit_bytes=limit << 20),
        )(*placed)

    return run


def exchange(value, axis="slab"):
    return lax.all_to_all(value, axis, split_axis=0, concat_axis=0, tiled=True)


tie = lax.optimization_barrier


def solution(mesh):
    table, one_x, one_z = make_tables()
    const = {name: value.astype(ml_dtypes.bfloat16) for name, value in table.items()}
    ones_x = np.repeat(split(one_x).T[:, :, None], LENGTH, axis=2)
    ones_y = np.tile(split(one_x).reshape(2, 2, 1, K), (1, 1, 8, 1)).reshape(2, 2, LENGTH)
    ones_y = ones_y.transpose(1, 0, 2)
    ones_z = np.repeat(split(one_z)[:, :, None], LENGTH, axis=2)

    def on_device(fields, lift_weight, lift_bias, spectral_weight, bypass_weight, bypass_bias):
        place = lax.axis_index("slab").reshape(1)
        lift_bias = lift_bias[None]
        packed, cube = (1024, LENGTH), (32, 2, 128, 128)
        (spectrum,) = call(
            start_kernel,
            "start",
            "hhh",
            [("v", (128, LENGTH), BF)],
            [((4, 2, 128, 128), BF), ((64, 128), BF), ((64, 256), BF), ((128, 128), F32)],
            sems=3,
        )(fields, const["pair_y"], const["fwd_x"])
        spectrum, spectral_weight = tie((spectrum, spectral_weight))
        spectrum = exchange(spectrum)
        weight = spectral_weight.reshape(2, 2, LENGTH, 256)
        folded, later = call(
            fold_kernel,
            "fold",
            "hhh",
            [("v", (8, 64, 256), BF), ("h", (2, LENGTH, 256), BF)],
            [((4, 32), BF), ((1, 32), BF), ((2, 128, 256), BF), ((2, 128, 256), BF)],
            sems=5,
        )(lift_weight, lift_bias, weight)
        folded, bypass_weight, later, _ = tie((folded, bypass_weight, later, spectrum))
        gathered = lax.all_gather(later, "section", axis=0)
        folded = exchange(folded.reshape(512, 256), "section").reshape(8, 64, 256)
        kb, kc, bias0, bias1, fwd_y, inv_y, ones, z_table, x_table = call(
            spread_kernel,
            "spread",
            "s" + "f" * 10,
            [
                ("h", (512, 512), BF),
                ("v", (512, 128), BF),
                ("v", (512, LENGTH), F32),
                ("h", (512, LENGTH), F32),
                ("h", (512, 256), BF),
                ("v", (256, 512), BF),
                ("v", (HALF, LENGTH), F32),
                ("v", (2112, 128), BF),
                ("v", (320, 256), BF),
            ],
            [((512, 512), BF), ((512, LENGTH), F32), ((512, 256), BF)],
            sems=3,
        )(
            place, ones_x, bypass_weight, lift_weight, bypass_bias, lift_bias, const["pair_y"],
            ones_y, ones_z, const["z"], const["x"],
        )
        (planes,) = call(
            first_mix_kernel,
            "mix0",
            "spppp",
            [("v", packed, BF)],
            [((128, 128), F32), ((2, 2, 8, 128), F32)],
        )(place, spectrum, folded, ones, z_table)
        hidden, spectrum = call(
            middle_kernel,
            "middle",
            "pppphph",
            [("v", cube, BF), ("v", packed, BF)],
            [((4, 2, 128, 128), BF), ((512, 256), BF), (packed, F32), (cube, F32)],
            sems=2,
        )(exchange(planes), kc, bias0, inv_y, fwd_y, x_table, fields)
        (planes,) = call(
            mix_kernel,
            "mix1",
            "spph",
            [("v", packed, BF)],
            [
                ((8, 2, 128, 256), BF), ((128, 128), F32), ((2, 2, 32, 128), F32),
                ((16, 2, 2, 8, 128), F32),
            ],
            sems=4,
        )(place, exchange(spectrum), z_table, gathered)
        (features,) = call(
            last_kernel,
            "last",
            "phhppp",
            [("h", (1,) + cube, BF)],
            [((512, 512), BF), ((512, LENGTH), F32), (packed, F32), (cube, F32), (cube, BF)],
            sems=10,
        )(exchange(planes), kb, bias1, inv_y, x_table, hidden)
        return features

    placed = (
        P("section", None, "slab", None, None),
        P(),
        P(),
        P(None, None, None, "section", "slab"),
        P(),
        P(),
    )
    return jax.shard_map(
        on_device,
        mesh=mesh,
        in_specs=placed,
        out_specs=P("section", None, "slab", None, None),
        check_vma=False,
    )
```
